32 devices in a mesh: wide: 8 (over z, y), narrow: 4 (over x, core).
Axes of the slice: x: 2, y: 2, z: 4, core: 2. Of those that a mesh axis runs over, the one named last changes fastest.
Arguments:
- rows: bfloat16 [32, 1152, 768], P(('wide', 'narrow')), may hold values from -6 to 6
- cotangent: bfloat16 [32, 1152, 768], P(('wide', 'narrow')), may hold values from -6 to 6
- page_rows: int32 [32], P(('wide', 'narrow')), may hold values from 709 to 1089, as said below
- pos_bucket: int32 [32, 1152, 1152], P(('wide', 'narrow')), may hold values from 0 to 31
- x_bucket: int32 [32, 1152, 1152], P(('wide', 'narrow')), may hold values from 0 to 63
- y_bucket: int32 [32, 1152, 1152], P(('wide', 'narrow')), may hold values from 0 to 63
- wq: float32 [768, 768], P(('wide', 'narrow')), may hold values from -0.21875 to 0.21875
- bq: float32 [768], P(('wide', 'narrow')), may hold values from -3 to 3
- wk: float32 [768, 768], P(('wide', 'narrow')), may hold values from -0.21875 to 0.21875
- wv: float32 [768, 768], P(('wide', 'narrow')), may hold values from -0.21875 to 0.21875
- bv: float32 [768], P(('wide', 'narrow')), may hold values from -3 to 3
- wo: float32 [768, 768], P(('wide', 'narrow')), may hold values from -2.5 to 2.5
- bo: float32 [768], P(('wide', 'narrow')), may hold values from -3 to 3
- ln1_gain: float32 [768], P(('wide', 'narrow')), may hold values from 0.25 to 1.75
- ln1_bias: float32 [768], P(('wide', 'narrow')), may hold values from -3 to 3
- w1: float32 [768, 3072], P(('wide', 'narrow')), may hold values from -0.21875 to 0.21875
- b1: float32 [3072], P(('wide', 'narrow')), may hold values from -3 to 3
- w2: float32 [3072, 768], P(('wide', 'narrow')), may hold values from -0.109375 to 0.109375
- b2: float32 [768], P(('wide', 'narrow')), may hold values from -3 to 3
- ln2_gain: float32 [768], P(('wide', 'narrow')), may hold values from 0.25 to 1.75
- ln2_bias: float32 [768], P(('wide', 'narrow')), may hold values from -3 to 3
- pos_table: float32 [32, 12], replicated, may hold values from -3 to 3
- x_table: float32 [64, 12], replicated, may hold values from -3 to 3
- y_table: float32 [64, 12], replicated, may hold values from -3 to 3
Outputs:
- out_rows: bfloat16 [32, 1152, 768], P(('wide', 'narrow'))
- rows_grad: bfloat16 [32, 1152, 768], P(('wide', 'narrow'))
- wq_grad: float32 [768, 768], P(('wide', 'narrow'))
- bq_grad: float32 [768], P(('wide', 'narrow'))
- wk_grad: float32 [768, 768], P(('wide', 'narrow'))
- wv_grad: float32 [768, 768], P(('wide', 'narrow'))
- bv_grad: float32 [768], P(('wide', 'narrow'))
- wo_grad: float32 [768, 768], P(('wide', 'narrow'))
- bo_grad: float32 [768], P(('wide', 'narrow'))
- ln1_gain_grad: float32 [768], P(('wide', 'narrow'))
- ln1_bias_grad: float32 [768], P(('wide', 'narrow'))
- w1_grad: float32 [768, 3072], P(('wide', 'narrow'))
- b1_grad: float32 [3072], P(('wide', 'narrow'))
- w2_grad: float32 [3072, 768], P(('wide', 'narrow'))
- b2_grad: float32 [768], P(('wide', 'narrow'))
- ln2_gain_grad: float32 [768], P(('wide', 'narrow'))
- ln2_bias_grad: float32 [768], P(('wide', 'narrow'))
- pos_table_grad: float32 [32, 12], replicated
- x_table_grad: float32 [64, 12], replicated
- y_table_grad: float32 [64, 12], replicated
The draws below stay inside these ranges and needn't reach their ends.
Inputs may be any that keep to these rules, and one draw needn't show every extreme that they name: `page_rows`: every page has either 709 or 1089 live rows, the first ones of its slots; both kinds occur in every draw.
All inputs are finite; a program needn't handle non-finite values.
Results may differ from the reference program's by a relative error of at most 0.015.
The reference program's roundings to bfloat16 on the way count: a program that leaves them out, or rounds other values in their place, can miss the bound.
Values may be sent and summed in bfloat16 or wider, within the bound.
A program may use at most 576 MiB of HBM per device.

```python
import jax
import jax.numpy as jnp
from jax import lax

D = 768
HEADS = 12
HEAD_DIM = 64
FF = 3072
NB_POS = 32
NB_2D = 64
SLOT = 1152
LONG_ROWS = 1089
SHORT_ROWS = 709
QBLK = 576
PAGES = 32


def draw_page_rows(key, part):
    coin = jax.random.randint(key, (PAGES,), 0, 2)
    counts = jnp.where(coin == 1, LONG_ROWS, SHORT_ROWS)
    counts = counts.at[0].set(LONG_ROWS).at[1].set(SHORT_ROWS)
    return counts.astype(jnp.int32)


def with_ends(drawn, stream_key, least, largest):
    index_at = [jax.random.randint(jax.random.fold_in(stream_key, axis), (), 0, length) for axis, length in enumerate(drawn.shape)]
    widest = drawn.shape.index(max(drawn.shape))
    beside = index_at[:widest] + [(index_at[widest] + 1) % drawn.shape[widest]] + index_at[widest + 1:]
    return drawn.at[tuple(index_at)].set(least).at[tuple(beside)].set(largest)


def shard_levels(key, shape, shards, low, top_value):
    level, own = 1.0, jax.random.fold_in(key, 6)
    for dim, blocks in shards:
        draws = jnp.exp(jax.random.uniform(jax.random.fold_in(own, dim), (blocks,), jnp.float32, low / len(shards), top_value / len(shards)))
        level = level * jnp.repeat(draws, shape[dim] // blocks).reshape([-1 if axis == dim else 1 for axis in range(len(shape))])
    return level


def normal_values(key, shape, deviation, limit, cuts=(), kind=jnp.bfloat16):
    loudness = shard_levels(key, shape, cuts, -0.22, 0.18) if cuts else 1.0
    result = jax.random.normal(key, shape, jnp.float32) * deviation * loudness
    return jnp.minimum(jnp.maximum(result, -limit), limit).astype(kind)


def setup_inputs(seed: int = 0) -> dict:
    arg_keys = jax.random.split(jax.random.key(seed), 25)
    rows = normal_values(arg_keys[0], (PAGES, SLOT, D), 1.0, 6.0, ((0, 32),))
    cotangent = normal_values(arg_keys[1], (PAGES, SLOT, D), 1.0, 6.0, ((0, 32),))
    page_rows = draw_page_rows(jax.random.fold_in(arg_keys[24], 71), 0)
    pos_bucket = with_ends(jax.random.randint(arg_keys[3], (PAGES, SLOT, SLOT), 0, NB_POS), jax.random.fold_in(arg_keys[3], 1), 0, NB_POS - 1).astype(jnp.int32)
    x_bucket = with_ends(jax.random.randint(arg_keys[4], (PAGES, SLOT, SLOT), 0, NB_2D), jax.random.fold_in(arg_keys[4], 1), 0, NB_2D - 1).astype(jnp.int32)
    y_bucket = with_ends(jax.random.randint(arg_keys[5], (PAGES, SLOT, SLOT), 0, NB_2D), jax.random.fold_in(arg_keys[5], 1), 0, NB_2D - 1).astype(jnp.int32)
    wq = normal_values(arg_keys[6], (D, D), D ** -0.5, 0.21875, ((0, 32),), jnp.float32)
    bq = normal_values(arg_keys[7], (D,), 0.5, 3.0, ((0, 32),), jnp.float32)
    wk = normal_values(arg_keys[8], (D, D), D ** -0.5, 0.21875, ((0, 32),), jnp.float32)
    wv = normal_values(arg_keys[9], (D, D), D ** -0.5, 0.21875, ((0, 32),), jnp.float32)
    bv = normal_values(arg_keys[10], (D,), 0.5, 3.0, ((0, 32),), jnp.float32)
    wo = normal_values(arg_keys[11], (D, D), (max(D * 8 // SLOT, 1)) ** -0.5, 2.5, ((0, 32),), jnp.float32)
    bo = normal_values(arg_keys[12], (D,), 0.5, 3.0, ((0, 32),), jnp.float32)
    ln1_gain = jnp.clip(1.0 + 0.15 * jax.random.normal(arg_keys[13], (D,), jnp.float32), 0.25, 1.75)
    ln1_bias = normal_values(arg_keys[14], (D,), 0.5, 3.0, ((0, 32),), jnp.float32)
    w1 = normal_values(arg_keys[15], (D, FF), D ** -0.5, 0.21875, ((0, 32),), jnp.float32)
    b1 = normal_values(arg_keys[16], (FF,), 0.5, 3.0, ((0, 32),), jnp.float32)
    w2 = normal_values(arg_keys[17], (FF, D), FF ** -0.5, 0.109375, ((0, 32),), jnp.float32)
    b2 = normal_values(arg_keys[18], (D,), 0.5, 3.0, ((0, 32),), jnp.float32)
    ln2_gain = jnp.clip(1.0 + 0.15 * jax.random.normal(arg_keys[19], (D,), jnp.float32), 0.25, 1.75)
    ln2_bias = normal_values(arg_keys[20], (D,), 0.5, 3.0, ((0, 32),), jnp.float32)
    pos_table = normal_values(arg_keys[21], (NB_POS, HEADS), 0.5, 3.0, (), jnp.float32)
    x_table = normal_values(arg_keys[22], (NB_2D, HEADS), 0.5, 3.0, (), jnp.float32)
    y_table = normal_values(arg_keys[23], (NB_2D, HEADS), 0.5, 3.0, (), jnp.float32)
    return dict(rows=rows, cotangent=cotangent, page_rows=page_rows, pos_bucket=pos_bucket, x_bucket=x_bucket, y_bucket=y_bucket, wq=wq, bq=bq, wk=wk, wv=wv, bv=bv, wo=wo, bo=bo, ln1_gain=ln1_gain, ln1_bias=ln1_bias, w1=w1, b1=b1, w2=w2, b2=b2, ln2_gain=ln2_gain, ln2_bias=ln2_bias, pos_table=pos_table, x_table=x_table, y_table=y_table)


@jax.custom_vjp
def low(v):
    return lax.optimization_barrier(v.astype(jnp.bfloat16)).astype(jnp.float32)

@jax.custom_vjp
def low_back(v):
    return v

def low_keep(v):
    return (low(v), None)

def low_pass(kept, grad):
    return (grad,)

def back_keep(v):
    return (v, None)

def back_low(kept, grad):
    return (low(grad),)
low.defvjp(low_keep, low_pass)
low_back.defvjp(back_keep, back_low)
EPS = 1e-05
HIGH = lax.Precision.HIGHEST

def norm_rows(values, gain, shift):
    center = values - lax.optimization_barrier(jnp.mean(values, axis=-1, keepdims=True))
    spread = lax.optimization_barrier(jnp.mean(center * center, axis=-1, keepdims=True))
    return center * lax.rsqrt(spread + EPS) * gain + shift

def gelu_exact(values):
    return jax.nn.gelu(values, approximate=False)

def table_bias(buckets, table):
    codes = jnp.arange(table.shape[0], dtype=jnp.int32)
    hot = (buckets[:, :, None] == codes[None, None, :]).astype(table.dtype)
    return jnp.einsum('qkb,bh->hqk', hot, table, precision=HIGH)

def page_forward(params, page):
    w_query, b_query, w_key, w_value, b_value, w_out, b_out, gain_one, shift_one, w_up, b_up, w_down, b_down, gain_two, shift_two, pos_table, x_table, y_table = params
    x_rows, live_keys, pos_rows, xpos_rows, ypos_rows = page
    inputs = low(x_rows)
    query = low(low_back(jnp.dot(inputs, w_query, precision=HIGH) + b_query))
    keys = low(low_back(jnp.dot(inputs, w_key, precision=HIGH)))
    values = low(low_back(jnp.dot(inputs, w_value, precision=HIGH) + b_value))
    keys3 = keys.reshape(SLOT, HEADS, HEAD_DIM)
    values3 = values.reshape(SLOT, HEADS, HEAD_DIM)
    split = SLOT // QBLK

    def block(pieces):
        q_block, pos_block, xpos_block, ypos_block = pieces
        scores = jnp.einsum('qhd,khd->hqk', q_block, keys3, precision=HIGH) * 0.125
        scores = scores + table_bias(pos_block, pos_table) + table_bias(xpos_block, x_table) + table_bias(ypos_block, y_table)
        scores = low_back(scores)
        scores = jnp.where(live_keys[None, None, :], scores, -1000000000.0)
        prob = low(jax.nn.softmax(scores, axis=-1))
        return jnp.einsum('hqk,khd->qhd', prob, values3, precision=HIGH)
    blocks = lax.map(jax.checkpoint(block), (query.reshape(split, QBLK, HEADS, HEAD_DIM), pos_rows.reshape(split, QBLK, SLOT), xpos_rows.reshape(split, QBLK, SLOT), ypos_rows.reshape(split, QBLK, SLOT)))
    attended = low(low_back(blocks.reshape(SLOT, D)))
    mixed = low_back(jnp.dot(attended, w_out, precision=HIGH) + b_out)
    normed_one = norm_rows(x_rows + mixed, gain_one, shift_one)
    pre_act = low_back(jnp.dot(low(normed_one), w_up, precision=HIGH) + b_up)
    activated = low(gelu_exact(pre_act))
    ffn_out = low_back(jnp.dot(activated, w_down, precision=HIGH) + b_down)
    return norm_rows(normed_one + ffn_out, gain_two, shift_two)

def reference(rows, cotangent, page_rows, pos_bucket, x_bucket, y_bucket, wq, bq, wk, wv, bv, wo, bo, ln1_gain, ln1_bias, w1, b1, w2, b2, ln2_gain, ln2_bias, pos_table, x_table, y_table):
    masters = (wq, bq, wk, wv, bv, wo, bo, ln1_gain, ln1_bias, w1, b1, w2, b2, ln2_gain, ln2_bias, pos_table, x_table, y_table)
    live = jnp.arange(SLOT, dtype=jnp.int32)[None, :] < page_rows[:, None]

    def forward(inputs, *params):
        rounded = tuple((low(param) for param in params))

        def step(carry, page):
            return (carry, jax.checkpoint(page_forward)(rounded, page))
        _, outputs = lax.scan(step, jnp.zeros((), jnp.float32), (inputs, live, pos_bucket, x_bucket, y_bucket))
        return outputs
    outputs, pull = jax.vjp(forward, rows.astype(jnp.float32), *masters)
    grads = pull(cotangent.astype(jnp.float32) * live[:, :, None].astype(jnp.float32))
    return (outputs.astype(jnp.bfloat16), grads[0].astype(jnp.bfloat16), grads[1], grads[2], grads[3], grads[4], grads[5], grads[6], grads[7], grads[8], grads[9], grads[10], grads[11], grads[12], grads[13], grads[14], grads[15], grads[16], grads[17], grads[18])
```

```python
import jax
import jax.numpy as jnp
from jax import lax
from jax.experimental import pallas as pl
from jax.experimental.pallas import tpu as pltpu
from jax.sharding import PartitionSpec as P
bf=jnp.bfloat16; f32=jnp.float32
NT=(((1,),(1,)),((),())); NN=(((1,),(0,)),((),()))
BQ=128
VM=60<<20
TABLE_SCALE=3500.0

def take(t,i): return jnp.take_along_axis(t,i,axis=1,mode="promise_in_bounds")

def bias_kernel(pos_ref,x_ref,y_ref,tab_ref,out_ref,idx_ref,*,npair):
    S=out_ref.shape[1]
    packed=pos_ref[...]|(x_ref[...]<<5)|(y_ref[...]<<11)
    idx_ref[...]=packed.T
    tp=[jnp.broadcast_to(tab_ref[0,p:p+1,:],(8,128)) for p in range(npair)]
    tx=[jnp.broadcast_to(tab_ref[1,p:p+1,:],(8,128)) for p in range(npair)]
    def body(r,c):
        for u in range(4):
            sl=pl.ds(pl.multiple_of((r*4+u)*8,8),8)
            t=idx_ref[sl,:]
            p=t&31; x=(t>>5)&63; y=(t>>11)+64
            g=[take(a,p) for a in tp]
            g=[a+take(b,x) for a,b in zip(g,tx)]
            g=[a+take(b,y) for a,b in zip(g,tx)]
            for k in range(npair): out_ref[k,sl,:]=g[k]
        return c
    lax.fori_loop(0,S//32,body,0)

def bias_call(pos,x,y,tab):
    S=pos.shape[0]; npair=6
    return pl.pallas_call(lambda *a: bias_kernel(*a,npair=npair),grid=(S//BQ,),
      in_specs=[pl.BlockSpec((BQ,S),lambda i:(i,0))]*3+[pl.BlockSpec((2,8,128),lambda i:(0,0,0))],
      out_specs=[pl.BlockSpec((npair,S,BQ),lambda i:(0,0,i)),pl.BlockSpec((S,BQ),lambda i:(0,i))],
      out_shape=[jax.ShapeDtypeStruct((npair,S,S),jnp.int32),jax.ShapeDtypeStruct((S,S),jnp.int32)],
      compiler_params=pltpu.CompilerParams(vmem_limit_bytes=VM),name="bias_lookup")(pos,x,y,tab)

def make_tab(pos_t,x_t,y_t):
    def fix(t): return jnp.round(t.astype(bf).astype(f32)*TABLE_SCALE).astype(jnp.int32)
    def pack(t): f=fix(t); return (f[:,0::2]*65536+f[:,1::2]).T
    p=pack(pos_t); xy=jnp.concatenate([pack(x_t),pack(y_t)],axis=1)
    p=jnp.pad(p,((0,2),(0,128-p.shape[1]))); xy=jnp.pad(xy,((0,2),(0,128-xy.shape[1])))
    return jnp.stack([p,xy])

def stack2(a):
    lane=lax.broadcasted_iota(jnp.int32,a.shape,1)
    z=jnp.zeros_like(a)
    return jnp.concatenate([jnp.where(lane<64,a,z),jnp.where(lane<64,z,a)],axis=0)

def fwd_kernel(live_ref,q_ref,k_ref,v_ref,b_ref,e_ref,o_ref,l_ref,s_scr,*,CH):
    S=k_ref.shape[0]
    live=live_ref[0]
    c=1.0/(TABLE_SCALE*65536.0)
    nch=S//CH
    rows=lax.broadcasted_iota(jnp.int32,(CH,1),0)
    for p in range(6):
        ln=pl.ds(p*128,128)
        qs=stack2(q_ref[:,ln])
        m=jnp.full((8,256),-3e38,f32)
        for ch in range(nch):
            r=pl.ds(ch*CH,CH)
            s=lax.dot_general(k_ref[r,ln],qs,NT,preferred_element_type=f32)
            b=b_ref[p,r,:]
            b0=b.astype(f32)*c
            b1=(b<<16).astype(f32)*c
            s=s+jnp.concatenate([b0,b1],axis=1)
            s=jnp.where(rows+ch*CH<live,s,-1e9)
            s_scr[r,:]=s
            m=jnp.maximum(m,jnp.max(s.reshape(CH//8,8,256),axis=0))
        mx=jnp.max(m,axis=0,keepdims=True)
        l=jnp.zeros((8,256),f32)
        for ch in range(nch):
            r=pl.ds(ch*CH,CH)
            e=jnp.exp(s_scr[r,:]-mx)
            l=l+jnp.sum(e.reshape(CH//8,8,256),axis=0)
            eb=e.astype(bf)
            e_ref[2*p,r,:]=eb[:,:128]
            e_ref[2*p+1,r,:]=eb[:,128:]
        linv=1.0/jnp.sum(l,axis=0,keepdims=True)
        l_ref[2*p:2*p+1,:]=linv[:,:128]
        l_ref[2*p+1:2*p+2,:]=linv[:,128:]
        acc=jnp.zeros((128,256),f32)
        ecat=jnp.concatenate([e_ref[2*p],e_ref[2*p+1]],axis=1)
        acc=lax.dot_general(v_ref[:,ln],ecat,(((0,),(0,)),((),())),preferred_element_type=f32)
        acc=acc*linv
        sub=lax.broadcasted_iota(jnp.int32,(128,128),0)
        ot=jnp.where(sub<64,acc[:,:128],acc[:,128:])
        o_ref[:,ln]=ot.T.astype(bf)

def fwd_call(live,q,k,v,b,CH=128):
    S,D=k.shape
    full=pl.BlockSpec((S,D),lambda i,*_:(0,0))
    return pl.pallas_call(lambda *a: fwd_kernel(*a,CH=CH),
      grid_spec=pltpu.PrefetchScalarGridSpec(num_scalar_prefetch=1,grid=(S//BQ,),
        in_specs=[pl.BlockSpec((BQ,D),lambda i,*_:(i,0)),full,full,pl.BlockSpec((6,S,BQ),lambda i,*_:(0,0,i))],
        out_specs=[pl.BlockSpec((12,S,BQ),lambda i,*_:(0,0,i)),pl.BlockSpec((BQ,D),lambda i,*_:(i,0)),pl.BlockSpec((16,BQ),lambda i,*_:(0,i))],
        scratch_shapes=[pltpu.VMEM((S,256),f32)]),
      out_shape=[jax.ShapeDtypeStruct((12,S,S),bf),jax.ShapeDtypeStruct((S,D),bf),jax.ShapeDtypeStruct((16,S),f32)],
      compiler_params=pltpu.CompilerParams(vmem_limit_bytes=VM),name="attention_forward")(live,q,k,v,b)

def bwd_kernel(q_ref,do_ref,k_ref,v_ref,e_ref,l_ref,d_ref,idx_ref,dq_ref,dk_ref,dv_ref,h_ref,ds_scr,dk_acc,dv_acc,cat_scr,xi_scr,*,CH,U):
    S=k_ref.shape[0]
    pid=pl.program_id(0)
    @pl.when(pid==0)
    def _():
        dk_acc[...]=jnp.zeros_like(dk_acc); dv_acc[...]=jnp.zeros_like(dv_acc); h_ref[...]=jnp.zeros_like(h_ref)
    nch=S//CH
    for p in range(6):
        ln=pl.ds(p*128,128)
        qs=stack2(q_ref[:,ln])
        l2=l_ref[2*p:2*p+2,:]
        d2=d_ref[2*p:2*p+2,:]*l2
        lcol=jnp.concatenate([l2]*4,axis=0).T
        lane=lax.broadcasted_iota(jnp.int32,(BQ,128),1)
        dos=(do_ref[:,ln].astype(f32)*jnp.where(lane<64,lcol[:,0:1],lcol[:,1:2])).astype(bf)
        dst=stack2(dos)
        for ch in range(nch):
            r=pl.ds(ch*CH,CH)
            dp=lax.dot_general(v_ref[r,ln],dst,NT,preferred_element_type=f32)
            e0=e_ref[2*p,r,:]; e1=e_ref[2*p+1,r,:]
            s0=e0.astype(f32)*(dp[:,:128]-d2[0:1,:])
            s1=e1.astype(f32)*(dp[:,128:]-d2[1:2,:])
            ds_scr[pl.ds(ch*CH*16+2*p,CH,stride=16),:]=s0
            ds_scr[pl.ds(ch*CH*16+2*p+1,CH,stride=16),:]=s1
            sc=jnp.concatenate([s0.astype(bf),s1.astype(bf)],axis=1)
            cat_scr[r,:]=sc
            ec=jnp.concatenate([e0,e1],axis=1)
            dk_acc[r,ln]+=lax.dot_general(sc,qs,NN,preferred_element_type=f32)
            dv_acc[r,ln]+=lax.dot_general(ec,dst,NN,preferred_element_type=f32)
        a=lax.dot_general(k_ref[:,ln],cat_scr[...],(((0,),(0,)),((),())),preferred_element_type=f32)
        sub=lax.broadcasted_iota(jnp.int32,(128,128),0)
        dq_ref[:,ln]=(jnp.where(sub<64,a[:,:128],a[:,128:]).T*0.125).astype(bf)
    t=idx_ref[...]
    xi_scr[0]=(t&31).astype(f32); xi_scr[1]=((t>>5)&63).astype(f32); xi_scr[2]=(t>>11).astype(f32)
    iot=lax.broadcasted_iota(jnp.int32,(16,128),0).astype(f32).astype(bf)
    one=jnp.ones((16,128),bf); zero=jnp.zeros((16,128),bf)
    def one_j(j):
        bp,bx,by=[jnp.broadcast_to(xi_scr[n,pl.ds(j,1),:],(16,128)).astype(bf) for n in range(3)]
        d=ds_scr[pl.ds(pl.multiple_of(j*16,16),16),:].astype(bf)
        xh=bx>=32; yh=by>=32
        bxl=jnp.where(xh,bx-32,bx); byl=jnp.where(yh,by-32,by)
        rows=[jnp.where(b==iot+bf(16*k),one,zero) for b in (bxl,byl,bp) for k in range(2)]
        rhs=[d,jnp.where(xh,zero,d),jnp.where(xh,d,zero),jnp.where(yh,zero,d),jnp.where(yh,d,zero)]
        return jnp.concatenate(rows,0),jnp.concatenate(rhs,0)
    def body(t,acc):
        for u in range(U):
            l0,r0=one_j(t*2*U+2*u); l1,r1=one_j(t*2*U+2*u+1)
            acc=acc+lax.dot_general(jnp.concatenate([l0,l1],1),jnp.concatenate([r0,r1],1),NT,preferred_element_type=f32)
        return acc
    h_ref[...]+=lax.fori_loop(0,S//(2*U),body,jnp.zeros((96,80),f32))
    @pl.when(pid==pl.num_programs(0)-1)
    def _():
        dk_ref[...]=dk_acc[...].astype(bf); dv_ref[...]=dv_acc[...].astype(bf)

def bwd_call(q,do,k,v,e,linv,dd,idx,CH=128,U=32):
    S,D=k.shape
    full=pl.BlockSpec((S,D),lambda i:(0,0))
    blk=pl.BlockSpec((BQ,D),lambda i:(i,0))
    row=pl.BlockSpec((16,BQ),lambda i:(0,i))
    return pl.pallas_call(lambda *a: bwd_kernel(*a,CH=CH,U=U),grid=(S//BQ,),
        in_specs=[blk,blk,full,full,pl.BlockSpec((12,S,BQ),lambda i:(0,0,i)),row,row,pl.BlockSpec((S,BQ),lambda i:(0,i))],
        out_specs=[blk,full,full,pl.BlockSpec((96,80),lambda i:(0,0))],
        scratch_shapes=[pltpu.VMEM((S*16,BQ),f32),pltpu.VMEM((S,D),f32),pltpu.VMEM((S,D),f32),pltpu.VMEM((S,256),bf),pltpu.VMEM((3,S,BQ),f32)],
      out_shape=[jax.ShapeDtypeStruct((S,D),bf)]*3+[jax.ShapeDtypeStruct((96,80),f32)],
      compiler_params=pltpu.CompilerParams(vmem_limit_bytes=VM),name="attention_backward")(q,do,k,v,e,linv,dd,idx)

def unpack_hist(h):
    gx=jnp.concatenate([h[0:32,16:28],h[0:32,32:44]],axis=0)
    gy=jnp.concatenate([h[32:64,48:60],h[32:64,64:76]],axis=0)
    gp=h[64:96,0:12]
    return gp,gx,gy


AXES = ("wide", "narrow")
EPS = 1e-05


def norm_rows(values, gain, shift):
    center = values - jnp.mean(values, axis=-1, keepdims=True)
    spread = jnp.mean(center * center, axis=-1, keepdims=True)
    return center * lax.rsqrt(spread + EPS) * gain + shift


def gelu_exact(values):
    return jax.nn.gelu(values, approximate=False)


def gather(shard):
    return lax.all_gather(shard, AXES, axis=0, tiled=True)


def scatter(grad):
    return lax.psum_scatter(grad, AXES, scatter_dimension=0, tiled=True)


def local(rows, cotangent, page_rows, pos_bucket, x_bucket, y_bucket, wq, bq, wk, wv, bv, wo, bo,
          ln1_gain, ln1_bias, w1, b1, w2, b2, ln2_gain, ln2_bias, pos_table, x_table, y_table):
    length, width = rows.shape[1:]
    heads = pos_table.shape[1]
    size = width // heads
    share = wq.shape[0]
    vectors = jnp.stack([bq, bv, bo, ln1_gain, ln1_bias, b2, ln2_gain, ln2_bias], axis=1)
    vectors = jnp.concatenate([vectors, b1.reshape(share, 4)], axis=1)
    vectors = jnp.pad(vectors, ((0, 0), (0, 116)))
    first = gather(jnp.concatenate([wq, wk, wv, vectors], axis=1).astype(bf))
    second = gather(jnp.concatenate([wo, w1], axis=1).astype(bf))
    w_down = gather(w2.astype(bf))
    w_qkv = first[:, : 3 * width]
    small = first[:, 3 * width : 3 * width + 12].astype(f32)
    b_query, b_value, b_out, gain_one, shift_one, b_down, gain_two, shift_two = [small[:, n] for n in range(8)]
    b_up = small[:, 8:12].reshape(-1)
    w_out = second[:, :width]
    w_up = second[:, width:]
    x_rows = rows[0]
    x_full = x_rows.astype(f32)
    bias, codes = bias_call(pos_bucket[0], x_bucket[0], y_bucket[0], make_tab(pos_table, x_table, y_table))
    qkv = jnp.dot(x_rows, w_qkv, preferred_element_type=f32)
    query = (qkv[:, :width] + b_query).astype(bf) * bf(0.125)
    keys = qkv[:, width : 2 * width].astype(bf)
    values = (qkv[:, 2 * width :] + b_value).astype(bf)
    prob, attended, inverse = fwd_call(page_rows, query, keys, values, bias)
    mixed = jnp.dot(attended, w_out, preferred_element_type=f32) + b_out
    branch_one = x_full + mixed
    normed_one, pull_one = jax.vjp(norm_rows, branch_one, gain_one, shift_one)
    normed_low = normed_one.astype(bf)
    pre_act = jnp.dot(normed_low, w_up, preferred_element_type=f32) + b_up
    activated, pull_gelu = jax.vjp(gelu_exact, pre_act)
    act_low = activated.astype(bf)
    branch_two = normed_one + jnp.dot(act_low, w_down, preferred_element_type=f32) + b_down
    result, pull_two = jax.vjp(norm_rows, branch_two, gain_two, shift_two)
    out_rows = result.astype(bf)[None]
    live = lax.broadcasted_iota(jnp.int32, (length, 1), 0) < page_rows[0]
    upstream = jnp.where(live, cotangent[0].astype(f32), 0.0)
    d_branch_two, grad_gain_two, grad_shift_two = pull_two(upstream)
    d_ffn = d_branch_two.astype(bf)
    grad_down = jnp.einsum("sf,sd->fd", act_low, d_ffn, preferred_element_type=f32)
    grad_bdown = jnp.sum(d_ffn.astype(f32), axis=0)
    d_act = jnp.einsum("sd,fd->sf", d_ffn, w_down, preferred_element_type=f32)
    (d_pre,) = pull_gelu(d_act)
    d_pre_low = d_pre.astype(bf)
    grad_up = jnp.einsum("sd,sf->df", normed_low, d_pre_low, preferred_element_type=f32)
    grad_bup = jnp.sum(d_pre_low.astype(f32), axis=0)
    d_normed = d_branch_two + jnp.einsum("sf,df->sd", d_pre_low, w_up, preferred_element_type=f32)
    d_branch_one, grad_gain_one, grad_shift_one = pull_one(d_normed)
    d_mixed = d_branch_one.astype(bf)
    grad_out = jnp.einsum("sa,sd->ad", attended, d_mixed, preferred_element_type=f32)
    grad_bout = jnp.sum(d_mixed.astype(f32), axis=0)
    d_attended = jnp.einsum("sd,ad->sa", d_mixed, w_out, preferred_element_type=f32).astype(bf)
    inner = jnp.sum((d_attended.astype(f32) * attended.astype(f32)).reshape(length, heads, size), axis=-1)
    inner = jnp.pad(inner.T, ((0, 16 - heads), (0, 0)))
    dq, dk, dv, table_sums = bwd_call(query, d_attended, keys, values, prob, inverse, inner, codes)
    d_qkv = jnp.concatenate([dq, dk, dv], axis=1)
    grad_qkv = jnp.einsum("sd,se->de", x_rows, d_qkv, preferred_element_type=f32)
    grad_bquery = jnp.sum(dq.astype(f32), axis=0)
    grad_bvalue = jnp.sum(dv.astype(f32), axis=0)
    d_rows = d_branch_one + jnp.einsum("se,de->sd", d_qkv, w_qkv, preferred_element_type=f32)
    rows_grad = d_rows.astype(bf)[None]
    sums = jnp.stack([grad_bquery, grad_bvalue, grad_bout, grad_gain_one, grad_shift_one, grad_bdown, grad_gain_two, grad_shift_two], axis=1)
    sums = jnp.concatenate([sums, grad_bup.reshape(width, 4)], axis=1)
    sums = jnp.pad(sums, ((0, 0), (0, 116)))
    share_down = scatter(grad_down)
    share_second = scatter(jnp.concatenate([grad_out, grad_up], axis=1))
    share_first = scatter(jnp.concatenate([grad_qkv, sums], axis=1))
    g_pos, g_x, g_y = unpack_hist(lax.psum(table_sums, AXES))
    vec = share_first[:, 3 * width :]
    return (
        out_rows,
        rows_grad,
        share_first[:, :width],
        vec[:, 0],
        share_first[:, width : 2 * width],
        share_first[:, 2 * width : 3 * width],
        vec[:, 1],
        share_second[:, :width],
        vec[:, 2],
        vec[:, 3],
        vec[:, 4],
        share_second[:, width:],
        vec[:, 8:12].reshape(-1),
        share_down,
        vec[:, 5],
        vec[:, 6],
        vec[:, 7],
        g_pos,
        g_x,
        g_y,
    )


def solution(mesh):
    cut3 = P(AXES, None, None)
    cut2 = P(AXES, None)
    cut1 = P(AXES)
    params = (cut2, cut1, cut2, cut2, cut1, cut2, cut1, cut1, cut1, cut2, cut1, cut2, cut1, cut1, cut1)
    in_specs = (cut3, cut3, cut1, cut3, cut3, cut3) + params + (P(), P(), P())
    out_specs = (cut3, cut3) + params + (P(), P(), P())
    return jax.shard_map(local, mesh=mesh, in_specs=in_specs, out_specs=out_specs, check_vma=False)
```

```python
import jax
import jax.numpy as jnp
from jax import lax
from jax.experimental import pallas as pl
from jax.experimental.pallas import tpu as pltpu
from jax.sharding import PartitionSpec as P

bf = jnp.bfloat16
f32 = jnp.float32
NT = (((1,), (1,)), ((), ()))
NN = (((1,), (0,)), ((), ()))
TN = (((0,), (0,)), ((), ()))
AXES = ("wide", "narrow")
MESH = pl.DeviceIdType.MESH
BQ = 128
VM = 60 << 20
TABLE_SCALE = 3500.0
EPS = 1e-05


class Place:
    def __init__(self, wide, narrow, span):
        self.n = wide * narrow
        self.half = self.n // 2
        self.narrow = narrow
        self.span = span
        self.outer = self.half // span
        self.flat = lax.axis_index("wide") * narrow + lax.axis_index("narrow")
        self.par = lax.rem(lax.div(self.flat, span), 2)
        self.group = lax.div(self.flat, 2 * span) * span + lax.rem(self.flat, span)

    def flat_of(self, group, par):
        return (lax.div(group, self.span) * 2 + par) * self.span + lax.rem(group, self.span)

    def device(self, flat):
        return (lax.div(flat, self.narrow), lax.rem(flat, self.narrow))

    def peer(self, k):
        return lax.rem(self.group + k, self.half)

    def partner(self):
        return self.device(self.flat_of(self.group, 1 - self.par))

    def peer_device(self, k):
        return self.device(self.flat_of(self.peer(k), self.par))

    def greet(self):
        barrier = pltpu.get_barrier_semaphore()
        pl.semaphore_signal(barrier, inc=1, device_id=self.partner(), device_id_type=MESH)

        def one(k, c):
            pl.semaphore_signal(barrier, inc=1, device_id=self.peer_device(k), device_id_type=MESH)
            return c

        lax.fori_loop(1, self.half, one, 0)
        pl.semaphore_wait(barrier, self.half)


def send(src, dst, send_sem, recv_sem, device):
    pltpu.make_async_remote_copy(src, dst, send_sem, recv_sem, device_id=device, device_id_type=MESH).start()


def drain(ref, sem):
    pltpu.make_async_copy(ref, ref, sem).wait()


def take(t, i):
    return jnp.take_along_axis(t, i, axis=1, mode="promise_in_bounds")


def front_kernel(where, pos_ref, x_ref, y_ref, pt_ref, xt_ref, yt_ref, wq_ref, wk_ref, wv_ref, *rest):
    vec_refs = rest[:9]
    out_ref, idx_ref, w_all, v_all, wpack, vpack, tab, lsem, ssem, rsem, xssem, xrsem = rest[9:]
    S = out_ref.shape[1]
    pid = pl.program_id(0)
    me = Place(*where)
    width = wq_ref.shape[1]

    @pl.when(pid == 0)
    def _():
        for n, ref in enumerate((wq_ref, wk_ref, wv_ref)):
            wpack[:, n * width : (n + 1) * width] = ref[...].astype(bf)
        vpack[...] = jnp.zeros_like(vpack)
        for n, ref in enumerate(vec_refs):
            vpack[n : n + 1, : ref.shape[1]] = ref[...].astype(bf)
        me.greet()
        pltpu.make_async_copy(wpack, w_all.at[me.flat], lsem.at[0]).start()
        pltpu.make_async_copy(vpack, v_all.at[me.flat], lsem.at[1]).start()
        send(vpack, v_all.at[me.flat], xssem.at[1], xrsem.at[1], me.partner())
        send(wpack, w_all.at[me.flat], xssem.at[0], xrsem.at[0], me.partner())

        def one(k, c):
            send(vpack, v_all.at[me.flat], ssem.at[1], rsem.at[1], me.peer_device(k))
            send(wpack, w_all.at[me.flat], ssem.at[0], rsem.at[0], me.peer_device(k))
            return c

        lax.fori_loop(1, me.half, one, 0)
        tab[...] = jnp.zeros_like(tab)

        def pack(ref, row, lane):
            fixed = jnp.floor(ref[...].astype(bf).astype(f32) * TABLE_SCALE + 0.5).astype(jnp.int32).T
            n = fixed.shape[1]
            for p in range(6):
                tab[row, p : p + 1, lane : lane + n] = fixed[2 * p : 2 * p + 1] * 65536 + fixed[2 * p + 1 : 2 * p + 2]

        pack(pt_ref, 0, 0)
        pack(xt_ref, 1, 0)
        pack(yt_ref, 1, 64)

    @pl.when(pid == pl.num_programs(0) - 1)
    def _():
        others = pl.ds(0, me.half - 1)
        drain(v_all.at[others], rsem.at[1])
        drain(w_all.at[others], rsem.at[0])

        def one(k, c):
            at = me.flat_of(me.peer(k), me.par)
            send(v_all.at[at], v_all.at[at], xssem.at[1], xrsem.at[1], me.partner())
            send(w_all.at[at], w_all.at[at], xssem.at[0], xrsem.at[0], me.partner())
            return c

        lax.fori_loop(1, me.half, one, 0)

    packed = pos_ref[...] | (x_ref[...] << 5) | (y_ref[...] << 11)
    idx_ref[...] = packed.T
    tp = [jnp.broadcast_to(tab[0, p : p + 1, :], (8, 128)) for p in range(6)]
    tx = [jnp.broadcast_to(tab[1, p : p + 1, :], (8, 128)) for p in range(6)]

    def body(r, c):
        for u in range(4):
            sl = pl.ds(pl.multiple_of((r * 4 + u) * 8, 8), 8)
            t = idx_ref[sl, :]
            p = t & 31
            x = (t >> 5) & 63
            y = (t >> 11) + 64
            g = [take(a, p) for a in tp]
            g = [a + take(b, x) for a, b in zip(g, tx)]
            g = [a + take(b, y) for a, b in zip(g, tx)]
            for k in range(6):
                out_ref[k, sl, :] = g[k]
        return c

    lax.fori_loop(0, S // 32, body, 0)

    @pl.when(pid == pl.num_programs(0) - 1)
    def _():
        others = pl.ds(0, me.half - 1)
        mine = pl.ds(0, me.half)
        pltpu.make_async_copy(wpack, w_all.at[me.flat], lsem.at[0]).wait()
        pltpu.make_async_copy(vpack, v_all.at[me.flat], lsem.at[1]).wait()
        drain(w_all.at[others], ssem.at[0])
        drain(v_all.at[others], ssem.at[1])
        for sem in (xssem, xrsem):
            drain(w_all.at[mine], sem.at[0])
            drain(v_all.at[mine], sem.at[1])


def front_call(where, pos, x, y, tables, weights, vectors):
    S = pos.shape[0]
    share, width = weights[0].shape
    n = where[0] * where[1]

    def whole(a):
        return pl.BlockSpec(a.shape, lambda i: (0,) * a.ndim)

    small = tuple(tables) + tuple(weights) + tuple(v.reshape(1, -1) for v in vectors)
    return pl.pallas_call(
        lambda *a: front_kernel(where, *a),
        grid=(S // BQ,),
        in_specs=[pl.BlockSpec((BQ, S), lambda i: (i, 0))] * 3 + [whole(a) for a in small],
        out_specs=[
            pl.BlockSpec((6, S, BQ), lambda i: (0, 0, i)),
            pl.BlockSpec((S, BQ), lambda i: (0, i)),
            pl.BlockSpec(memory_space=pl.ANY),
            pl.BlockSpec(memory_space=pl.ANY),
        ],
        out_shape=[
            jax.ShapeDtypeStruct((6, S, S), jnp.int32),
            jax.ShapeDtypeStruct((S, S), jnp.int32),
            jax.ShapeDtypeStruct((n, share, 3 * width), bf),
            jax.ShapeDtypeStruct((n, 16, 128), bf),
        ],
        scratch_shapes=[
            pltpu.VMEM((share, 3 * width), bf),
            pltpu.VMEM((16, 128), bf),
            pltpu.VMEM((2, 8, 128), jnp.int32),
        ]
        + [pltpu.SemaphoreType.DMA((2,))] * 5,
        compiler_params=pltpu.CompilerParams(vmem_limit_bytes=VM, collective_id=0, has_side_effects=True),
        name="bias_and_gather",
    )(pos, x, y, *small)


def pack_call(wo, w1, w2):
    share, width = wo.shape

    def kernel(wo_ref, w1_ref, w2_ref, a_ref, b_ref):
        a_ref[:, :width] = wo_ref[...].astype(bf)
        a_ref[:, width:] = w1_ref[...].astype(bf)
        b_ref[...] = w2_ref[...].astype(bf)

    return pl.pallas_call(
        kernel,
        out_shape=[
            jax.ShapeDtypeStruct((share, width + w1.shape[1]), bf),
            jax.ShapeDtypeStruct(w2.shape, bf),
        ],
        name="round_shares",
    )(wo, w1, w2)

def stack2(a):
    lane=lax.broadcasted_iota(jnp.int32,a.shape,1)
    z=jnp.zeros_like(a)
    return jnp.concatenate([jnp.where(lane<64,a,z),jnp.where(lane<64,z,a)],axis=0)

def fwd_kernel(live_ref,q_ref,k_ref,v_ref,b_ref,e_ref,o_ref,l_ref,s_scr,*,CH):
    S=k_ref.shape[0]
    live=live_ref[0]
    c=1.0/(TABLE_SCALE*65536.0)
    nch=S//CH
    rows=lax.broadcasted_iota(jnp.int32,(CH,1),0)
    for p in range(6):
        ln=pl.ds(p*128,128)
        qs=stack2(q_ref[:,ln])
        m=jnp.full((8,256),-3e38,f32)
        for ch in range(nch):
            r=pl.ds(ch*CH,CH)
            s=lax.dot_general(k_ref[r,ln],qs,NT,preferred_element_type=f32)
            b=b_ref[p,r,:]
            b0=b.astype(f32)*c
            b1=(b<<16).astype(f32)*c
            s=s+jnp.concatenate([b0,b1],axis=1)
            s=jnp.where(rows+ch*CH<live,s,-1e9)
            s_scr[r,:]=s
            m=jnp.maximum(m,jnp.max(s.reshape(CH//8,8,256),axis=0))
        mx=jnp.max(m,axis=0,keepdims=True)
        l=jnp.zeros((8,256),f32)
        for ch in range(nch):
            r=pl.ds(ch*CH,CH)
            e=jnp.exp(s_scr[r,:]-mx)
            l=l+jnp.sum(e.reshape(CH//8,8,256),axis=0)
            eb=e.astype(bf)
            e_ref[2*p,r,:]=eb[:,:128]
            e_ref[2*p+1,r,:]=eb[:,128:]
        linv=1.0/jnp.sum(l,axis=0,keepdims=True)
        l_ref[2*p:2*p+1,:]=linv[:,:128]
        l_ref[2*p+1:2*p+2,:]=linv[:,128:]
        acc=jnp.zeros((128,256),f32)
        ecat=jnp.concatenate([e_ref[2*p],e_ref[2*p+1]],axis=1)
        acc=lax.dot_general(v_ref[:,ln],ecat,(((0,),(0,)),((),())),preferred_element_type=f32)
        acc=acc*linv
        sub=lax.broadcasted_iota(jnp.int32,(128,128),0)
        ot=jnp.where(sub<64,acc[:,:128],acc[:,128:])
        o_ref[:,ln]=ot.T.astype(bf)

def fwd_call(live,q,k,v,b,CH=128):
    S,D=k.shape
    full=pl.BlockSpec((S,D),lambda i,*_:(0,0))
    return pl.pallas_call(lambda *a: fwd_kernel(*a,CH=CH),
      grid_spec=pltpu.PrefetchScalarGridSpec(num_scalar_prefetch=1,grid=(S//BQ,),
        in_specs=[pl.BlockSpec((BQ,D),lambda i,*_:(i,0)),full,full,pl.BlockSpec((6,S,BQ),lambda i,*_:(0,0,i))],
        out_specs=[pl.BlockSpec((12,S,BQ),lambda i,*_:(0,0,i)),pl.BlockSpec((BQ,D),lambda i,*_:(i,0)),pl.BlockSpec((16,BQ),lambda i,*_:(0,i))],
        scratch_shapes=[pltpu.VMEM((S,256),f32)]),
      out_shape=[jax.ShapeDtypeStruct((12,S,S),bf),jax.ShapeDtypeStruct((S,D),bf),jax.ShapeDtypeStruct((16,S),f32)],
      compiler_params=pltpu.CompilerParams(vmem_limit_bytes=VM),name="attention_forward")(live,q,k,v,b)


def bwd_kernel(q_ref, do_ref, k_ref, v_ref, e_ref, l_ref, d_ref, dq_ref, dk_ref, dv_ref, ds_ref, ds_scr, dk_acc, dv_acc, cat_scr, *, CH):
    S = k_ref.shape[0]
    pid = pl.program_id(0)

    @pl.when(pid == 0)
    def _():
        dk_acc[...] = jnp.zeros_like(dk_acc)
        dv_acc[...] = jnp.zeros_like(dv_acc)

    nch = S // CH
    for p in range(6):
        ln = pl.ds(p * 128, 128)
        qs = stack2(q_ref[:, ln])
        l2 = l_ref[2 * p : 2 * p + 2, :]
        d2 = d_ref[2 * p : 2 * p + 2, :] * l2
        lcol = jnp.concatenate([l2] * 4, axis=0).T
        lane = lax.broadcasted_iota(jnp.int32, (BQ, 128), 1)
        dos = (do_ref[:, ln].astype(f32) * jnp.where(lane < 64, lcol[:, 0:1], lcol[:, 1:2])).astype(bf)
        dst = stack2(dos)
        for ch in range(nch):
            r = pl.ds(ch * CH, CH)
            dp = lax.dot_general(v_ref[r, ln], dst, NT, preferred_element_type=f32)
            e0 = e_ref[2 * p, r, :]
            e1 = e_ref[2 * p + 1, r, :]
            s0 = e0.astype(f32) * (dp[:, :128] - d2[0:1, :])
            s1 = e1.astype(f32) * (dp[:, 128:] - d2[1:2, :])
            ds_scr[pl.ds(ch * CH * 16 + 2 * p, CH, stride=16), :] = s0
            ds_scr[pl.ds(ch * CH * 16 + 2 * p + 1, CH, stride=16), :] = s1
            sc = jnp.concatenate([s0.astype(bf), s1.astype(bf)], axis=1)
            cat_scr[r, :] = sc
            ec = jnp.concatenate([e0, e1], axis=1)
            dk_acc[r, ln] += lax.dot_general(sc, qs, NN, preferred_element_type=f32)
            dv_acc[r, ln] += lax.dot_general(ec, dst, NN, preferred_element_type=f32)
        a = lax.dot_general(k_ref[:, ln], cat_scr[...], TN, preferred_element_type=f32)
        sub = lax.broadcasted_iota(jnp.int32, (128, 128), 0)
        dq_ref[:, ln] = (jnp.where(sub < 64, a[:, :128], a[:, 128:]).T * 0.125).astype(bf)
    ds_ref[...] = ds_scr[...].astype(bf)

    @pl.when(pid == pl.num_programs(0) - 1)
    def _():
        dk_ref[...] = dk_acc[...].astype(bf)
        dv_ref[...] = dv_acc[...].astype(bf)


def bwd_call(q, do, k, v, e, linv, dd, CH=128):
    S, D = k.shape
    full = pl.BlockSpec((S, D), lambda i: (0, 0))
    blk = pl.BlockSpec((BQ, D), lambda i: (i, 0))
    row = pl.BlockSpec((16, BQ), lambda i: (0, i))
    return pl.pallas_call(
        lambda *a: bwd_kernel(*a, CH=CH),
        grid=(S // BQ,),
        in_specs=[blk, blk, full, full, pl.BlockSpec((12, S, BQ), lambda i: (0, 0, i)), row, row],
        out_specs=[blk, full, full, pl.BlockSpec((S * 16, BQ), lambda i: (0, i))],
        scratch_shapes=[
            pltpu.VMEM((S * 16, BQ), f32),
            pltpu.VMEM((S, D), f32),
            pltpu.VMEM((S, D), f32),
            pltpu.VMEM((S, 256), bf),
        ],
        out_shape=[jax.ShapeDtypeStruct((S, D), bf)] * 3 + [jax.ShapeDtypeStruct((S * 16, S), bf)],
        compiler_params=pltpu.CompilerParams(vmem_limit_bytes=VM),
        name="attention_backward",
    )(q, do, k, v, e, linv, dd)


def tail_kernel(where, U, ds_ref, idx_ref, gw_ref, gv_ref, gp_ref, gx_ref, gy_ref, w_out, v_out, *rest):
    acc, xi_scr, w_in, w_mine, w_recv, v_in, v_mine, v_recv, h_mine, h_in, h_recv, lsem, xssem, xrsem, ssem, rsem = rest
    S = idx_ref.shape[0]
    pid = pl.program_id(0)
    me = Place(*where)
    others = pl.ds(0, me.half - 1)

    @pl.when(pid == 0)
    def _():
        acc[...] = jnp.zeros_like(acc)
        me.greet()
        pltpu.make_async_copy(gw_ref.at[:, me.par], w_mine, lsem.at[0]).start()
        send(gw_ref.at[:, 1 - me.par], w_in, xssem.at[0], xrsem.at[0], me.partner())
        send(gv_ref, v_in, xssem.at[1], xrsem.at[1], me.partner())

    @pl.when(pid == 1)
    def _():
        pltpu.make_async_copy(gw_ref.at[:, me.par], w_mine, lsem.at[0]).wait()
        drain(w_in, xssem.at[0])
        drain(w_in, xrsem.at[0])
        drain(v_in, xssem.at[1])
        drain(v_in, xrsem.at[1])
        v_mine[...] = gv_ref[...] + v_in[...]

        def add(k, c):
            a, b = lax.div(k, me.span), lax.rem(k, me.span)
            w_mine[a, b] = (w_mine[a, b].astype(f32) + w_in[a, b].astype(f32)).astype(bf)
            return c

        lax.fori_loop(0, me.half, add, 0)

        def one(k, c):
            g = me.peer(k)
            send(w_mine.at[lax.div(g, me.span), lax.rem(g, me.span)], w_recv.at[me.group], ssem.at[0], rsem.at[0], me.peer_device(k))
            send(v_mine, v_recv.at[me.group], ssem.at[1], rsem.at[1], me.peer_device(k))
            return c

        lax.fori_loop(1, me.half, one, 0)

    t = idx_ref[...]
    xi_scr[0] = (t & 31).astype(f32)
    xi_scr[1] = ((t >> 5) & 63).astype(f32)
    xi_scr[2] = (t >> 11).astype(f32)
    iot = lax.broadcasted_iota(jnp.int32, (16, 128), 0).astype(f32).astype(bf)
    one = jnp.ones((16, 128), bf)
    zero = jnp.zeros((16, 128), bf)

    def one_j(j):
        bp, bx, by = [jnp.broadcast_to(xi_scr[n, pl.ds(j, 1), :], (16, 128)).astype(bf) for n in range(3)]
        d = ds_ref[pl.ds(pl.multiple_of(j * 16, 16), 16), :]
        xh = bx >= 32
        yh = by >= 32
        bxl = jnp.where(xh, bx - 32, bx)
        byl = jnp.where(yh, by - 32, by)
        rows = [jnp.where(b == iot + bf(16 * k), one, zero) for b in (bxl, byl, bp) for k in range(2)]
        rhs = [d, jnp.where(xh, zero, d), jnp.where(xh, d, zero), jnp.where(yh, zero, d), jnp.where(yh, d, zero)]
        return jnp.concatenate(rows, 0), jnp.concatenate(rhs, 0)

    def body(t, total):
        for u in range(U):
            l0, r0 = one_j(t * 2 * U + 2 * u)
            l1, r1 = one_j(t * 2 * U + 2 * u + 1)
            total = total + lax.dot_general(
                jnp.concatenate([l0, l1], 1), jnp.concatenate([r0, r1], 1), NT, preferred_element_type=f32
            )
        return total

    acc[:, :80] += lax.fori_loop(0, S // (2 * U), body, jnp.zeros((96, 80), f32))

    @pl.when(pid == pl.num_programs(0) - 1)
    def _():
        h = acc[...].T
        parts = [h[16:32, 0:32], h[32:48, 0:32], h[48:64, 32:64], h[64:80, 32:64], h[0:16, 64:96], jnp.zeros((16, 96), f32)]
        h = jnp.concatenate(parts, axis=1)
        h_mine[...] = jnp.where(lax.broadcasted_iota(jnp.int32, h.shape, 0) < 12, h, 0.0)
        send(h_mine, h_in, xssem.at[2], xrsem.at[2], me.partner())
        drain(w_recv.at[others], ssem.at[0])
        drain(w_recv.at[others], rsem.at[0])
        drain(v_recv.at[others], ssem.at[1])
        drain(v_recv.at[others], rsem.at[1])
        drain(h_in, xssem.at[2])
        drain(h_in, xrsem.at[2])
        h_mine[...] = h_mine[...] + h_in[...]

        def one(k, c):
            send(h_mine, h_recv.at[me.group], ssem.at[2], rsem.at[2], me.peer_device(k))
            return c

        lax.fori_loop(1, me.half, one, 0)
        w_out[...] = w_mine[lax.div(me.group, me.span), lax.rem(me.group, me.span)].astype(f32)
        v_out[...] = v_mine[...]

        def add(k, c):
            g = me.peer(k)
            w_out[...] += w_recv[g].astype(f32)
            v_out[...] += v_recv[g]
            return c

        lax.fori_loop(1, me.half, add, 0)
        drain(h_recv.at[others], ssem.at[2])
        drain(h_recv.at[others], rsem.at[2])
        total = lax.fori_loop(1, me.half, lambda k, s: s + h_recv[me.peer(k)], h_mine[...])
        total = jnp.concatenate([total, jnp.zeros((112, 256), f32)], axis=0).T
        gx_ref[...] = total[0:64, 0:12]
        gy_ref[...] = total[64:128, 0:12]
        gp_ref[...] = total[128:160, 0:12]


def tail_call(where, ds, codes, gw, gv, U=32):
    S = codes.shape[0]
    wide, narrow, span = where
    half = wide * narrow // 2
    outer = half // span
    share, cols = gw.shape[3:]
    block = (outer, span, share, cols)

    def whole(shape):
        return pl.BlockSpec(shape, lambda i: (0,) * len(shape))

    outs = [(32, 12), (64, 12), (64, 12), (share, cols), gv.shape]
    return pl.pallas_call(
        lambda *a: tail_kernel(where, U, *a),
        grid=(S // BQ,),
        in_specs=[
            pl.BlockSpec((S * 16, BQ), lambda i: (0, i)),
            pl.BlockSpec((S, BQ), lambda i: (0, i)),
            pl.BlockSpec(memory_space=pl.ANY),
            whole(gv.shape),
        ],
        out_specs=[whole(s) for s in outs],
        out_shape=[jax.ShapeDtypeStruct(s, f32) for s in outs],
        scratch_shapes=[
            pltpu.VMEM((96, 128), f32),
            pltpu.VMEM((3, S, BQ), f32),
            pltpu.VMEM(block, bf),
            pltpu.VMEM(block, bf),
            pltpu.VMEM((half, share, cols), bf),
            pltpu.VMEM(gv.shape, f32),
            pltpu.VMEM(gv.shape, f32),
            pltpu.VMEM((half,) + gv.shape, f32),
            pltpu.VMEM((16, 256), f32),
            pltpu.VMEM((16, 256), f32),
            pltpu.VMEM((half, 16, 256), f32),
            pltpu.SemaphoreType.DMA((1,)),
        ]
        + [pltpu.SemaphoreType.DMA((3,))] * 4,
        compiler_params=pltpu.CompilerParams(vmem_limit_bytes=VM, collective_id=1, has_side_effects=True),
        name="table_sums_and_scatter",
    )(ds, codes, gw, gv)


def norm_rows(values, gain, shift):
    center = values - jnp.mean(values, axis=-1, keepdims=True)
    spread = jnp.mean(center * center, axis=-1, keepdims=True)
    return center * lax.rsqrt(spread + EPS) * gain + shift


def gelu_exact(values):
    return jax.nn.gelu(values, approximate=False)


def gather(shard):
    return lax.all_gather(shard, AXES, axis=0, tiled=True)


def scatter(grad):
    return lax.psum_scatter(grad, AXES, scatter_dimension=0, tiled=True)


def local(where, rows, cotangent, page_rows, pos_bucket, x_bucket, y_bucket, wq, bq, wk, wv, bv, wo, bo,
          ln1_gain, ln1_bias, w1, b1, w2, b2, ln2_gain, ln2_bias, pos_table, x_table, y_table):
    length, width = rows.shape[1:]
    heads = pos_table.shape[1]
    size = width // heads
    share = wq.shape[0]
    wide, narrow, span = where
    n = wide * narrow
    second, down = pack_call(wo, w1, w2)
    second = gather(second)
    w_down = gather(down)
    bias, codes, w_all, v_all = front_call(
        where, pos_bucket[0], x_bucket[0], y_bucket[0], (pos_table, x_table, y_table), (wq, wk, wv),
        (bq, bv, bo, ln1_gain, ln1_bias, b2, ln2_gain, ln2_bias, b1),
    )
    w_qkv = w_all.reshape(width, 3 * width)
    small = jnp.transpose(v_all[:, :8, :share], (1, 0, 2)).reshape(8, width).astype(f32)
    b_query, b_value, b_out, gain_one, shift_one, b_down, gain_two, shift_two = [small[k] for k in range(8)]
    b_up = v_all[:, 8, : 4 * share].reshape(-1).astype(f32)
    w_out = second[:, :width]
    w_up = second[:, width:]
    x_rows = rows[0]
    x_full = x_rows.astype(f32)
    qkv = jnp.dot(x_rows, w_qkv, preferred_element_type=f32)
    query = (qkv[:, :width] + b_query).astype(bf) * bf(0.125)
    keys = qkv[:, width : 2 * width].astype(bf)
    values = (qkv[:, 2 * width :] + b_value).astype(bf)
    prob, attended, inverse = fwd_call(page_rows, query, keys, values, bias)
    mixed = jnp.dot(attended, w_out, preferred_element_type=f32) + b_out
    branch_one = x_full + mixed
    normed_one, pull_one = jax.vjp(norm_rows, branch_one, gain_one, shift_one)
    normed_low = normed_one.astype(bf)
    pre_act = jnp.dot(normed_low, w_up, preferred_element_type=f32) + b_up
    activated, pull_gelu = jax.vjp(gelu_exact, pre_act)
    act_low = activated.astype(bf)
    branch_two = normed_one + jnp.dot(act_low, w_down, preferred_element_type=f32) + b_down
    result, pull_two = jax.vjp(norm_rows, branch_two, gain_two, shift_two)
    out_rows = result.astype(bf)[None]
    live = lax.broadcasted_iota(jnp.int32, (length, 1), 0) < page_rows[0]
    upstream = jnp.where(live, cotangent[0].astype(f32), 0.0)
    d_branch_two, grad_gain_two, grad_shift_two = pull_two(upstream)
    d_ffn = d_branch_two.astype(bf)
    grad_down = jnp.einsum("sf,sd->fd", act_low, d_ffn, preferred_element_type=f32).astype(bf)
    grad_bdown = jnp.sum(d_ffn.astype(f32), axis=0)
    d_act = jnp.einsum("sd,fd->sf", d_ffn, w_down, preferred_element_type=f32)
    (d_pre,) = pull_gelu(d_act)
    d_pre_low = d_pre.astype(bf)
    grad_up = jnp.einsum("sd,sf->df", normed_low, d_pre_low, preferred_element_type=f32).astype(bf)
    grad_bup = jnp.sum(d_pre_low.astype(f32), axis=0)
    d_normed = d_branch_two + jnp.einsum("sf,df->sd", d_pre_low, w_up, preferred_element_type=f32)
    d_branch_one, grad_gain_one, grad_shift_one = pull_one(d_normed)
    d_mixed = d_branch_one.astype(bf)
    grad_out = jnp.einsum("sa,sd->ad", attended, d_mixed, preferred_element_type=f32).astype(bf)
    grad_bout = jnp.sum(d_mixed.astype(f32), axis=0)
    shares = jnp.concatenate([grad_out, grad_up, grad_down.reshape(width, 4 * width)], axis=1)
    d_attended = jnp.einsum("sd,ad->sa", d_mixed, w_out, preferred_element_type=f32).astype(bf)
    shares, d_attended = lax.optimization_barrier((shares, d_attended))
    shares = scatter(shares)
    inner = jnp.sum((d_attended.astype(f32) * attended.astype(f32)).reshape(length, heads, size), axis=-1)
    inner = jnp.pad(inner.T, ((0, 16 - heads), (0, 0)))
    dq, dk, dv, ds = bwd_call(query, d_attended, keys, values, prob, inverse, inner)
    d_qkv = jnp.concatenate([dq, dk, dv], axis=1)
    grad_qkv = jnp.einsum("sd,se->de", x_rows, d_qkv, preferred_element_type=f32).astype(bf)
    grad_bquery = jnp.sum(dq.astype(f32), axis=0)
    grad_bvalue = jnp.sum(dv.astype(f32), axis=0)
    d_rows = d_branch_one + jnp.einsum("se,de->sd", d_qkv, w_qkv, preferred_element_type=f32)
    rows_grad = d_rows.astype(bf)[None]
    sums = jnp.stack([grad_bquery, grad_bvalue, grad_bout, grad_gain_one, grad_shift_one, grad_bdown, grad_gain_two, grad_shift_two], axis=0)
    sums = jnp.concatenate([sums, grad_bup.reshape(4, width), jnp.zeros((4, width), f32)], axis=0)
    grad_qkv = grad_qkv.reshape(n // (2 * span), 2, span, share, 3 * width)
    g_pos, g_x, g_y, share_first, vec = tail_call(where, ds, codes, grad_qkv, sums)
    flat = lax.axis_index("wide") * narrow + lax.axis_index("narrow")
    own = lax.dynamic_slice(vec[:8], (0, flat * share), (8, share))
    own_up = lax.dynamic_slice(vec[8:12].reshape(-1), (flat * 4 * share,), (4 * share,))
    share_down = shares[:, 5 * width :].astype(f32).reshape(4 * share, width)
    return (
        out_rows,
        rows_grad,
        share_first[:, :width],
        own[0],
        share_first[:, width : 2 * width],
        share_first[:, 2 * width :],
        own[1],
        shares[:, :width].astype(f32),
        own[2],
        own[3],
        own[4],
        shares[:, width : 5 * width].astype(f32),
        own_up,
        share_down,
        own[5],
        own[6],
        own[7],
        g_pos,
        g_x,
        g_y,
    )


def solution(mesh):
    wide, narrow = mesh.shape["wide"], mesh.shape["narrow"]
    where = (wide, narrow, 1 if wide <= 8 else narrow)
    cut3 = P(AXES, None, None)
    cut2 = P(AXES, None)
    cut1 = P(AXES)
    params = (cut2, cut1, cut2, cut2, cut1, cut2, cut1, cut1, cut1, cut2, cut1, cut2, cut1, cut1, cut1)
    in_specs = (cut3, cut3, cut1, cut3, cut3, cut3) + params + (P(), P(), P())
    out_specs = (cut3, cut3) + params + (P(), P(), P())
    return jax.shard_map(lambda *a: local(where, *a), mesh=mesh, in_specs=in_specs, out_specs=out_specs, check_vma=False)
```

```python
import jax
import jax.numpy as jnp
from jax import lax
from jax.experimental import pallas as pl
from jax.experimental.pallas import tpu as pltpu
from jax.sharding import PartitionSpec as P

bf = jnp.bfloat16
f32 = jnp.float32
NT = (((1,), (1,)), ((), ()))
NN = (((1,), (0,)), ((), ()))
TN = (((0,), (0,)), ((), ()))
AXES = ("wide", "narrow")
MESH = pl.DeviceIdType.MESH
BQ = 128
VM = 60 << 20
TABLE_SCALE = 3500.0
EPS = 1e-05
SHORTEST = 709


class Place:
    def __init__(self, wide, narrow, span):
        self.n = wide * narrow
        self.half = self.n // 2
        self.narrow = narrow
        self.span = span
        self.outer = self.half // span
        self.flat = lax.axis_index("wide") * narrow + lax.axis_index("narrow")
        self.par = lax.rem(lax.div(self.flat, span), 2)
        self.group = lax.div(self.flat, 2 * span) * span + lax.rem(self.flat, span)

    def flat_of(self, group, par):
        return (lax.div(group, self.span) * 2 + par) * self.span + lax.rem(group, self.span)

    def device(self, flat):
        return (lax.div(flat, self.narrow), lax.rem(flat, self.narrow))

    def peer(self, k):
        return lax.rem(self.group + k, self.half)

    def partner(self):
        return self.device(self.flat_of(self.group, 1 - self.par))

    def peer_device(self, k):
        return self.device(self.flat_of(self.peer(k), self.par))

    def greet(self):
        barrier = pltpu.get_barrier_semaphore()
        pl.semaphore_signal(barrier, inc=1, device_id=self.partner(), device_id_type=MESH)

        def one(k, c):
            pl.semaphore_signal(barrier, inc=1, device_id=self.peer_device(k), device_id_type=MESH)
            return c

        lax.fori_loop(1, self.half, one, 0)
        pl.semaphore_wait(barrier, self.half)


def send(src, dst, send_sem, recv_sem, device):
    pltpu.make_async_remote_copy(src, dst, send_sem, recv_sem, device_id=device, device_id_type=MESH).start()


def drain(ref, sem):
    pltpu.make_async_copy(ref, ref, sem).wait()


def take(t, i):
    return jnp.take_along_axis(t, i, axis=1, mode="promise_in_bounds")


def front_kernel(where, pos_ref, x_ref, y_ref, pt_ref, xt_ref, yt_ref, wq_ref, wk_ref, wv_ref, *rest):
    vec_refs = rest[:9]
    out_ref, idx_ref, w_all, small_ref, up_ref, v_all, wpack, vpack, tab, lsem, ssem, rsem, xssem, xrsem = rest[9:]
    S = out_ref.shape[1]
    pid = pl.program_id(0)
    me = Place(*where)
    width = wq_ref.shape[1]

    @pl.when(pid == 0)
    def _():
        for n, ref in enumerate((wq_ref, wk_ref, wv_ref)):
            wpack[:, n * width : (n + 1) * width] = ref[...].astype(bf)
        vpack[...] = jnp.zeros_like(vpack)
        for n, ref in enumerate(vec_refs):
            vpack[n : n + 1, : ref.shape[1]] = ref[...].astype(bf)
        me.greet()
        pltpu.make_async_copy(wpack, w_all.at[me.flat], lsem.at[0]).start()
        pltpu.make_async_copy(vpack, v_all.at[me.flat], lsem.at[1]).start()
        send(vpack, v_all.at[me.flat], xssem.at[1], xrsem.at[1], me.partner())
        send(wpack, w_all.at[me.flat], xssem.at[0], xrsem.at[0], me.partner())

        def one(k, c):
            send(vpack, v_all.at[me.flat], ssem.at[1], rsem.at[1], me.peer_device(k))
            send(wpack, w_all.at[me.flat], ssem.at[0], rsem.at[0], me.peer_device(k))
            return c

        lax.fori_loop(1, me.half, one, 0)
        tab[...] = jnp.zeros_like(tab)

        def pack(ref, row, lane):
            fixed = jnp.floor(ref[...].astype(bf).astype(f32) * TABLE_SCALE + 0.5).astype(jnp.int32)
            n = fixed.shape[1]
            for p in range(6):
                tab[row, p : p + 1, lane : lane + n] = fixed[2 * p : 2 * p + 1] * 65536 + fixed[2 * p + 1 : 2 * p + 2]

        pack(pt_ref, 0, 0)
        pack(xt_ref, 1, 0)
        pack(yt_ref, 1, 64)

    @pl.when(pid == pl.num_programs(0) - 1)
    def _():
        others = pl.ds(0, me.half - 1)
        drain(v_all.at[others], rsem.at[1])
        drain(w_all.at[others], rsem.at[0])

        def one(k, c):
            at = me.flat_of(me.peer(k), me.par)
            send(v_all.at[at], v_all.at[at], xssem.at[1], xrsem.at[1], me.partner())
            send(w_all.at[at], w_all.at[at], xssem.at[0], xrsem.at[0], me.partner())
            return c

        lax.fori_loop(1, me.half, one, 0)

    packed = pos_ref[...] | (x_ref[...] << 5) | (y_ref[...] << 11)
    idx_ref[...] = packed.T
    tp = [jnp.broadcast_to(tab[0, p : p + 1, :], (8, 128)) for p in range(6)]
    tx = [jnp.broadcast_to(tab[1, p : p + 1, :], (8, 128)) for p in range(6)]

    def body(r, c):
        for u in range(48):
            sl = pl.ds(pl.multiple_of((r * 48 + u) * 8, 8), 8)
            t = idx_ref[sl, :]
            p = t & 31
            x = (t >> 5) & 63
            y = (t >> 11) + 64
            g = [take(a, p) for a in tp]
            g = [a + take(b, x) for a, b in zip(g, tx)]
            g = [a + take(b, y) for a, b in zip(g, tx)]
            for k in range(6):
                out_ref[k, sl, :] = g[k]
        return c

    lax.fori_loop(0, S // (48 * 8), body, 0)

    @pl.when(pid == pl.num_programs(0) - 1)
    def _():
        others = pl.ds(0, me.half - 1)
        mine = pl.ds(0, me.half)
        pltpu.make_async_copy(wpack, w_all.at[me.flat], lsem.at[0]).wait()
        pltpu.make_async_copy(vpack, v_all.at[me.flat], lsem.at[1]).wait()
        drain(w_all.at[others], ssem.at[0])
        drain(v_all.at[others], ssem.at[1])
        for sem in (xssem, xrsem):
            drain(w_all.at[mine], sem.at[0])
            drain(v_all.at[mine], sem.at[1])
        share = wpack.shape[0]
        for d in range(me.n):
            block = v_all[d].astype(f32)
            at = pl.ds(d * share, share)
            small_ref[:, at] = block[0:8, :share]
            for m in range(4):
                up_ref[m : m + 1, at] = block[8:9, m * share : (m + 1) * share]


def front_call(where, pos, x, y, tables, weights, vectors):
    S = pos.shape[0]
    share, width = weights[0].shape
    n = where[0] * where[1]

    def whole(a):
        return pl.BlockSpec(a.shape, lambda i: (0,) * a.ndim)

    small = tuple(tables) + tuple(weights) + tuple(v.reshape(1, -1) for v in vectors)
    return pl.pallas_call(
        lambda *a: front_kernel(where, *a),
        grid=(S // BQ,),
        in_specs=[pl.BlockSpec((BQ, S), lambda i: (i, 0))] * 3 + [whole(a) for a in small],
        out_specs=[
            pl.BlockSpec((6, S, BQ), lambda i: (0, 0, i)),
            pl.BlockSpec((S, BQ), lambda i: (0, i)),
            pl.BlockSpec(memory_space=pl.ANY),
            pl.BlockSpec((8, width), lambda i: (0, 0)),
            pl.BlockSpec((4, width), lambda i: (0, 0)),
        ],
        out_shape=[
            jax.ShapeDtypeStruct((6, S, S), jnp.int32),
            jax.ShapeDtypeStruct((S, S), jnp.int32),
            jax.ShapeDtypeStruct((n, share, 3 * width), bf),
            jax.ShapeDtypeStruct((8, width), f32),
            jax.ShapeDtypeStruct((4, width), f32),
        ],
        scratch_shapes=[
            pltpu.VMEM((n, 16, 128), bf),
            pltpu.VMEM((share, 3 * width), bf),
            pltpu.VMEM((16, 128), bf),
            pltpu.VMEM((2, 8, 128), jnp.int32),
        ]
        + [pltpu.SemaphoreType.DMA((2,))] * 5,
        compiler_params=pltpu.CompilerParams(vmem_limit_bytes=VM, collective_id=0, has_side_effects=True),
        name="bias_and_gather",
    )(pos, x, y, *small)


def pack_call(wo, w1, w2, n):
    share, width = wo.shape
    pieces = share % 8 == 0
    if not pieces:
        w1 = jnp.transpose(w1.reshape(share, n, 4, share), (0, 2, 1, 3)).reshape(share, 4 * width)

    def kernel(wo_ref, w1_ref, w2_ref, a_ref, scr):
        a_ref[:, :width] = wo_ref[...].astype(bf)
        if pieces:
            for d in range(n):
                for m in range(4):
                    at = m * width + d * share
                    scr[:, at : at + share] = w1_ref[:, (4 * d + m) * share : (4 * d + m + 1) * share]
            a_ref[:, width : 5 * width] = scr[...].astype(bf)
        else:
            a_ref[:, width : 5 * width] = w1_ref[...].astype(bf)
        for m in range(4):
            a_ref[:, (5 + m) * width : (6 + m) * width] = w2_ref[m * share : (m + 1) * share, :].astype(bf)

    return pl.pallas_call(
        kernel,
        out_shape=jax.ShapeDtypeStruct((share, 9 * width), bf),
        scratch_shapes=[pltpu.VMEM((share, 4 * width), f32)],
        name="round_shares",
    )(wo, w1, w2)


def finish_call(shares, first, vec, tables, n, narrow):
    share, width = shares.shape[0], vec.shape[1]
    pieces = share % 8 == 0

    def kernel(s_ref, f_ref, v_ref, t_ref, wo_ref, w1_ref, w2_ref, wq_ref, wk_ref, wv_ref, gp_ref, gx_ref, gy_ref, *rest):
        vec_refs, scr = rest[:9], rest[9]
        for k, ref in enumerate((wq_ref, wk_ref, wv_ref)):
            ref[...] = f_ref[:, k * width : (k + 1) * width]
        gx_ref[...] = t_ref[0:12, 0:64]
        gy_ref[...] = t_ref[0:12, 64:128]
        gp_ref[...] = t_ref[0:12, 128:160]
        flat = lax.axis_index("wide") * narrow + lax.axis_index("narrow")
        wo_ref[...] = s_ref[:, :width].astype(f32)
        scr[...] = s_ref[:, width : 5 * width].astype(f32)
        if pieces:
            for d in range(n):
                for m in range(4):
                    at = m * width + d * share
                    w1_ref[:, (4 * d + m) * share : (4 * d + m + 1) * share] = scr[:, at : at + share]
        else:
            w1_ref[...] = scr[...]
        for m in range(4):
            w2_ref[m * share : (m + 1) * share, :] = s_ref[:, (5 + m) * width : (6 + m) * width].astype(f32)
        own = jnp.zeros((16, share), f32)
        for d in range(n):
            own = jnp.where(flat == d, v_ref[:, d * share : (d + 1) * share], own)
        for k in range(8):
            vec_refs[k][...] = own[k : k + 1, :]
        for m in range(4):
            vec_refs[8][:, m * share : (m + 1) * share] = own[8 + m : 9 + m, :]

    outs = [(share, width), (share, 4 * width), (4 * share, width)] + [(share, width)] * 3 + [(12, 32), (12, 64), (12, 64)] + [(1, share)] * 8 + [(1, 4 * share)]
    outs = pl.pallas_call(
        kernel,
        out_shape=[jax.ShapeDtypeStruct(s, f32) for s in outs],
        scratch_shapes=[pltpu.VMEM((share, 4 * width), f32)],
        name="own_shares",
    )(shares, first, vec, tables)
    g_up = outs[1]
    if not pieces:
        g_up = jnp.transpose(g_up.reshape(share, 4, n, share), (0, 2, 1, 3)).reshape(share, 4 * width)
    return [outs[0], g_up, outs[2], *outs[3:6], *[t.T for t in outs[6:9]], [v.reshape(-1) for v in outs[9:]]]


def stack2(a):
    lane=lax.broadcasted_iota(jnp.int32,a.shape,1)
    z=jnp.zeros_like(a)
    return jnp.concatenate([jnp.where(lane<64,a,z),jnp.where(lane<64,z,a)],axis=0)

def fwd_kernel(live_ref,q_ref,k_ref,v_ref,b_ref,e_ref,o_ref,l_ref,s_scr,*,CH):
    S=k_ref.shape[0]
    live=live_ref[0]
    c=1.0/(TABLE_SCALE*65536.0)
    nch=S//CH
    rows=lax.broadcasted_iota(jnp.int32,(CH,1),0)
    for p in range(6):
        ln=pl.ds(p*128,128)
        qs=stack2(q_ref[:,ln])
        m=jnp.full((8,256),-3e38,f32)
        for ch in range(nch):
            r=pl.ds(ch*CH,CH)
            s=lax.dot_general(k_ref[r,ln],qs,NT,preferred_element_type=f32)
            b=b_ref[p,r,:]
            b0=b.astype(f32)*c
            b1=(b<<16).astype(f32)*c
            s=s+jnp.concatenate([b0,b1],axis=1)
            if (ch+1)*CH>SHORTEST: s=jnp.where(rows+ch*CH<live,s,-1e9)
            s_scr[r,:]=s
            m=jnp.maximum(m,jnp.max(s.reshape(CH//8,8,256),axis=0))
        mx=jnp.max(m,axis=0,keepdims=True)
        l=jnp.zeros((8,256),f32)
        for ch in range(nch):
            r=pl.ds(ch*CH,CH)
            e=jnp.exp(s_scr[r,:]-mx)
            l=l+jnp.sum(e.reshape(CH//8,8,256),axis=0)
            eb=e.astype(bf)
            e_ref[2*p,r,:]=eb[:,:128]
            e_ref[2*p+1,r,:]=eb[:,128:]
        linv=1.0/jnp.sum(l,axis=0,keepdims=True)
        l_ref[2*p:2*p+1,:]=linv[:,:128]
        l_ref[2*p+1:2*p+2,:]=linv[:,128:]
        acc=jnp.zeros((128,256),f32)
        ecat=jnp.concatenate([e_ref[2*p],e_ref[2*p+1]],axis=1)
        acc=lax.dot_general(v_ref[:,ln],ecat,(((0,),(0,)),((),())),preferred_element_type=f32)
        acc=acc*linv
        sub=lax.broadcasted_iota(jnp.int32,(128,128),0)
        ot=jnp.where(sub<64,acc[:,:128],acc[:,128:])
        o_ref[:,ln]=ot.T.astype(bf)

def fwd_call(live,q,k,v,b,CH=128):
    S,D=k.shape
    full=pl.BlockSpec((S,D),lambda i,*_:(0,0))
    return pl.pallas_call(lambda *a: fwd_kernel(*a,CH=CH),
      grid_spec=pltpu.PrefetchScalarGridSpec(num_scalar_prefetch=1,grid=(S//BQ,),
        in_specs=[pl.BlockSpec((BQ,D),lambda i,*_:(i,0)),full,full,pl.BlockSpec((6,S,BQ),lambda i,*_:(0,0,i))],
        out_specs=[pl.BlockSpec((12,S,BQ),lambda i,*_:(0,0,i)),pl.BlockSpec((BQ,D),lambda i,*_:(i,0)),pl.BlockSpec((16,BQ),lambda i,*_:(0,i))],
        scratch_shapes=[pltpu.VMEM((S,256),f32)]),
      out_shape=[jax.ShapeDtypeStruct((12,S,S),bf),jax.ShapeDtypeStruct((S,D),bf),jax.ShapeDtypeStruct((16,S),f32)],
      compiler_params=pltpu.CompilerParams(vmem_limit_bytes=VM),name="attention_forward")(live,q,k,v,b)


def bwd_kernel(q_ref, do_ref, k_ref, v_ref, e_ref, l_ref, d_ref, dq_ref, dk_ref, dv_ref, ds_ref, ds_scr, dk_acc, dv_acc, cat_scr, *, CH):
    S = k_ref.shape[0]
    pid = pl.program_id(0)

    @pl.when(pid == 0)
    def _():
        dk_acc[...] = jnp.zeros_like(dk_acc)
        dv_acc[...] = jnp.zeros_like(dv_acc)

    nch = S // CH
    for p in range(6):
        ln = pl.ds(p * 128, 128)
        qs = stack2(q_ref[:, ln])
        l2 = l_ref[2 * p : 2 * p + 2, :]
        d2 = d_ref[2 * p : 2 * p + 2, :] * l2
        lcol = jnp.concatenate([l2] * 4, axis=0).T
        lane = lax.broadcasted_iota(jnp.int32, (BQ, 128), 1)
        dos = (do_ref[:, ln].astype(f32) * jnp.where(lane < 64, lcol[:, 0:1], lcol[:, 1:2])).astype(bf)
        dst = stack2(dos)
        for ch in range(nch):
            r = pl.ds(ch * CH, CH)
            dp = lax.dot_general(v_ref[r, ln], dst, NT, preferred_element_type=f32)
            e0 = e_ref[2 * p, r, :]
            e1 = e_ref[2 * p + 1, r, :]
            s0 = e0.astype(f32) * (dp[:, :128] - d2[0:1, :])
            s1 = e1.astype(f32) * (dp[:, 128:] - d2[1:2, :])
            ds_scr[pl.ds(ch * CH * 16 + 2 * p, CH, stride=16), :] = s0
            ds_scr[pl.ds(ch * CH * 16 + 2 * p + 1, CH, stride=16), :] = s1
            sc = jnp.concatenate([s0.astype(bf), s1.astype(bf)], axis=1)
            cat_scr[r, :] = sc
            ec = jnp.concatenate([e0, e1], axis=1)
            dk_acc[r, ln] += lax.dot_general(sc, qs, NN, preferred_element_type=f32)
            dv_acc[r, ln] += lax.dot_general(ec, dst, NN, preferred_element_type=f32)
        a = lax.dot_general(k_ref[:, ln], cat_scr[...], TN, preferred_element_type=f32)
        sub = lax.broadcasted_iota(jnp.int32, (128, 128), 0)
        dq_ref[:, ln] = (jnp.where(sub < 64, a[:, :128], a[:, 128:]).T * 0.125).astype(bf)
    ds_ref[...] = ds_scr[...].astype(bf)

    @pl.when(pid == pl.num_programs(0) - 1)
    def _():
        dk_ref[...] = dk_acc[...].astype(bf)
        dv_ref[...] = dv_acc[...].astype(bf)


def bwd_call(q, do, k, v, e, linv, dd, CH=128):
    S, D = k.shape
    full = pl.BlockSpec((S, D), lambda i: (0, 0))
    blk = pl.BlockSpec((BQ, D), lambda i: (i, 0))
    row = pl.BlockSpec((16, BQ), lambda i: (0, i))
    return pl.pallas_call(
        lambda *a: bwd_kernel(*a, CH=CH),
        grid=(S // BQ,),
        in_specs=[blk, blk, full, full, pl.BlockSpec((12, S, BQ), lambda i: (0, 0, i)), row, row],
        out_specs=[blk, full, full, pl.BlockSpec((S * 16, BQ), lambda i: (0, i))],
        scratch_shapes=[
            pltpu.VMEM((S * 16, BQ), f32),
            pltpu.VMEM((S, D), f32),
            pltpu.VMEM((S, D), f32),
            pltpu.VMEM((S, 256), bf),
        ],
        out_shape=[jax.ShapeDtypeStruct((S, D), bf)] * 3 + [jax.ShapeDtypeStruct((S * 16, S), bf)],
        compiler_params=pltpu.CompilerParams(vmem_limit_bytes=VM),
        name="attention_backward",
    )(q, do, k, v, e, linv, dd)


def tail_kernel(where, U, ds_ref, idx_ref, gw_ref, gv_ref, t_ref, w_out, v_out, *rest):
    acc, xi_scr, w_in, w_mine, w_recv, v_in, v_mine, v_recv, h_mine, h_in, h_recv, lsem, xssem, xrsem, ssem, rsem = rest
    S = idx_ref.shape[0]
    pid = pl.program_id(0)
    me = Place(*where)
    others = pl.ds(0, me.half - 1)

    @pl.when(pid == 0)
    def _():
        acc[...] = jnp.zeros_like(acc)
        me.greet()
        pltpu.make_async_copy(gw_ref.at[:, me.par], w_mine, lsem.at[0]).start()
        send(gw_ref.at[:, 1 - me.par], w_in, xssem.at[0], xrsem.at[0], me.partner())
        send(gv_ref, v_in, xssem.at[1], xrsem.at[1], me.partner())

    @pl.when(pid == 1)
    def _():
        pltpu.make_async_copy(gw_ref.at[:, me.par], w_mine, lsem.at[0]).wait()
        drain(w_in, xssem.at[0])
        drain(w_in, xrsem.at[0])
        drain(v_in, xssem.at[1])
        drain(v_in, xrsem.at[1])
        v_mine[...] = gv_ref[...] + v_in[...]

        def add(k, c):
            a, b = lax.div(k, me.span), lax.rem(k, me.span)
            w_mine[a, b] = (w_mine[a, b].astype(f32) + w_in[a, b].astype(f32)).astype(bf)
            return c

        lax.fori_loop(0, me.half, add, 0)

        def one(k, c):
            g = me.peer(k)
            send(w_mine.at[lax.div(g, me.span), lax.rem(g, me.span)], w_recv.at[me.group], ssem.at[0], rsem.at[0], me.peer_device(k))
            send(v_mine, v_recv.at[me.group], ssem.at[1], rsem.at[1], me.peer_device(k))
            return c

        lax.fori_loop(1, me.half, one, 0)

    t = idx_ref[...]
    xi_scr[0] = (t & 31).astype(f32)
    xi_scr[1] = ((t >> 5) & 63).astype(f32)
    xi_scr[2] = (t >> 11).astype(f32)
    iot = lax.broadcasted_iota(jnp.int32, (16, 128), 0).astype(f32).astype(bf)
    one = jnp.ones((16, 128), bf)
    zero = jnp.zeros((16, 128), bf)

    def one_j(j):
        bp, bx, by = [jnp.broadcast_to(xi_scr[n, pl.ds(j, 1), :], (16, 128)).astype(bf) for n in range(3)]
        d = ds_ref[pl.ds(pl.multiple_of(j * 16, 16), 16), :]
        xh = bx >= 32
        yh = by >= 32
        bxl = jnp.where(xh, bx - 32, bx)
        byl = jnp.where(yh, by - 32, by)
        ph = bp >= 16
        bpl = jnp.where(ph, bp - 16, bp)
        rows = [jnp.where(b == iot + bf(16 * k), one, zero) for b in (bxl, byl) for k in range(2)]
        rows.append(jnp.where(bpl == iot, one, zero))
        rhs = [d, jnp.where(xh, d, zero), jnp.where(yh, d, zero), jnp.where(ph, d, zero)]
        return jnp.concatenate(rows, 0), jnp.concatenate(rhs, 0)

    def body(t, total):
        for u in range(U):
            l0, r0 = one_j(t * 2 * U + 2 * u)
            l1, r1 = one_j(t * 2 * U + 2 * u + 1)
            total = total + lax.dot_general(
                jnp.concatenate([l0, l1], 1), jnp.concatenate([r0, r1], 1), NT, preferred_element_type=f32
            )
        return total

    acc[:, :64] += lax.fori_loop(0, S // (2 * U), body, jnp.zeros((80, 64), f32))

    @pl.when(pid == pl.num_programs(0) - 1)
    def _():
        h = acc[...].T
        total, x1, y1, p1 = h[0:16], h[16:32, 0:32], h[32:48, 32:64], h[48:64, 64:80]
        parts = [total[:, 0:32] - x1, x1, total[:, 32:64] - y1, y1, total[:, 64:80] - p1, p1, jnp.zeros((16, 96), f32)]
        h = jnp.concatenate(parts, axis=1)
        h_mine[...] = jnp.where(lax.broadcasted_iota(jnp.int32, h.shape, 0) < 12, h, 0.0)
        send(h_mine, h_in, xssem.at[2], xrsem.at[2], me.partner())
        drain(w_recv.at[others], ssem.at[0])
        drain(w_recv.at[others], rsem.at[0])
        drain(v_recv.at[others], ssem.at[1])
        drain(v_recv.at[others], rsem.at[1])
        drain(h_in, xssem.at[2])
        drain(h_in, xrsem.at[2])
        h_mine[...] = h_mine[...] + h_in[...]

        def one(k, c):
            send(h_mine, h_recv.at[me.group], ssem.at[2], rsem.at[2], me.peer_device(k))
            return c

        lax.fori_loop(1, me.half, one, 0)
        w_out[...] = w_mine[lax.div(me.group, me.span), lax.rem(me.group, me.span)].astype(f32)
        v_out[...] = v_mine[...]

        def add(k, c):
            g = me.peer(k)
            w_out[...] += w_recv[g].astype(f32)
            v_out[...] += v_recv[g]
            return c

        lax.fori_loop(1, me.half, add, 0)
        drain(h_recv.at[others], ssem.at[2])
        drain(h_recv.at[others], rsem.at[2])
        t_ref[...] = lax.fori_loop(1, me.half, lambda k, s: s + h_recv[me.peer(k)], h_mine[...])


def tail_call(where, ds, codes, gw, gv, U=96):
    S = codes.shape[0]
    wide, narrow, span = where
    half = wide * narrow // 2
    outer = half // span
    share, cols = gw.shape[3:]
    block = (outer, span, share, cols)

    def whole(shape):
        return pl.BlockSpec(shape, lambda i: (0,) * len(shape))

    outs = [(16, 256), (share, cols), gv.shape]
    return pl.pallas_call(
        lambda *a: tail_kernel(where, U, *a),
        grid=(S // BQ,),
        in_specs=[
            pl.BlockSpec((S * 16, BQ), lambda i: (0, i)),
            pl.BlockSpec((S, BQ), lambda i: (0, i)),
            pl.BlockSpec(memory_space=pl.ANY),
            whole(gv.shape),
        ],
        out_specs=[whole(s) for s in outs],
        out_shape=[jax.ShapeDtypeStruct(s, f32) for s in outs],
        scratch_shapes=[
            pltpu.VMEM((80, 128), f32),
            pltpu.VMEM((3, S, BQ), f32),
            pltpu.VMEM(block, bf),
            pltpu.VMEM(block, bf),
            pltpu.VMEM((half, share, cols), bf),
            pltpu.VMEM(gv.shape, f32),
            pltpu.VMEM(gv.shape, f32),
            pltpu.VMEM((half,) + gv.shape, f32),
            pltpu.VMEM((16, 256), f32),
            pltpu.VMEM((16, 256), f32),
            pltpu.VMEM((half, 16, 256), f32),
            pltpu.SemaphoreType.DMA((1,)),
        ]
        + [pltpu.SemaphoreType.DMA((3,))] * 4,
        compiler_params=pltpu.CompilerParams(vmem_limit_bytes=VM, collective_id=1, has_side_effects=True),
        name="table_sums_and_scatter",
    )(ds, codes, gw, gv)


GELU_COEFS = (0.254829592, -0.284496736, 1.421413741, -1.453152027, 1.061405429)


def gelu_both(z):
    t = pltpu.reciprocal(1.0 + (0.3275911 * 0.7071067811865476) * jnp.abs(z), approx=False)
    q = jnp.exp(z * z * -0.5)
    poly = 0.5 * GELU_COEFS[4] * t + 0.5 * GELU_COEFS[3]
    for c in GELU_COEFS[2::-1]:
        poly = poly * t + 0.5 * c
    half = poly * t * q
    cdf = jnp.where(z >= 0, 1.0 - half, half)
    return z * cdf, cdf + z * (q * 0.3989422804014327)


def norm_stats(u):
    mean = jnp.mean(u, axis=-1, keepdims=True)
    center = u - mean
    inv = lax.rsqrt(jnp.mean(center * center, axis=-1, keepdims=True) + EPS)
    return center * inv, inv


def norm_pull(e, normed, inv):
    return (e - jnp.mean(e, axis=-1, keepdims=True) - normed * jnp.mean(e * normed, axis=-1, keepdims=True)) * inv


def fold8(u):
    return jnp.sum(u.reshape(u.shape[0] // 8, 8, u.shape[1]), axis=0)


def row_kernel(live_ref, at_ref, x_ref, ct_ref, w_ref, v_ref, b1_ref,
               out_ref, h_ref, g_ref, df_ref, dz_ref, da_ref, dr_ref, dat_ref, dd_ref, sum_ref, sb1_ref,
               gp_scr, z_scr, acc, h_scr, n1_scr, i1_scr, *, R, SL):
    pid = pl.program_id(0)
    D = x_ref.shape[1]
    live = live_ref[0]
    b_out, g1, s1, b_down, g2, s2 = [v_ref[n : n + 1, :] for n in range(2, 8)]

    @pl.when(pid == 0)
    def _():
        sum_ref[...] = jnp.zeros_like(sum_ref)
        sb1_ref[...] = jnp.zeros_like(sb1_ref)

    def add(row, part):
        sum_ref[row : row + 1, :] += jnp.sum(part, axis=0, keepdims=True)

    acc[...] = lax.dot_general(at_ref[...], w_ref[:, :D], NN, preferred_element_type=f32)
    for r in range(0, R, SL):
        sl = pl.ds(r, SL)
        n1, inv = norm_stats(x_ref[sl, :].astype(f32) + acc[sl, :] + b_out)
        n1_scr[sl, :] = n1
        i1_scr[sl, :] = jnp.broadcast_to(inv, (SL, 128))
        h1 = n1 * g1 + s1
        h_scr[sl, :] = h1
        h_ref[sl, :] = h1.astype(bf)
    for c in range(4):
        cols = pl.ds(c * D, D)
        z_scr[c % 2] = lax.dot_general(h_ref[...], w_ref[:, pl.ds((1 + c) * D, D)], NN, preferred_element_type=f32)
        for r in range(0, R, SL):
            sl = pl.ds(r, SL)
            g, gp = gelu_both(z_scr[c % 2, sl, :] + b1_ref[c : c + 1, :])
            g_ref[sl, cols] = g.astype(bf)
            gp_scr[sl, cols] = gp
        part = lax.dot_general(g_ref[:, cols], w_ref[:, pl.ds((5 + c) * D, D)], NN, preferred_element_type=f32)
        if c == 0:
            acc[...] = part
        else:
            acc[...] += part
    p_gain = p_shift = p_down = jnp.zeros((8, D), f32)
    rows = lax.broadcasted_iota(jnp.int32, (SL, 1), 0) + pid * R
    for r in range(0, R, SL):
        sl = pl.ds(r, SL)
        n2, inv = norm_stats(h_scr[sl, :] + acc[sl, :] + b_down)
        out_ref[sl, :] = (n2 * g2 + s2).astype(bf)
        dy = jnp.where(rows + r < live, ct_ref[sl, :].astype(f32), 0.0)
        dr2 = norm_pull(dy * g2, n2, inv)
        df = dr2.astype(bf)
        df_ref[sl, :] = df
        h_scr[sl, :] = dr2
        p_gain = p_gain + fold8(dy * n2)
        p_shift = p_shift + fold8(dy)
        p_down = p_down + fold8(df.astype(f32))
    add(5, p_down)
    add(6, p_gain)
    add(7, p_shift)
    for c in range(4):
        cols = pl.ds(c * D, D)
        z_scr[c % 2] = lax.dot_general(df_ref[...], w_ref[:, pl.ds((5 + c) * D, D)], NT, preferred_element_type=f32)
        p_up = jnp.zeros((8, D), f32)
        for r in range(0, R, SL):
            sl = pl.ds(r, SL)
            dz = (z_scr[c % 2, sl, :] * gp_scr[sl, cols]).astype(bf)
            dz_ref[sl, cols] = dz
            p_up = p_up + fold8(dz.astype(f32))
        sb1_ref[c : c + 1, :] += jnp.sum(p_up, axis=0, keepdims=True)
        part = lax.dot_general(dz_ref[:, cols], w_ref[:, pl.ds((1 + c) * D, D)], NT, preferred_element_type=f32)
        if c == 0:
            acc[...] = part
        else:
            acc[...] += part
    p_gain = p_shift = p_out = jnp.zeros((8, D), f32)
    for r in range(0, R, SL):
        sl = pl.ds(r, SL)
        dh = h_scr[sl, :] + acc[sl, :]
        n1 = n1_scr[sl, :]
        dr1 = norm_pull(dh * g1, n1, i1_scr[sl, 0:1])
        da = dr1.astype(bf)
        dr_ref[sl, :] = dr1
        da_ref[sl, :] = da
        p_gain = p_gain + fold8(dh * n1)
        p_shift = p_shift + fold8(dh)
        p_out = p_out + fold8(da.astype(f32))
    add(2, p_out)
    add(3, p_gain)
    add(4, p_shift)
    dat_ref[...] = lax.dot_general(da_ref[...], w_ref[:, :D], NT, preferred_element_type=f32).astype(bf)
    seg = (lax.div(lax.broadcasted_iota(jnp.int32, (D, 128), 0), 64) == lax.broadcasted_iota(jnp.int32, (D, 128), 1)).astype(f32).astype(bf)
    for r in range(0, R, 128):
        sl = pl.ds(r, 128)
        prod = dat_ref[sl, :].astype(f32) * at_ref[sl, :].astype(f32)
        high = prod.astype(bf)
        low = (prod - high.astype(f32)).astype(bf)
        d = lax.dot_general(high, seg, NN, preferred_element_type=f32) + lax.dot_general(low, seg, NN, preferred_element_type=f32)
        dd_ref[:, sl] = d.T[0:16, :]


def row_call(live, attended, x, ct, w, v, b1, R=384, SL=16):
    S, D = x.shape
    blk = pl.BlockSpec((R, D), lambda i, *_: (i, 0))
    big = pl.BlockSpec((R, 4 * D), lambda i, *_: (i, 0))

    def whole(shape, **kw):
        return pl.BlockSpec(shape, lambda i, *_: (0,) * len(shape), **kw)

    shapes = [((S, D), bf), ((S, D), bf), ((S, 4 * D), bf), ((S, D), bf), ((S, 4 * D), bf), ((S, D), bf), ((S, D), f32), ((S, D), bf),
              ((16, S), f32), ((8, D), f32), ((4, D), f32)]
    return pl.pallas_call(
        lambda *a: row_kernel(*a, R=R, SL=SL),
        grid_spec=pltpu.PrefetchScalarGridSpec(
            num_scalar_prefetch=1,
            grid=(S // R,),
            in_specs=[blk, blk, blk, whole(w.shape, pipeline_mode=pl.Buffered(1)), whole(v.shape), whole(b1.shape)],
            out_specs=[blk, blk, big, blk, big, blk, blk, blk, pl.BlockSpec((16, R), lambda i, *_: (0, i)), whole((8, D)), whole((4, D))],
            scratch_shapes=[
                pltpu.VMEM((R, 4 * D), f32),
                pltpu.VMEM((2, R, D), f32),
                pltpu.VMEM((R, D), f32),
                pltpu.VMEM((R, D), f32),
                pltpu.VMEM((R, D), f32),
                pltpu.VMEM((R, 128), f32),
            ],
        ),
        out_shape=[jax.ShapeDtypeStruct(s, d) for s, d in shapes],
        compiler_params=pltpu.CompilerParams(vmem_limit_bytes=VM),
        name="rows_forward_backward",
    )(live, attended, x, ct, w, v, b1)


def share_kernel(at_ref, h_ref, g_ref, da_ref, dz_ref, df_ref, out_ref):
    c = pl.program_id(0)

    @pl.when(c == 0)
    def _():
        out_ref[...] = lax.dot_general(at_ref[...], da_ref[...], TN, preferred_element_type=f32).astype(bf)

    @pl.when((c > 0) & (c < 5))
    def _():
        out_ref[...] = lax.dot_general(h_ref[...], dz_ref[...], TN, preferred_element_type=f32).astype(bf)

    @pl.when(c > 4)
    def _():
        out_ref[...] = lax.dot_general(g_ref[...], df_ref[...], TN, preferred_element_type=f32).astype(bf)


def share_call(attended, h, g, da, dz, df):
    S, D = h.shape

    def fixed():
        return pl.BlockSpec((S, D), lambda c: (0, 0), pipeline_mode=pl.Buffered(1))

    return pl.pallas_call(
        share_kernel,
        grid=(9,),
        in_specs=[
            fixed(),
            fixed(),
            pl.BlockSpec((S, D), lambda c: (0, jnp.clip(c - 5, 0, 3))),
            fixed(),
            pl.BlockSpec((S, D), lambda c: (0, jnp.clip(c - 1, 0, 3))),
            fixed(),
        ],
        out_specs=pl.BlockSpec((D, D), lambda c: (0, c)),
        out_shape=jax.ShapeDtypeStruct((D, 9 * D), bf),
        compiler_params=pltpu.CompilerParams(vmem_limit_bytes=VM),
        name="weight_gradients",
    )(attended, h, g, da, dz, df)


def qkv_call(x, w, v, R=384):
    S, D = x.shape

    def kernel(x_ref, w_ref, v_ref, q_ref, k_ref, o_ref):
        x = x_ref[...]
        q_ref[...] = (lax.dot_general(x, w_ref[:, :D], NN, preferred_element_type=f32) + v_ref[0:1, :]).astype(bf) * bf(0.125)
        k_ref[...] = lax.dot_general(x, w_ref[:, D : 2 * D], NN, preferred_element_type=f32).astype(bf)
        o_ref[...] = (lax.dot_general(x, w_ref[:, 2 * D :], NN, preferred_element_type=f32) + v_ref[1:2, :]).astype(bf)

    blk = pl.BlockSpec((R, D), lambda i: (i, 0))
    return pl.pallas_call(
        kernel,
        grid=(S // R,),
        in_specs=[blk, pl.BlockSpec(w.shape, lambda i: (0, 0), pipeline_mode=pl.Buffered(1)), pl.BlockSpec(v.shape, lambda i: (0, 0))],
        out_specs=[blk] * 3,
        out_shape=[jax.ShapeDtypeStruct((S, D), bf)] * 3,
        compiler_params=pltpu.CompilerParams(vmem_limit_bytes=VM),
        name="project_qkv",
    )(x, w, v)


def input_kernel(x_ref, dq_ref, dk_ref, dv_ref, dr_ref, w_ref, s_ref, b1_ref, gw_ref, rg_ref, v_ref):
    D = x_ref.shape[1]
    for n, ref in enumerate((dq_ref, dk_ref, dv_ref)):
        gw_ref[:, n * D : (n + 1) * D] = lax.dot_general(x_ref[...], ref[...], TN, preferred_element_type=f32).astype(bf)
    S = x_ref.shape[0]
    v_ref[...] = jnp.concatenate([s_ref[...], b1_ref[...], jnp.zeros((4, D), f32)], axis=0)
    for row, ref in ((0, dq_ref), (1, dv_ref)):
        part = jnp.zeros((8, D), f32)
        for r in range(0, S, 64):
            part = part + fold8(ref[pl.ds(r, 64), :].astype(f32))
        v_ref[row : row + 1, :] = jnp.sum(part, axis=0, keepdims=True)
    for r in range(0, S, 384):
        sl = pl.ds(r, 384)
        total = dr_ref[sl, :]
        for n, ref in enumerate((dq_ref, dk_ref, dv_ref)):
            total = total + lax.dot_general(ref[sl, :], w_ref[:, n * D : (n + 1) * D], NT, preferred_element_type=f32)
        rg_ref[sl, :] = total.astype(bf)


def input_call(x, dq, dk, dv, dr, w, sums, sb1):
    S, D = x.shape
    return pl.pallas_call(
        input_kernel,
        out_shape=[jax.ShapeDtypeStruct((D, 3 * D), bf), jax.ShapeDtypeStruct((S, D), bf), jax.ShapeDtypeStruct((16, D), f32)],
        compiler_params=pltpu.CompilerParams(vmem_limit_bytes=VM),
        name="input_gradients",
    )(x, dq, dk, dv, dr, w, sums, sb1)


def gather(shard):
    return lax.all_gather(shard, AXES, axis=0, tiled=True)


def scatter(grad):
    return lax.psum_scatter(grad, AXES, scatter_dimension=0, tiled=True)


def local(where, rows, cotangent, page_rows, pos_bucket, x_bucket, y_bucket, wq, bq, wk, wv, bv, wo, bo,
          ln1_gain, ln1_bias, w1, b1, w2, b2, ln2_gain, ln2_bias, pos_table, x_table, y_table):
    length, width = rows.shape[1:]
    share = wq.shape[0]
    wide, narrow, span = where
    n = wide * narrow
    w_rest = gather(pack_call(wo, w1, w2, n))
    bias, codes, w_all, small, b_up = front_call(
        where, pos_bucket[0], x_bucket[0], y_bucket[0], (pos_table.T, x_table.T, y_table.T), (wq, wk, wv),
        (bq, bv, bo, ln1_gain, ln1_bias, b2, ln2_gain, ln2_bias, b1),
    )
    w_qkv = w_all.reshape(width, 3 * width)
    query, keys, values = qkv_call(rows[0], w_qkv, small)
    prob, attended, inverse = fwd_call(page_rows, query, keys, values, bias)
    out_rows, normed, act, d_ffn, d_pre, d_mixed, d_branch, d_attended, inner, sums, sum_up = row_call(
        page_rows, attended, rows[0], cotangent[0], w_rest, small, b_up
    )
    shares = share_call(attended, normed, act, d_mixed, d_pre, d_ffn)
    shares, d_attended = lax.optimization_barrier((shares, d_attended))
    shares = scatter(shares)
    dq, dk, dv, ds = bwd_call(query, d_attended, keys, values, prob, inverse, inner)
    grad_qkv, rows_grad, sums = input_call(rows[0], dq, dk, dv, d_branch, w_qkv, sums, sum_up)
    grad_qkv = grad_qkv.reshape(n // (2 * span), 2, span, share, 3 * width)
    tables, first, vec = tail_call(where, ds, codes, grad_qkv, sums)
    g_out, g_up, g_down, g_query, g_key, g_value, g_pos, g_x, g_y, own = finish_call(shares, first, vec, tables, n, narrow)
    return (
        out_rows[None], rows_grad[None], g_query, own[0], g_key, g_value, own[1], g_out, own[2], own[3], own[4],
        g_up, own[8], g_down, own[5], own[6], own[7], g_pos, g_x, g_y,
    )


def solution(mesh):
    wide, narrow = mesh.shape["wide"], mesh.shape["narrow"]
    where = (wide, narrow, 1 if wide <= 8 else narrow)
    cut3 = P(AXES, None, None)
    cut2 = P(AXES, None)
    cut1 = P(AXES)
    params = (cut2, cut1, cut2, cut2, cut1, cut2, cut1, cut1, cut1, cut2, cut1, cut2, cut1, cut1, cut1)
    in_specs = (cut3, cut3, cut1, cut3, cut3, cut3) + params + (P(), P(), P())
    out_specs = (cut3, cut3) + params + (P(), P(), P())
    return jax.shard_map(lambda *a: local(where, *a), mesh=mesh, in_specs=in_specs, out_specs=out_specs, check_vma=False)
```

```python
import jax
import jax.numpy as jnp
from jax import lax
from jax.experimental import pallas as pl
from jax.experimental.pallas import tpu as pltpu
from jax.sharding import PartitionSpec as P

bf = jnp.bfloat16
f32 = jnp.float32
NT = (((1,), (1,)), ((), ()))
NN = (((1,), (0,)), ((), ()))
TN = (((0,), (0,)), ((), ()))
AXES = ("wide", "narrow")
MESH = pl.DeviceIdType.MESH
BQ = 128
VM = 60 << 20
TABLE_SCALE = 3500.0
EPS = 1e-05
KIN = 4
SHORTEST = 709


class Place:
    def __init__(self, wide, narrow, span, depth, low):
        self.n = wide * narrow
        self.half = self.n // 2
        self.narrow = narrow
        self.span = span
        self.depth = depth
        self.low = low
        self.plane = self.half // depth
        self.flat = lax.axis_index("wide") * narrow + lax.axis_index("narrow")
        self.par = lax.rem(lax.div(self.flat, span), 2)
        self.group = lax.div(self.flat, 2 * span) * span + lax.rem(self.flat, span)
        self.q, self.z = self.split(self.group)

    def split(self, group):
        q = lax.div(group, self.depth * self.low) * self.low + lax.rem(group, self.low)
        return q, lax.rem(lax.div(group, self.low), self.depth)

    def join(self, q, z):
        return (lax.div(q, self.low) * self.depth + z) * self.low + lax.rem(q, self.low)

    def flat_of(self, group, par):
        return (lax.div(group, self.span) * 2 + par) * self.span + lax.rem(group, self.span)

    def device(self, flat):
        return (lax.div(flat, self.narrow), lax.rem(flat, self.narrow))

    def partner(self):
        return self.device(self.flat_of(self.group, 1 - self.par))

    def peer(self, k):
        return lax.rem(self.group + k, self.half)

    def peer_device(self, k):
        return self.device(self.flat_of(self.peer(k), self.par))

    def column(self, k):
        z = lax.rem(self.z + k, self.depth)
        return z, self.device(self.flat_of(self.join(self.q, z), self.par))

    def across(self, k):
        q = lax.rem(self.q + k, self.plane)
        return q, self.device(self.flat_of(self.join(q, self.z), self.par))

    def greet(self):
        barrier = pltpu.get_barrier_semaphore()
        pl.semaphore_signal(barrier, inc=1, device_id=self.partner(), device_id_type=MESH)

        def one(k, c):
            pl.semaphore_signal(barrier, inc=1, device_id=self.peer_device(k), device_id_type=MESH)
            return c

        lax.fori_loop(1, self.half, one, 0)
        pl.semaphore_wait(barrier, self.half)


def loop(first, last, body):
    def one(k, c):
        body(k)
        return c

    lax.fori_loop(first, last, one, 0)


class Scatter:
    shapes = staticmethod(
        lambda half, depth, block, kind: [
            pltpu.VMEM((half // depth, depth) + block, kind),
            pltpu.VMEM((half // depth, depth) + block, kind),
            pltpu.VMEM((half // depth, depth) + block, kind),
            pltpu.VMEM((depth,) + block, kind),
            pltpu.SemaphoreType.DMA((7,)),
        ]
    )

    def __init__(self, me, src, mine, came, plane, column, sem):
        self.me, self.src, self.mine, self.came, self.plane, self.column, self.sem = me, src, mine, came, plane, column, sem

    def begin(self):
        me, sem = self.me, self.sem

        def one(g):
            q, z = me.split(g)
            a, b = lax.div(g, me.span), lax.rem(g, me.span)
            send(self.src.at[a, 1 - me.par, b], self.came.at[q, z], sem.at[1], sem.at[2], me.partner())
            pltpu.make_async_copy(self.src.at[a, me.par, b], self.mine.at[q, z], sem.at[0]).start()

        loop(0, me.half, one)

    def to_plane(self):
        me, sem = self.me, self.sem
        drain(self.mine, sem.at[0])
        drain(self.came, sem.at[1])
        drain(self.came, sem.at[2])

        def add(g):
            q, z = me.split(g)
            self.mine[q, z] = (self.mine[q, z].astype(f32) + self.came[q, z].astype(f32)).astype(bf)

        loop(0, me.half, add)

        def one(k):
            q, device = me.across(k)
            send(self.mine.at[q], self.plane.at[me.q], sem.at[3], sem.at[4], device)

        loop(1, me.plane, one)

    def to_column(self):
        me, sem = self.me, self.sem
        others = pl.ds(0, me.plane - 1)
        drain(self.plane.at[others], sem.at[3])
        drain(self.plane.at[others], sem.at[4])

        def add(z):
            total = self.mine[me.q, z].astype(f32)
            for k in range(1, me.plane):
                total = total + self.plane[me.across(k)[0], z].astype(f32)
            self.mine[me.q, z] = total.astype(bf)

        loop(0, me.depth, add)

        def one(k):
            z, device = me.column(k)
            send(self.mine.at[me.q, z], self.column.at[me.z], sem.at[5], sem.at[6], device)

        loop(1, me.depth, one)

    def end(self, out):
        me, sem = self.me, self.sem
        others = pl.ds(0, me.depth - 1)
        drain(self.column.at[others], sem.at[5])
        drain(self.column.at[others], sem.at[6])
        total = self.mine[me.q, me.z].astype(f32)
        for k in range(1, me.depth):
            total = total + self.column[me.column(k)[0]].astype(f32)
        out[...] = total


def send(src, dst, send_sem, recv_sem, device):
    pltpu.make_async_remote_copy(src, dst, send_sem, recv_sem, device_id=device, device_id_type=MESH).start()


def drain(ref, sem):
    pltpu.make_async_copy(ref, ref, sem).wait()


def take(t, i):
    return jnp.take_along_axis(t, i, axis=1, mode="promise_in_bounds")


def front_kernel(where, pos_ref, x_ref, y_ref, pt_ref, xt_ref, yt_ref, wq_ref, wk_ref, wv_ref, wo_ref, *rest):
    vec_refs = rest[:9]
    out_ref, idx_ref, w_all, small_ref, up_ref, v_all, wpack, vpack, tab, lsem, ssem, rsem, xssem, xrsem = rest[9:]
    S = out_ref.shape[1]
    pid = pl.program_id(0)
    me = Place(*where)
    width = wq_ref.shape[1]

    @pl.when(pid == 0)
    def _():
        for n, ref in enumerate((wq_ref, wk_ref, wv_ref, wo_ref)):
            wpack[:, n * width : (n + 1) * width] = ref[...].astype(bf)
        vpack[...] = jnp.zeros_like(vpack)
        for n, ref in enumerate(vec_refs):
            vpack[n : n + 1, : ref.shape[1]] = ref[...].astype(bf)
        me.greet()
        pltpu.make_async_copy(wpack, w_all.at[me.flat], lsem.at[0]).start()
        pltpu.make_async_copy(vpack, v_all.at[me.flat], lsem.at[1]).start()
        send(vpack, v_all.at[me.flat], xssem.at[1], xrsem.at[1], me.partner())
        send(wpack, w_all.at[me.flat], xssem.at[0], xrsem.at[0], me.partner())

        def one(k):
            device = me.column(k)[1]
            send(vpack, v_all.at[me.flat], ssem.at[1], rsem.at[1], device)
            send(wpack, w_all.at[me.flat], ssem.at[0], rsem.at[0], device)

        loop(1, me.depth, one)
        tab[...] = jnp.zeros_like(tab)

        def pack(ref, row, lane):
            fixed = jnp.floor(ref[...].astype(bf).astype(f32) * TABLE_SCALE + 0.5).astype(jnp.int32)
            n = fixed.shape[1]
            for p in range(6):
                tab[row, p : p + 1, lane : lane + n] = fixed[2 * p : 2 * p + 1] * 65536 + fixed[2 * p + 1 : 2 * p + 2]

        pack(pt_ref, 0, 0)
        pack(xt_ref, 1, 0)
        pack(yt_ref, 1, 64)

    @pl.when(pid == 2)
    def _():
        others = pl.ds(0, me.depth - 1)
        drain(v_all.at[others], rsem.at[1])
        drain(w_all.at[others], rsem.at[0])
        pltpu.make_async_copy(wpack, w_all.at[me.flat], lsem.at[0]).wait()
        pltpu.make_async_copy(vpack, v_all.at[me.flat], lsem.at[1]).wait()

        def one(k):
            device = me.across(k)[1]

            def block(z):
                at = me.flat_of(me.join(me.q, z), me.par)
                send(v_all.at[at], v_all.at[at], ssem.at[3], rsem.at[3], device)
                send(w_all.at[at], w_all.at[at], ssem.at[2], rsem.at[2], device)

            loop(0, me.depth, block)

        loop(1, me.plane, one)

    @pl.when(pid == pl.num_programs(0) - 1)
    def _():
        others = pl.ds(0, (me.plane - 1) * me.depth)
        drain(v_all.at[others], rsem.at[3])
        drain(w_all.at[others], rsem.at[2])

        def one(k):
            at = me.flat_of(me.peer(k), me.par)
            send(v_all.at[at], v_all.at[at], xssem.at[1], xrsem.at[1], me.partner())
            send(w_all.at[at], w_all.at[at], xssem.at[0], xrsem.at[0], me.partner())

        loop(1, me.half, one)

    packed = pos_ref[...] | (x_ref[...] << 5) | (y_ref[...] << 11)
    idx_ref[...] = packed.T
    tp = [jnp.broadcast_to(tab[0, p : p + 1, :], (8, 128)) for p in range(6)]
    tx = [jnp.broadcast_to(tab[1, p : p + 1, :], (8, 128)) for p in range(6)]

    def body(r, c):
        for u in range(48):
            sl = pl.ds(pl.multiple_of((r * 48 + u) * 8, 8), 8)
            t = idx_ref[sl, :]
            p = t & 31
            x = (t >> 5) & 63
            y = (t >> 11) + 64
            g = [take(a, p) for a in tp]
            g = [a + take(b, x) for a, b in zip(g, tx)]
            g = [a + take(b, y) for a, b in zip(g, tx)]
            for k in range(6):
                out_ref[k, sl, :] = g[k]
        return c

    lax.fori_loop(0, S // (48 * 8), body, 0)

    @pl.when(pid == pl.num_programs(0) - 1)
    def _():
        mine = pl.ds(0, me.half)
        near, far = pl.ds(0, me.depth - 1), pl.ds(0, (me.plane - 1) * me.depth)
        drain(w_all.at[near], ssem.at[0])
        drain(v_all.at[near], ssem.at[1])
        drain(w_all.at[far], ssem.at[2])
        drain(v_all.at[far], ssem.at[3])
        for sem in (xssem, xrsem):
            drain(w_all.at[mine], sem.at[0])
            drain(v_all.at[mine], sem.at[1])
        share = wpack.shape[0]
        for d in range(me.n):
            block = v_all[d].astype(f32)
            at = pl.ds(d * share, share)
            small_ref[:, at] = block[0:8, :share]
            for m in range(4):
                up_ref[m : m + 1, at] = block[8:9, m * share : (m + 1) * share]


def front_call(where, pos, x, y, tables, weights, vectors):
    S = pos.shape[0]
    share, width = weights[0].shape
    n = where[0] * where[1]

    def whole(a):
        return pl.BlockSpec(a.shape, lambda i: (0,) * a.ndim)

    small = tuple(tables) + tuple(weights) + tuple(v.reshape(1, -1) for v in vectors)
    return pl.pallas_call(
        lambda *a: front_kernel(where, *a),
        grid=(S // BQ,),
        in_specs=[pl.BlockSpec((BQ, S), lambda i: (i, 0))] * 3 + [whole(a) for a in small],
        out_specs=[
            pl.BlockSpec((6, S, BQ), lambda i: (0, 0, i)),
            pl.BlockSpec((S, BQ), lambda i: (0, i)),
            pl.BlockSpec(memory_space=pl.ANY),
            pl.BlockSpec((8, width), lambda i: (0, 0)),
            pl.BlockSpec((4, width), lambda i: (0, 0)),
        ],
        out_shape=[
            jax.ShapeDtypeStruct((6, S, S), jnp.int32),
            jax.ShapeDtypeStruct((S, S), jnp.int32),
            jax.ShapeDtypeStruct((n, share, 4 * width), bf),
            jax.ShapeDtypeStruct((8, width), f32),
            jax.ShapeDtypeStruct((4, width), f32),
        ],
        scratch_shapes=[
            pltpu.VMEM((n, 16, 128), bf),
            pltpu.VMEM((share, 4 * width), bf),
            pltpu.VMEM((16, 128), bf),
            pltpu.VMEM((2, 8, 128), jnp.int32),
        ]
        + [pltpu.SemaphoreType.DMA((4,))] * 5,
        compiler_params=pltpu.CompilerParams(vmem_limit_bytes=VM, collective_id=0, has_side_effects=True),
        name="bias_and_gather",
    )(pos, x, y, *small)


def pack_call(w1, w2, n):
    share, wide = w1.shape
    width = wide // 4
    pieces = share % 8 == 0
    if not pieces:
        w1 = jnp.transpose(w1.reshape(share, n, 4, share), (0, 2, 1, 3)).reshape(share, 4 * width)

    def kernel(w1_ref, w2_ref, a_ref, scr):
        if pieces:
            for d in range(n):
                for m in range(4):
                    at = m * width + d * share
                    scr[:, at : at + share] = w1_ref[:, (4 * d + m) * share : (4 * d + m + 1) * share]
            a_ref[:, : 4 * width] = scr[...].astype(bf)
        else:
            a_ref[:, : 4 * width] = w1_ref[...].astype(bf)
        for m in range(4):
            a_ref[:, (4 + m) * width : (5 + m) * width] = w2_ref[m * share : (m + 1) * share, :].astype(bf)

    return pl.pallas_call(
        kernel,
        out_shape=jax.ShapeDtypeStruct((share, 8 * width), bf),
        scratch_shapes=[pltpu.VMEM((share, 4 * width), f32)],
        name="round_shares",
    )(w1, w2)


def finish_call(early, late, first, vec, tables, n, narrow):
    share, width = first.shape[0], vec.shape[1]
    pieces = share % 8 == 0
    kin = early.shape[1] // width

    def kernel(e_ref, s_ref, f_ref, v_ref, t_ref, wo_ref, w1_ref, w2_ref, wq_ref, wk_ref, wv_ref, gp_ref, gx_ref, gy_ref, *rest):
        vec_refs, scr = rest[:9], rest[9]
        flat = lax.axis_index("wide") * narrow + lax.axis_index("narrow")

        def part(k):
            if k < kin:
                return e_ref[:, k * width : (k + 1) * width]
            return s_ref[:, (k - kin) * width : (k - kin + 1) * width].astype(f32)

        for k, ref in enumerate((wq_ref, wk_ref, wv_ref)):
            ref[...] = f_ref[:, k * width : (k + 1) * width]
        gx_ref[...] = t_ref[0:12, 0:64]
        gy_ref[...] = t_ref[0:12, 64:128]
        gp_ref[...] = t_ref[0:12, 128:160]
        wo_ref[...] = part(0)
        for m in range(4):
            scr[:, m * width : (m + 1) * width] = part(1 + m)
            w2_ref[m * share : (m + 1) * share, :] = part(5 + m)
        if pieces:
            for d in range(n):
                for m in range(4):
                    at = m * width + d * share
                    w1_ref[:, (4 * d + m) * share : (4 * d + m + 1) * share] = scr[:, at : at + share]
        else:
            w1_ref[...] = scr[...]
        own = jnp.zeros((16, share), f32)
        for d in range(n):
            own = jnp.where(flat == d, v_ref[:, d * share : (d + 1) * share], own)
        for k in range(8):
            vec_refs[k][...] = own[k : k + 1, :]
        for m in range(4):
            vec_refs[8][:, m * share : (m + 1) * share] = own[8 + m : 9 + m, :]

    outs = [(share, width), (share, 4 * width), (4 * share, width)] + [(share, width)] * 3 + [(12, 32), (12, 64), (12, 64)]
    outs += [(1, share)] * 8 + [(1, 4 * share)]
    outs = pl.pallas_call(
        kernel,
        out_shape=[jax.ShapeDtypeStruct(s, f32) for s in outs],
        scratch_shapes=[pltpu.VMEM((share, 4 * width), f32)],
        name="own_shares",
    )(early, late, first, vec, tables)
    g_up = outs[1]
    if not pieces:
        g_up = jnp.transpose(g_up.reshape(share, 4, n, share), (0, 2, 1, 3)).reshape(share, 4 * width)
    return [outs[0], g_up, outs[2], *outs[3:6], *[t.T for t in outs[6:9]], [v.reshape(-1) for v in outs[9:]]]


def stack2(a):
    lane=lax.broadcasted_iota(jnp.int32,a.shape,1)
    z=jnp.zeros_like(a)
    return jnp.concatenate([jnp.where(lane<64,a,z),jnp.where(lane<64,z,a)],axis=0)

def fwd_kernel(live_ref, q_ref, k_ref, vt_ref, b_ref, e_ref, o_ref, l_ref, s_scr, *, CH):
    S = k_ref.shape[0]
    live = live_ref[0]
    c = 1.0 / (TABLE_SCALE * 65536.0)
    chunks = range(S // CH)
    rows = lax.broadcasted_iota(jnp.int32, (CH, 1), 0)
    sub = lax.broadcasted_iota(jnp.int32, (128, 128), 0)

    def scores(p, qs, top, ch):
        r = pl.ds(ch * CH, CH)
        s = lax.dot_general(k_ref[r, pl.ds(p * 128, 128)], qs, NT, preferred_element_type=f32)
        b = b_ref[p, r, :]
        s = s + jnp.concatenate([b.astype(f32) * c, (b << 16).astype(f32) * c], axis=1)
        if (ch + 1) * CH > SHORTEST:
            s = jnp.where(rows + ch * CH < live, s, -1e9)
        s_scr[p % 2, r, :] = s
        return jnp.maximum(top, jnp.max(s.reshape(CH // 8, 8, 256), axis=0))

    low = jnp.full((8, 256), -3e38, f32)
    top = low
    qs = stack2(q_ref[:, pl.ds(0, 128)])
    for ch in chunks:
        top = scores(0, qs, top, ch)
    for p in range(6):
        ln = pl.ds(p * 128, 128)
        peak = jnp.max(top, axis=0, keepdims=True)
        top = low
        total = jnp.zeros((8, 256), f32)
        if p < 5:
            qs = stack2(q_ref[:, pl.ds((p + 1) * 128, 128)])
        for ch in chunks:
            if p < 5:
                top = scores(p + 1, qs, top, ch)
            r = pl.ds(ch * CH, CH)
            e = jnp.exp(s_scr[p % 2, r, :] - peak)
            total = total + jnp.sum(e.reshape(CH // 8, 8, 256), axis=0)
            eb = e.astype(bf)
            e_ref[2 * p, r, :] = eb[:, :128]
            e_ref[2 * p + 1, r, :] = eb[:, 128:]
        linv = 1.0 / jnp.sum(total, axis=0, keepdims=True)
        l_ref[2 * p : 2 * p + 1, :] = linv[:, :128]
        l_ref[2 * p + 1 : 2 * p + 2, :] = linv[:, 128:]
        both = jnp.concatenate([e_ref[2 * p], e_ref[2 * p + 1]], axis=1)
        acc = lax.dot_general(vt_ref[ln, :], both, NN, preferred_element_type=f32) * linv
        o_ref[:, ln] = jnp.where(sub < 64, acc[:, :128], acc[:, 128:]).T.astype(bf)


def fwd_call(live, q, k, vt, b, CH=128):
    S, D = k.shape
    return pl.pallas_call(
        lambda *a: fwd_kernel(*a, CH=CH),
        grid_spec=pltpu.PrefetchScalarGridSpec(
            num_scalar_prefetch=1,
            grid=(S // BQ,),
            in_specs=[
                pl.BlockSpec((BQ, D), lambda i, *_: (i, 0)),
                pl.BlockSpec((S, D), lambda i, *_: (0, 0)),
                pl.BlockSpec((D, S), lambda i, *_: (0, 0)),
                pl.BlockSpec((6, S, BQ), lambda i, *_: (0, 0, i)),
            ],
            out_specs=[
                pl.BlockSpec((12, S, BQ), lambda i, *_: (0, 0, i)),
                pl.BlockSpec((BQ, D), lambda i, *_: (i, 0)),
                pl.BlockSpec((16, BQ), lambda i, *_: (0, i)),
            ],
            scratch_shapes=[pltpu.VMEM((2, S, 256), f32)],
        ),
        out_shape=[
            jax.ShapeDtypeStruct((12, S, S), bf),
            jax.ShapeDtypeStruct((S, D), bf),
            jax.ShapeDtypeStruct((16, S), f32),
        ],
        compiler_params=pltpu.CompilerParams(vmem_limit_bytes=VM),
        name="attention_forward",
    )(live, q, k, vt, b)


def bwd_kernel(where, q_ref, do_ref, kt_ref, v_ref, e_ref, l_ref, d_ref, g_ref, dq_ref, dk_ref, dv_ref, ds_ref, out_ref, ds_scr, dk_acc, dv_acc, *rest):
    S = v_ref.shape[0]
    pid = pl.program_id(0)
    me = Place(*where)
    travel = Scatter(me, g_ref, *rest)

    @pl.when(pid == 0)
    def _():
        me.greet()
        travel.begin()

    @pl.when(pid == 1)
    def _():
        travel.to_plane()

    @pl.when(pid == 6)
    def _():
        travel.to_column()

    @pl.when(pid == 0)
    def _():
        dk_acc[...] = jnp.zeros_like(dk_acc)
        dv_acc[...] = jnp.zeros_like(dv_acc)

    lane = lax.broadcasted_iota(jnp.int32, (BQ, 128), 1)
    sub = lax.broadcasted_iota(jnp.int32, (128, 128), 0)
    for p in range(6):
        ln = pl.ds(p * 128, 128)
        qs = stack2(q_ref[:, ln])
        l2 = l_ref[2 * p : 2 * p + 2, :]
        d2 = d_ref[2 * p : 2 * p + 2, :] * l2
        lcol = jnp.concatenate([l2] * 4, axis=0).T
        dos = stack2((do_ref[:, ln].astype(f32) * jnp.where(lane < 64, lcol[:, 0:1], lcol[:, 1:2])).astype(bf))
        dp = lax.dot_general(v_ref[:, ln], dos, NT, preferred_element_type=f32)
        e0 = e_ref[2 * p]
        e1 = e_ref[2 * p + 1]
        s0 = e0.astype(f32) * (dp[:, :128] - d2[0:1, :])
        s1 = e1.astype(f32) * (dp[:, 128:] - d2[1:2, :])
        ds_scr[pl.ds(2 * p, S, stride=16), :] = s0
        ds_scr[pl.ds(2 * p + 1, S, stride=16), :] = s1
        both = jnp.concatenate([s0.astype(bf), s1.astype(bf)], axis=1)
        dk_acc[:, ln] += lax.dot_general(both, qs, NN, preferred_element_type=f32)
        dv_acc[:, ln] += lax.dot_general(jnp.concatenate([e0, e1], axis=1), dos, NN, preferred_element_type=f32)
        a = lax.dot_general(kt_ref[ln, :], both, NN, preferred_element_type=f32)
        dq_ref[:, ln] = (jnp.where(sub < 64, a[:, :128], a[:, 128:]).T * 0.125).astype(bf)
    ds_ref[...] = ds_scr[...].astype(bf)

    @pl.when(pid == pl.num_programs(0) - 1)
    def _():
        dk_ref[...] = dk_acc[...].astype(bf)
        dv_ref[...] = dv_acc[...].astype(bf)
        travel.end(out_ref)


def bwd_call(where, q, do, kt, v, e, linv, dd, g):
    S, D = v.shape
    half = where[0] * where[1] // 2
    block = g.shape[3:]
    fixed = pl.Buffered(1)
    full = pl.BlockSpec((S, D), lambda i: (0, 0))
    blk = pl.BlockSpec((BQ, D), lambda i: (i, 0))
    row = pl.BlockSpec((16, BQ), lambda i: (0, i))
    return pl.pallas_call(
        lambda *a: bwd_kernel(where, *a),
        grid=(S // BQ,),
        in_specs=[
            blk,
            blk,
            pl.BlockSpec((D, S), lambda i: (0, 0), pipeline_mode=fixed),
            pl.BlockSpec((S, D), lambda i: (0, 0), pipeline_mode=fixed),
            pl.BlockSpec((12, S, BQ), lambda i: (0, 0, i)),
            row,
            row,
            pl.BlockSpec(memory_space=pl.ANY),
        ],
        out_specs=[blk, full, full, pl.BlockSpec((S * 16, BQ), lambda i: (0, i)), pl.BlockSpec(block, lambda i: (0, 0))],
        scratch_shapes=[pltpu.VMEM((S * 16, BQ), f32), pltpu.VMEM((S, D), f32), pltpu.VMEM((S, D), f32)]
        + Scatter.shapes(half, where[3], block, bf),
        out_shape=[jax.ShapeDtypeStruct((S, D), bf)] * 3 + [jax.ShapeDtypeStruct((S * 16, S), bf), jax.ShapeDtypeStruct(block, f32)],
        compiler_params=pltpu.CompilerParams(vmem_limit_bytes=VM, collective_id=2, has_side_effects=True),
        name="attention_backward_and_scatter",
    )(q, do, kt, v, e, linv, dd, g)


def tail_kernel(where, U, ds_ref, idx_ref, gw_ref, gv_ref, t_ref, w_out, v_out, *rest):
    acc, xi_scr, v_in, v_mine, v_near, v_far, h_mine, h_in, h_recv, xssem, xrsem, ssem, rsem = rest[:13]
    S = idx_ref.shape[0]
    pid = pl.program_id(0)
    me = Place(*where)
    travel = Scatter(me, gw_ref, *rest[13:])
    others = pl.ds(0, me.half - 1)
    near, far = pl.ds(0, me.plane - 1), pl.ds(0, me.depth - 1)

    @pl.when(pid == 0)
    def _():
        acc[...] = jnp.zeros_like(acc)
        me.greet()
        send(gv_ref, v_in, xssem.at[1], xrsem.at[1], me.partner())
        travel.begin()

    @pl.when(pid == 1)
    def _():
        drain(v_in, xssem.at[1])
        drain(v_in, xrsem.at[1])
        v_mine[0] = gv_ref[...] + v_in[...]

        def one(k):
            send(v_mine.at[0], v_near.at[me.q], ssem.at[0], rsem.at[0], me.across(k)[1])

        loop(1, me.plane, one)
        travel.to_plane()

    @pl.when(pid == 5)
    def _():
        drain(v_near.at[near], ssem.at[0])
        drain(v_near.at[near], rsem.at[0])
        v_mine[1] = lax.fori_loop(1, me.plane, lambda k, t: t + v_near[me.across(k)[0]], v_mine[0])

        def one(k):
            send(v_mine.at[1], v_far.at[me.z], ssem.at[1], rsem.at[1], me.column(k)[1])

        loop(1, me.depth, one)
        travel.to_column()

    t = idx_ref[...]
    xi_scr[0] = (t & 31).astype(f32)
    xi_scr[1] = ((t >> 5) & 63).astype(f32)
    xi_scr[2] = (t >> 11).astype(f32)
    iot = lax.broadcasted_iota(jnp.int32, (16, 128), 0).astype(f32).astype(bf)
    one = jnp.ones((16, 128), bf)
    zero = jnp.zeros((16, 128), bf)

    def one_j(j):
        bp, bx, by = [jnp.broadcast_to(xi_scr[n, pl.ds(j, 1), :], (16, 128)).astype(bf) for n in range(3)]
        d = ds_ref[pl.ds(pl.multiple_of(j * 16, 16), 16), :]
        xh = bx >= 32
        yh = by >= 32
        bxl = jnp.where(xh, bx - 32, bx)
        byl = jnp.where(yh, by - 32, by)
        ph = bp >= 16
        bpl = jnp.where(ph, bp - 16, bp)
        rows = [jnp.where(b == iot + bf(16 * k), one, zero) for b in (bxl, byl) for k in range(2)]
        rows.append(jnp.where(bpl == iot, one, zero))
        rhs = [d, jnp.where(xh, d, zero), jnp.where(yh, d, zero), jnp.where(ph, d, zero)]
        return jnp.concatenate(rows, 0), jnp.concatenate(rhs, 0)

    def body(t, total):
        for u in range(U):
            l0, r0 = one_j(t * 2 * U + 2 * u)
            l1, r1 = one_j(t * 2 * U + 2 * u + 1)
            total = total + lax.dot_general(
                jnp.concatenate([l0, l1], 1), jnp.concatenate([r0, r1], 1), NT, preferred_element_type=f32
            )
        return total

    acc[:, :64] += lax.fori_loop(0, S // (2 * U), body, jnp.zeros((80, 64), f32))

    @pl.when(pid == pl.num_programs(0) - 1)
    def _():
        h = acc[...].T
        total, x1, y1, p1 = h[0:16], h[16:32, 0:32], h[32:48, 32:64], h[48:64, 64:80]
        parts = [total[:, 0:32] - x1, x1, total[:, 32:64] - y1, y1, total[:, 64:80] - p1, p1, jnp.zeros((16, 96), f32)]
        h = jnp.concatenate(parts, axis=1)
        h_mine[...] = jnp.where(lax.broadcasted_iota(jnp.int32, h.shape, 0) < 12, h, 0.0)
        send(h_mine, h_in, xssem.at[2], xrsem.at[2], me.partner())
        drain(v_far.at[far], ssem.at[1])
        drain(v_far.at[far], rsem.at[1])
        v_out[...] = lax.fori_loop(1, me.depth, lambda k, t: t + v_far[me.column(k)[0]], v_mine[1])
        travel.end(w_out)
        drain(h_in, xssem.at[2])
        drain(h_in, xrsem.at[2])
        h_mine[...] = h_mine[...] + h_in[...]

        def one(k, c):
            send(h_mine, h_recv.at[me.group], ssem.at[2], rsem.at[2], me.peer_device(k))
            return c

        lax.fori_loop(1, me.half, one, 0)
        drain(h_recv.at[others], ssem.at[2])
        drain(h_recv.at[others], rsem.at[2])
        t_ref[...] = lax.fori_loop(1, me.half, lambda k, s: s + h_recv[me.peer(k)], h_mine[...])


def tail_call(where, ds, codes, gw, gv, U=96):
    S = codes.shape[0]
    half, depth = where[0] * where[1] // 2, where[3]
    share, cols = gw.shape[3:]

    def whole(shape):
        return pl.BlockSpec(shape, lambda i: (0,) * len(shape))

    outs = [(16, 256), (share, cols), gv.shape]
    return pl.pallas_call(
        lambda *a: tail_kernel(where, U, *a),
        grid=(S // BQ,),
        in_specs=[
            pl.BlockSpec((S * 16, BQ), lambda i: (0, i)),
            pl.BlockSpec((S, BQ), lambda i: (0, i)),
            pl.BlockSpec(memory_space=pl.ANY),
            whole(gv.shape),
        ],
        out_specs=[whole(s) for s in outs],
        out_shape=[jax.ShapeDtypeStruct(s, f32) for s in outs],
        scratch_shapes=[
            pltpu.VMEM((80, 128), f32),
            pltpu.VMEM((3, S, BQ), f32),
            pltpu.VMEM(gv.shape, f32),
            pltpu.VMEM((2,) + gv.shape, f32),
            pltpu.VMEM((half // depth,) + gv.shape, f32),
            pltpu.VMEM((depth,) + gv.shape, f32),
            pltpu.VMEM((16, 256), f32),
            pltpu.VMEM((16, 256), f32),
            pltpu.VMEM((half, 16, 256), f32),
        ]
        + [pltpu.SemaphoreType.DMA((3,))] * 4
        + Scatter.shapes(half, depth, (share, cols), bf),
        compiler_params=pltpu.CompilerParams(vmem_limit_bytes=VM, collective_id=1, has_side_effects=True),
        name="table_sums_and_scatter",
    )(ds, codes, gw, gv)


GELU_COEFS = (0.254829592, -0.284496736, 1.421413741, -1.453152027, 1.061405429)


def gelu_both(z):
    t = pltpu.reciprocal(1.0 + (0.3275911 * 0.7071067811865476) * jnp.abs(z), approx=False)
    q = jnp.exp(z * z * -0.5)
    poly = 0.5 * GELU_COEFS[4] * t + 0.5 * GELU_COEFS[3]
    for c in GELU_COEFS[2::-1]:
        poly = poly * t + 0.5 * c
    half = poly * t * q
    cdf = jnp.where(z >= 0, 1.0 - half, half)
    return z * cdf, cdf + z * (q * 0.3989422804014327)


def norm_stats(u):
    mean = jnp.mean(u, axis=-1, keepdims=True)
    center = u - mean
    inv = lax.rsqrt(jnp.mean(center * center, axis=-1, keepdims=True) + EPS)
    return center * inv, inv


def norm_pull(e, normed, inv):
    return (e - jnp.mean(e, axis=-1, keepdims=True) - normed * jnp.mean(e * normed, axis=-1, keepdims=True)) * inv


def fold8(u):
    return jnp.sum(u.reshape(u.shape[0] // 8, 8, u.shape[1]), axis=0)


def row_kernel(live_ref, at_ref, x_ref, ct_ref, wo_ref, w_ref, v_ref, b1_ref,
               out_ref, h_ref, g_ref, df_ref, dz_ref, da_ref, dr_ref, dat_ref, dd_ref, sum_ref, sb1_ref,
               gp_scr, z_scr, acc, h_scr, n1_scr, i1_scr, *, R, SL):
    pid = pl.program_id(0)
    D = x_ref.shape[1]
    live = live_ref[0]
    b_out, g1, s1, b_down, g2, s2 = [v_ref[n : n + 1, :] for n in range(2, 8)]

    @pl.when(pid == 0)
    def _():
        sum_ref[...] = jnp.zeros_like(sum_ref)
        sb1_ref[...] = jnp.zeros_like(sb1_ref)

    def add(row, part):
        sum_ref[row : row + 1, :] += jnp.sum(part, axis=0, keepdims=True)

    acc[...] = lax.dot_general(at_ref[...], wo_ref[...], NN, preferred_element_type=f32)
    for r in range(0, R, SL):
        sl = pl.ds(r, SL)
        n1, inv = norm_stats(x_ref[sl, :].astype(f32) + acc[sl, :] + b_out)
        n1_scr[sl, :] = n1
        i1_scr[sl, :] = jnp.broadcast_to(inv, (SL, 128))
        h1 = n1 * g1 + s1
        h_scr[sl, :] = h1
        h_ref[sl, :] = h1.astype(bf)
    for c in range(4):
        cols = pl.ds(c * D, D)
        z_scr[c % 2] = lax.dot_general(h_ref[...], w_ref[:, pl.ds(c * D, D)], NN, preferred_element_type=f32)
        for r in range(0, R, SL):
            sl = pl.ds(r, SL)
            g, gp = gelu_both(z_scr[c % 2, sl, :] + b1_ref[c : c + 1, :])
            g_ref[sl, cols] = g.astype(bf)
            gp_scr[sl, cols] = gp
        part = lax.dot_general(g_ref[:, cols], w_ref[:, pl.ds((4 + c) * D, D)], NN, preferred_element_type=f32)
        if c == 0:
            acc[...] = part
        else:
            acc[...] += part
    p_gain = p_shift = p_down = jnp.zeros((8, D), f32)
    rows = lax.broadcasted_iota(jnp.int32, (SL, 1), 0) + pid * R
    for r in range(0, R, SL):
        sl = pl.ds(r, SL)
        n2, inv = norm_stats(h_scr[sl, :] + acc[sl, :] + b_down)
        out_ref[sl, :] = (n2 * g2 + s2).astype(bf)
        dy = jnp.where(rows + r < live, ct_ref[sl, :].astype(f32), 0.0)
        dr2 = norm_pull(dy * g2, n2, inv)
        df = dr2.astype(bf)
        df_ref[sl, :] = df
        h_scr[sl, :] = dr2
        p_gain = p_gain + fold8(dy * n2)
        p_shift = p_shift + fold8(dy)
        p_down = p_down + fold8(df.astype(f32))
    add(5, p_down)
    add(6, p_gain)
    add(7, p_shift)
    for c in range(4):
        cols = pl.ds(c * D, D)
        z_scr[c % 2] = lax.dot_general(df_ref[...], w_ref[:, pl.ds((4 + c) * D, D)], NT, preferred_element_type=f32)
        p_up = jnp.zeros((8, D), f32)
        for r in range(0, R, SL):
            sl = pl.ds(r, SL)
            dz = (z_scr[c % 2, sl, :] * gp_scr[sl, cols]).astype(bf)
            dz_ref[sl, cols] = dz
            p_up = p_up + fold8(dz.astype(f32))
        sb1_ref[c : c + 1, :] += jnp.sum(p_up, axis=0, keepdims=True)
        part = lax.dot_general(dz_ref[:, cols], w_ref[:, pl.ds(c * D, D)], NT, preferred_element_type=f32)
        if c == 0:
            acc[...] = part
        else:
            acc[...] += part
    p_gain = p_shift = p_out = jnp.zeros((8, D), f32)
    for r in range(0, R, SL):
        sl = pl.ds(r, SL)
        dh = h_scr[sl, :] + acc[sl, :]
        n1 = n1_scr[sl, :]
        dr1 = norm_pull(dh * g1, n1, i1_scr[sl, 0:1])
        da = dr1.astype(bf)
        dr_ref[sl, :] = dr1
        da_ref[sl, :] = da
        p_gain = p_gain + fold8(dh * n1)
        p_shift = p_shift + fold8(dh)
        p_out = p_out + fold8(da.astype(f32))
    add(2, p_out)
    add(3, p_gain)
    add(4, p_shift)
    dat_ref[...] = lax.dot_general(da_ref[...], wo_ref[...], NT, preferred_element_type=f32).astype(bf)
    seg = (lax.div(lax.broadcasted_iota(jnp.int32, (D, 128), 0), 64) == lax.broadcasted_iota(jnp.int32, (D, 128), 1)).astype(f32).astype(bf)
    for r in range(0, R, 128):
        sl = pl.ds(r, 128)
        prod = dat_ref[sl, :].astype(f32) * at_ref[sl, :].astype(f32)
        high = prod.astype(bf)
        low = (prod - high.astype(f32)).astype(bf)
        d = lax.dot_general(high, seg, NN, preferred_element_type=f32) + lax.dot_general(low, seg, NN, preferred_element_type=f32)
        dd_ref[:, sl] = d.T[0:16, :]


def row_call(live, attended, x, ct, wo, w, v, b1, R=384, SL=16):
    S, D = x.shape
    blk = pl.BlockSpec((R, D), lambda i, *_: (i, 0))
    big = pl.BlockSpec((R, 4 * D), lambda i, *_: (i, 0))

    def whole(shape, **kw):
        return pl.BlockSpec(shape, lambda i, *_: (0,) * len(shape), **kw)

    shapes = [((S, D), bf), ((S, D), bf), ((S, 4 * D), bf), ((S, D), bf), ((S, 4 * D), bf), ((S, D), bf), ((S, D), f32), ((S, D), bf),
              ((16, S), f32), ((8, D), f32), ((4, D), f32)]
    return pl.pallas_call(
        lambda *a: row_kernel(*a, R=R, SL=SL),
        grid_spec=pltpu.PrefetchScalarGridSpec(
            num_scalar_prefetch=1,
            grid=(S // R,),
            in_specs=[blk, blk, blk, pl.BlockSpec((D, D), lambda i, *_: (0, 3), pipeline_mode=pl.Buffered(1)), whole(w.shape, pipeline_mode=pl.Buffered(1)), whole(v.shape), whole(b1.shape)],
            out_specs=[blk, blk, big, blk, big, blk, blk, blk, pl.BlockSpec((16, R), lambda i, *_: (0, i)), whole((8, D)), whole((4, D))],
            scratch_shapes=[
                pltpu.VMEM((R, 4 * D), f32),
                pltpu.VMEM((2, R, D), f32),
                pltpu.VMEM((R, D), f32),
                pltpu.VMEM((R, D), f32),
                pltpu.VMEM((R, D), f32),
                pltpu.VMEM((R, 128), f32),
            ],
        ),
        out_shape=[jax.ShapeDtypeStruct(s, d) for s, d in shapes],
        compiler_params=pltpu.CompilerParams(vmem_limit_bytes=VM),
        name="rows_forward_backward",
    )(live, attended, x, ct, wo, w, v, b1)


def share_kernel(kin, at_ref, h_ref, g_ref, da_ref, dz_ref, df_ref, early_ref, late_ref):
    c = pl.program_id(0)
    for first, last, a_ref, b_ref in ((0, 1, at_ref, da_ref), (1, 5, h_ref, dz_ref), (5, 9, g_ref, df_ref)):
        for low, high, out in ((first, min(last, kin), early_ref), (max(first, kin), last, late_ref)):
            if low < high:

                @pl.when((c >= low) & (c < high))
                def _(a_ref=a_ref, b_ref=b_ref, out=out):
                    out[...] = lax.dot_general(a_ref[...], b_ref[...], TN, preferred_element_type=f32).astype(bf)


def share_call(attended, h, g, da, dz, df, kin):
    S, D = h.shape

    def fixed():
        return pl.BlockSpec((S, D), lambda c: (0, 0), pipeline_mode=pl.Buffered(1))

    return pl.pallas_call(
        lambda *a: share_kernel(kin, *a),
        grid=(9,),
        in_specs=[
            fixed(),
            fixed(),
            pl.BlockSpec((S, D), lambda c: (0, jnp.clip(c - 5, 0, 3))),
            fixed(),
            pl.BlockSpec((S, D), lambda c: (0, jnp.clip(c - 1, 0, 3))),
            fixed(),
        ],
        out_specs=[
            pl.BlockSpec((D, D), lambda c: (0, jnp.minimum(c, kin - 1))),
            pl.BlockSpec((D, D), lambda c: (0, jnp.maximum(c - kin, 0))),
        ],
        out_shape=[jax.ShapeDtypeStruct((D, kin * D), bf), jax.ShapeDtypeStruct((D, (9 - kin) * D), bf)],
        compiler_params=pltpu.CompilerParams(vmem_limit_bytes=VM),
        name="weight_gradients",
    )(attended, h, g, da, dz, df)


def qkv_call(x, w, v, R=384):
    S, D = x.shape

    def kernel(x_ref, w_ref, v_ref, q_ref, k_ref, o_ref, kt_ref, ot_ref):
        x = x_ref[...]
        q_ref[...] = (lax.dot_general(x, w_ref[:, :D], NN, preferred_element_type=f32) + v_ref[0:1, :]).astype(bf) * bf(0.125)
        k_ref[...] = lax.dot_general(x, w_ref[:, D : 2 * D], NN, preferred_element_type=f32).astype(bf)
        o_ref[...] = (lax.dot_general(x, w_ref[:, 2 * D :], NN, preferred_element_type=f32) + v_ref[1:2, :]).astype(bf)
        kt_ref[...] = k_ref[...].T
        ot_ref[...] = o_ref[...].T

    blk = pl.BlockSpec((R, D), lambda i: (i, 0))
    turned = pl.BlockSpec((D, R), lambda i: (0, i))
    return pl.pallas_call(
        kernel,
        grid=(S // R,),
        in_specs=[blk, pl.BlockSpec((D, 3 * D), lambda i: (0, 0), pipeline_mode=pl.Buffered(1)), pl.BlockSpec(v.shape, lambda i: (0, 0))],
        out_specs=[blk] * 3 + [turned] * 2,
        out_shape=[jax.ShapeDtypeStruct((S, D), bf)] * 3 + [jax.ShapeDtypeStruct((D, S), bf)] * 2,
        compiler_params=pltpu.CompilerParams(vmem_limit_bytes=VM),
        name="project_qkv",
    )(x, w, v)


def input_kernel(x_ref, dq_ref, dk_ref, dv_ref, dr_ref, w_ref, s_ref, b1_ref, gw_ref, rg_ref, v_ref):
    D = x_ref.shape[1]
    for n, ref in enumerate((dq_ref, dk_ref, dv_ref)):
        gw_ref[:, n * D : (n + 1) * D] = lax.dot_general(x_ref[...], ref[...], TN, preferred_element_type=f32).astype(bf)
    S = x_ref.shape[0]
    v_ref[...] = jnp.concatenate([s_ref[...], b1_ref[...], jnp.zeros((4, D), f32)], axis=0)
    for row, ref in ((0, dq_ref), (1, dv_ref)):
        part = jnp.zeros((8, D), f32)
        for r in range(0, S, 64):
            part = part + fold8(ref[pl.ds(r, 64), :].astype(f32))
        v_ref[row : row + 1, :] = jnp.sum(part, axis=0, keepdims=True)
    for r in range(0, S, 384):
        sl = pl.ds(r, 384)
        total = dr_ref[sl, :]
        for n, ref in enumerate((dq_ref, dk_ref, dv_ref)):
            total = total + lax.dot_general(ref[sl, :], w_ref[:, n * D : (n + 1) * D], NT, preferred_element_type=f32)
        rg_ref[sl, :] = total.astype(bf)


def input_call(x, dq, dk, dv, dr, w, sums, sb1):
    S, D = x.shape
    return pl.pallas_call(
        input_kernel,
        grid=(1,),
        in_specs=[pl.BlockSpec(a.shape, lambda i: (0, 0)) for a in (x, dq, dk, dv, dr)]
        + [pl.BlockSpec((D, 3 * D), lambda i: (0, 0))]
        + [pl.BlockSpec(a.shape, lambda i: (0, 0)) for a in (sums, sb1)],
        out_specs=[pl.BlockSpec(s, lambda i: (0, 0)) for s in ((D, 3 * D), (S, D), (16, D))],
        out_shape=[jax.ShapeDtypeStruct((D, 3 * D), bf), jax.ShapeDtypeStruct((S, D), bf), jax.ShapeDtypeStruct((16, D), f32)],
        compiler_params=pltpu.CompilerParams(vmem_limit_bytes=VM),
        name="input_gradients",
    )(x, dq, dk, dv, dr, w, sums, sb1)


def gather(shard):
    return lax.all_gather(shard, AXES, axis=0, tiled=True)


def scatter(grad):
    return lax.psum_scatter(grad, AXES, scatter_dimension=0, tiled=True)


def local(where, rows, cotangent, page_rows, pos_bucket, x_bucket, y_bucket, wq, bq, wk, wv, bv, wo, bo,
          ln1_gain, ln1_bias, w1, b1, w2, b2, ln2_gain, ln2_bias, pos_table, x_table, y_table):
    length, width = rows.shape[1:]
    share = wq.shape[0]
    wide, narrow, span = where[:3]
    n = wide * narrow
    kin = KIN if share % 8 == 0 else 1
    w_rest = gather(pack_call(w1, w2, n))
    bias, codes, w_all, small, b_up = front_call(
        where, pos_bucket[0], x_bucket[0], y_bucket[0], (pos_table.T, x_table.T, y_table.T), (wq, wk, wv, wo),
        (bq, bv, bo, ln1_gain, ln1_bias, b2, ln2_gain, ln2_bias, b1),
    )
    w_qkvo = w_all.reshape(width, 4 * width)
    query, keys, values, keys_t, values_t = qkv_call(rows[0], w_qkvo, small)
    prob, attended, inverse = fwd_call(page_rows, query, keys, values_t, bias)
    out_rows, normed, act, d_ffn, d_pre, d_mixed, d_branch, d_attended, inner, sums, sum_up = row_call(
        page_rows, attended, rows[0], cotangent[0], w_qkvo, w_rest, small, b_up
    )
    early, late = share_call(attended, normed, act, d_mixed, d_pre, d_ffn, kin)
    early, late, d_attended = lax.optimization_barrier((early, late, d_attended))
    late = scatter(late)
    early = early.reshape(n // (2 * span), 2, span, share, kin * width)
    dq, dk, dv, ds, early = bwd_call(where, query, d_attended, keys_t, values, prob, inverse, inner, early)
    grad_qkv, rows_grad, sums = input_call(rows[0], dq, dk, dv, d_branch, w_qkvo, sums, sum_up)
    grad_qkv = grad_qkv.reshape(n // (2 * span), 2, span, share, 3 * width)
    tables, first, vec = tail_call(where, ds, codes, grad_qkv, sums)
    g_out, g_up, g_down, g_query, g_key, g_value, g_pos, g_x, g_y, own = finish_call(early, late, first, vec, tables, n, narrow)
    return (
        out_rows[None], rows_grad[None], g_query, own[0], g_key, g_value, own[1], g_out, own[2], own[3], own[4],
        g_up, own[8], g_down, own[5], own[6], own[7], g_pos, g_x, g_y,
    )


def solution(mesh):
    wide, narrow = mesh.shape["wide"], mesh.shape["narrow"]
    small = wide <= 8
    where = (wide, narrow, 1 if small else narrow, wide // 2 if small else 8, 4 if small else narrow)
    cut3 = P(AXES, None, None)
    cut2 = P(AXES, None)
    cut1 = P(AXES)
    params = (cut2, cut1, cut2, cut2, cut1, cut2, cut1, cut1, cut1, cut2, cut1, cut2, cut1, cut1, cut1)
    in_specs = (cut3, cut3, cut1, cut3, cut3, cut3) + params + (P(), P(), P())
    out_specs = (cut3, cut3) + params + (P(), P(), P())
    return jax.shard_map(lambda *a: local(where, *a), mesh=mesh, in_specs=in_specs, out_specs=out_specs, check_vma=False)
```

```python
import jax
import jax.numpy as jnp
from jax import lax
from jax.experimental import pallas as pl
from jax.experimental.pallas import tpu as pltpu
from jax.sharding import PartitionSpec as P

bf = jnp.bfloat16
f32 = jnp.float32
NT = (((1,), (1,)), ((), ()))
NN = (((1,), (0,)), ((), ()))
TN = (((0,), (0,)), ((), ()))
AXES = ("wide", "narrow")
MESH = pl.DeviceIdType.MESH
BQ = 128
VM = 60 << 20
TABLE_SCALE = 3500.0
EPS = 1e-05
KIN = 4
SHORTEST = 709


class Place:
    def __init__(self, wide, narrow, span, depth, low):
        self.n = wide * narrow
        self.half = self.n // 2
        self.narrow = narrow
        self.span = span
        self.depth = depth
        self.low = low
        self.plane = self.half // depth
        self.flat = lax.axis_index("wide") * narrow + lax.axis_index("narrow")
        self.par = lax.rem(lax.div(self.flat, span), 2)
        self.group = lax.div(self.flat, 2 * span) * span + lax.rem(self.flat, span)
        self.q, self.z = self.split(self.group)

    def split(self, group):
        q = lax.div(group, self.depth * self.low) * self.low + lax.rem(group, self.low)
        return q, lax.rem(lax.div(group, self.low), self.depth)

    def join(self, q, z):
        return (lax.div(q, self.low) * self.depth + z) * self.low + lax.rem(q, self.low)

    def flat_of(self, group, par):
        return (lax.div(group, self.span) * 2 + par) * self.span + lax.rem(group, self.span)

    def device(self, flat):
        return (lax.div(flat, self.narrow), lax.rem(flat, self.narrow))

    def partner(self):
        return self.device(self.flat_of(self.group, 1 - self.par))

    def peer(self, k):
        return lax.rem(self.group + k, self.half)

    def peer_device(self, k):
        return self.device(self.flat_of(self.peer(k), self.par))

    def column(self, k):
        z = lax.rem(self.z + k, self.depth)
        return z, self.device(self.flat_of(self.join(self.q, z), self.par))

    def across(self, k):
        q = lax.rem(self.q + k, self.plane)
        return q, self.device(self.flat_of(self.join(q, self.z), self.par))

    def greet(self):
        barrier = pltpu.get_barrier_semaphore()
        pl.semaphore_signal(barrier, inc=1, device_id=self.partner(), device_id_type=MESH)

        def one(k, c):
            pl.semaphore_signal(barrier, inc=1, device_id=self.peer_device(k), device_id_type=MESH)
            return c

        lax.fori_loop(1, self.half, one, 0)
        pl.semaphore_wait(barrier, self.half)


def loop(first, last, body):
    def one(k, c):
        body(k)
        return c

    lax.fori_loop(first, last, one, 0)


class Scatter:
    shapes = staticmethod(
        lambda half, depth, block, kind: [
            pltpu.VMEM((half // depth, depth) + block, kind),
            pltpu.VMEM((half // depth, depth) + block, kind),
            pltpu.VMEM((half // depth, depth) + block, kind),
            pltpu.VMEM((depth,) + block, kind),
            pltpu.SemaphoreType.DMA((7,)),
        ]
    )

    def __init__(self, me, src, mine, came, plane, column, sem):
        self.me, self.src, self.mine, self.came, self.plane, self.column, self.sem = me, src, mine, came, plane, column, sem

    def begin(self):
        me, sem = self.me, self.sem

        def one(g):
            q, z = me.split(g)
            a, b = lax.div(g, me.span), lax.rem(g, me.span)
            send(self.src.at[a, 1 - me.par, b], self.came.at[q, z], sem.at[1], sem.at[2], me.partner())
            pltpu.make_async_copy(self.src.at[a, me.par, b], self.mine.at[q, z], sem.at[0]).start()

        loop(0, me.half, one)

    def to_plane(self):
        me, sem = self.me, self.sem
        drain(self.mine, sem.at[0])
        drain(self.came, sem.at[1])
        drain(self.came, sem.at[2])

        def add(g):
            q, z = me.split(g)
            self.mine[q, z] = (self.mine[q, z].astype(f32) + self.came[q, z].astype(f32)).astype(bf)

        loop(0, me.half, add)

        def one(k):
            q, device = me.across(k)
            send(self.mine.at[q], self.plane.at[me.q], sem.at[3], sem.at[4], device)

        loop(1, me.plane, one)

    def to_column(self):
        me, sem = self.me, self.sem
        others = pl.ds(0, me.plane - 1)
        drain(self.plane.at[others], sem.at[3])
        drain(self.plane.at[others], sem.at[4])

        def add(z):
            total = self.mine[me.q, z].astype(f32)
            for k in range(1, me.plane):
                total = total + self.plane[me.across(k)[0], z].astype(f32)
            self.mine[me.q, z] = total.astype(bf)

        loop(0, me.depth, add)

        def one(k):
            z, device = me.column(k)
            send(self.mine.at[me.q, z], self.column.at[me.z], sem.at[5], sem.at[6], device)

        loop(1, me.depth, one)

    def end(self, out):
        me, sem = self.me, self.sem
        others = pl.ds(0, me.depth - 1)
        drain(self.column.at[others], sem.at[5])
        drain(self.column.at[others], sem.at[6])
        total = self.mine[me.q, me.z].astype(f32)
        for k in range(1, me.depth):
            total = total + self.column[me.column(k)[0]].astype(f32)
        out[...] = total


def send(src, dst, send_sem, recv_sem, device):
    pltpu.make_async_remote_copy(src, dst, send_sem, recv_sem, device_id=device, device_id_type=MESH).start()


def drain(ref, sem):
    pltpu.make_async_copy(ref, ref, sem).wait()


def take(t, i):
    return jnp.take_along_axis(t, i, axis=1, mode="promise_in_bounds")


def front_kernel(where, pos_ref, x_ref, y_ref, pt_ref, xt_ref, yt_ref, wq_ref, wk_ref, wv_ref, *rest):
    vec_refs = rest[:9]
    out_ref, idx_ref, w_all, small_ref, up_ref, v_all, wpack, vpack, tab, lsem, ssem, rsem, xssem, xrsem = rest[9:]
    S = out_ref.shape[1]
    pid = pl.program_id(0)
    me = Place(*where)
    width = wq_ref.shape[1]

    @pl.when(pid == 0)
    def _():
        for n, ref in enumerate((wq_ref, wk_ref, wv_ref)):
            wpack[:, n * width : (n + 1) * width] = ref[...].astype(bf)
        vpack[...] = jnp.zeros_like(vpack)
        for n, ref in enumerate(vec_refs):
            vpack[n : n + 1, : ref.shape[1]] = ref[...].astype(bf)
        me.greet()
        pltpu.make_async_copy(wpack, w_all.at[me.flat], lsem.at[0]).start()
        pltpu.make_async_copy(vpack, v_all.at[me.flat], lsem.at[1]).start()
        send(vpack, v_all.at[me.flat], xssem.at[1], xrsem.at[1], me.partner())
        send(wpack, w_all.at[me.flat], xssem.at[0], xrsem.at[0], me.partner())

        def one(k):
            device = me.column(k)[1]
            send(vpack, v_all.at[me.flat], ssem.at[1], rsem.at[1], device)
            send(wpack, w_all.at[me.flat], ssem.at[0], rsem.at[0], device)

        loop(1, me.depth, one)
        tab[...] = jnp.zeros_like(tab)

        def pack(ref, row, lane):
            fixed = jnp.floor(ref[...].astype(bf).astype(f32) * TABLE_SCALE + 0.5).astype(jnp.int32)
            n = fixed.shape[1]
            for p in range(6):
                tab[row, p : p + 1, lane : lane + n] = fixed[2 * p : 2 * p + 1] * 65536 + fixed[2 * p + 1 : 2 * p + 2]

        pack(pt_ref, 0, 0)
        pack(xt_ref, 1, 0)
        pack(yt_ref, 1, 64)

    @pl.when(pid == 2)
    def _():
        others = pl.ds(0, me.depth - 1)
        drain(v_all.at[others], rsem.at[1])
        drain(w_all.at[others], rsem.at[0])
        pltpu.make_async_copy(wpack, w_all.at[me.flat], lsem.at[0]).wait()
        pltpu.make_async_copy(vpack, v_all.at[me.flat], lsem.at[1]).wait()

        def one(k):
            device = me.across(k)[1]

            def block(z):
                at = me.flat_of(me.join(me.q, z), me.par)
                send(v_all.at[at], v_all.at[at], ssem.at[3], rsem.at[3], device)
                send(w_all.at[at], w_all.at[at], ssem.at[2], rsem.at[2], device)

            loop(0, me.depth, block)

        loop(1, me.plane, one)

    @pl.when(pid == pl.num_programs(0) - 1)
    def _():
        others = pl.ds(0, (me.plane - 1) * me.depth)
        drain(v_all.at[others], rsem.at[3])
        drain(w_all.at[others], rsem.at[2])

        def one(k):
            at = me.flat_of(me.peer(k), me.par)
            send(v_all.at[at], v_all.at[at], xssem.at[1], xrsem.at[1], me.partner())
            send(w_all.at[at], w_all.at[at], xssem.at[0], xrsem.at[0], me.partner())

        loop(1, me.half, one)

    packed = pos_ref[...] | (x_ref[...] << 5) | (y_ref[...] << 11)
    idx_ref[...] = packed.T
    tp = [jnp.broadcast_to(tab[0, p : p + 1, :], (8, 128)) for p in range(6)]
    tx = [jnp.broadcast_to(tab[1, p : p + 1, :], (8, 128)) for p in range(6)]

    def body(r, c):
        for u in range(48):
            sl = pl.ds(pl.multiple_of((r * 48 + u) * 8, 8), 8)
            t = idx_ref[sl, :]
            p = t & 31
            x = (t >> 5) & 63
            y = (t >> 11) + 64
            g = [take(a, p) for a in tp]
            g = [a + take(b, x) for a, b in zip(g, tx)]
            g = [a + take(b, y) for a, b in zip(g, tx)]
            for k in range(6):
                out_ref[k, sl, :] = g[k]
        return c

    lax.fori_loop(0, S // (48 * 8), body, 0)

    @pl.when(pid == pl.num_programs(0) - 1)
    def _():
        mine = pl.ds(0, me.half)
        near, far = pl.ds(0, me.depth - 1), pl.ds(0, (me.plane - 1) * me.depth)
        drain(w_all.at[near], ssem.at[0])
        drain(v_all.at[near], ssem.at[1])
        drain(w_all.at[far], ssem.at[2])
        drain(v_all.at[far], ssem.at[3])
        for sem in (xssem, xrsem):
            drain(w_all.at[mine], sem.at[0])
            drain(v_all.at[mine], sem.at[1])
        share = wpack.shape[0]
        for d in range(me.n):
            block = v_all[d].astype(f32)
            at = pl.ds(d * share, share)
            small_ref[:, at] = block[0:8, :share]
            for m in range(4):
                up_ref[m : m + 1, at] = block[8:9, m * share : (m + 1) * share]


def front_call(where, pos, x, y, tables, weights, vectors):
    S = pos.shape[0]
    share, width = weights[0].shape
    n = where[0] * where[1]

    def whole(a):
        return pl.BlockSpec(a.shape, lambda i: (0,) * a.ndim)

    small = tuple(tables) + tuple(weights) + tuple(v.reshape(1, -1) for v in vectors)
    return pl.pallas_call(
        lambda *a: front_kernel(where, *a),
        grid=(S // BQ,),
        in_specs=[pl.BlockSpec((BQ, S), lambda i: (i, 0))] * 3 + [whole(a) for a in small],
        out_specs=[
            pl.BlockSpec((6, S, BQ), lambda i: (0, 0, i)),
            pl.BlockSpec((S, BQ), lambda i: (0, i)),
            pl.BlockSpec(memory_space=pl.ANY),
            pl.BlockSpec((8, width), lambda i: (0, 0)),
            pl.BlockSpec((4, width), lambda i: (0, 0)),
        ],
        out_shape=[
            jax.ShapeDtypeStruct((6, S, S), jnp.int32),
            jax.ShapeDtypeStruct((S, S), jnp.int32),
            jax.ShapeDtypeStruct((n, share, 3 * width), bf),
            jax.ShapeDtypeStruct((8, width), f32),
            jax.ShapeDtypeStruct((4, width), f32),
        ],
        scratch_shapes=[
            pltpu.VMEM((n, 16, 128), bf),
            pltpu.VMEM((share, 3 * width), bf),
            pltpu.VMEM((16, 128), bf),
            pltpu.VMEM((2, 8, 128), jnp.int32),
        ]
        + [pltpu.SemaphoreType.DMA((4,))] * 5,
        compiler_params=pltpu.CompilerParams(vmem_limit_bytes=VM, collective_id=0, has_side_effects=True),
        name="bias_and_gather",
    )(pos, x, y, *small)


def pack_call(wo, w1, w2, n):
    share, wide = w1.shape
    width = wide // 4
    pieces = share % 8 == 0
    if not pieces:
        w1 = jnp.transpose(w1.reshape(share, n, 4, share), (0, 2, 1, 3)).reshape(share, 4 * width)

    def kernel(wo_ref, w1_ref, w2_ref, a_ref, scr):
        a_ref[:, 8 * width :] = wo_ref[...].astype(bf)
        if pieces:
            for d in range(n):
                for m in range(4):
                    at = m * width + d * share
                    scr[:, at : at + share] = w1_ref[:, (4 * d + m) * share : (4 * d + m + 1) * share]
            a_ref[:, : 4 * width] = scr[...].astype(bf)
        else:
            a_ref[:, : 4 * width] = w1_ref[...].astype(bf)
        for m in range(4):
            a_ref[:, (4 + m) * width : (5 + m) * width] = w2_ref[m * share : (m + 1) * share, :].astype(bf)

    return pl.pallas_call(
        kernel,
        out_shape=jax.ShapeDtypeStruct((share, 9 * width), bf),
        scratch_shapes=[pltpu.VMEM((share, 4 * width), f32)],
        name="round_shares",
    )(wo, w1, w2)


def finish_call(early, late, first, vec, tables, n, narrow):
    share, width = first.shape[0], vec.shape[1]
    pieces = share % 8 == 0
    kin = early.shape[1] // width

    def kernel(e_ref, s_ref, f_ref, v_ref, t_ref, wo_ref, w1_ref, w2_ref, wq_ref, wk_ref, wv_ref, gp_ref, gx_ref, gy_ref, *rest):
        vec_refs, scr = rest[:9], rest[9]
        flat = lax.axis_index("wide") * narrow + lax.axis_index("narrow")

        def part(k):
            if k < kin:
                return e_ref[:, k * width : (k + 1) * width]
            return s_ref[:, (k - kin) * width : (k - kin + 1) * width].astype(f32)

        for k, ref in enumerate((wq_ref, wk_ref, wv_ref)):
            ref[...] = f_ref[:, k * width : (k + 1) * width]
        gx_ref[...] = t_ref[0:12, 0:64]
        gy_ref[...] = t_ref[0:12, 64:128]
        gp_ref[...] = t_ref[0:12, 128:160]
        wo_ref[...] = part(0)
        for m in range(4):
            scr[:, m * width : (m + 1) * width] = part(1 + m)
            w2_ref[m * share : (m + 1) * share, :] = part(5 + m)
        if pieces:
            for d in range(n):
                for m in range(4):
                    at = m * width + d * share
                    w1_ref[:, (4 * d + m) * share : (4 * d + m + 1) * share] = scr[:, at : at + share]
        else:
            w1_ref[...] = scr[...]
        own = jnp.zeros((16, share), f32)
        for d in range(n):
            own = jnp.where(flat == d, v_ref[:, d * share : (d + 1) * share], own)
        for k in range(8):
            vec_refs[k][...] = own[k : k + 1, :]
        for m in range(4):
            vec_refs[8][:, m * share : (m + 1) * share] = own[8 + m : 9 + m, :]

    outs = [(share, width), (share, 4 * width), (4 * share, width)] + [(share, width)] * 3 + [(12, 32), (12, 64), (12, 64)]
    outs += [(1, share)] * 8 + [(1, 4 * share)]
    outs = pl.pallas_call(
        kernel,
        out_shape=[jax.ShapeDtypeStruct(s, f32) for s in outs],
        scratch_shapes=[pltpu.VMEM((share, 4 * width), f32)],
        name="own_shares",
    )(early, late, first, vec, tables)
    g_up = outs[1]
    if not pieces:
        g_up = jnp.transpose(g_up.reshape(share, 4, n, share), (0, 2, 1, 3)).reshape(share, 4 * width)
    return [outs[0], g_up, outs[2], *outs[3:6], *[t.T for t in outs[6:9]], [v.reshape(-1) for v in outs[9:]]]


def stack2(a):
    lane=lax.broadcasted_iota(jnp.int32,a.shape,1)
    z=jnp.zeros_like(a)
    return jnp.concatenate([jnp.where(lane<64,a,z),jnp.where(lane<64,z,a)],axis=0)

def fwd_kernel(live_ref, q_ref, k_ref, vt_ref, b_ref, e_ref, o_ref, l_ref, s_scr, *, CH):
    S = k_ref.shape[0]
    live = live_ref[0]
    c = 1.0 / (TABLE_SCALE * 65536.0)
    chunks = range(S // CH)
    rows = lax.broadcasted_iota(jnp.int32, (CH, 1), 0)
    sub = lax.broadcasted_iota(jnp.int32, (128, 128), 0)

    def scores(p, qs, top, ch):
        r = pl.ds(ch * CH, CH)
        s = lax.dot_general(k_ref[r, pl.ds(p * 128, 128)], qs, NT, preferred_element_type=f32)
        b = b_ref[p, r, :]
        s = s + jnp.concatenate([b.astype(f32) * c, (b << 16).astype(f32) * c], axis=1)
        if (ch + 1) * CH > SHORTEST:
            s = jnp.where(rows + ch * CH < live, s, -1e9)
        s_scr[p % 2, r, :] = s
        return jnp.maximum(top, jnp.max(s.reshape(CH // 8, 8, 256), axis=0))

    low = jnp.full((8, 256), -3e38, f32)
    top = low
    qs = stack2(q_ref[:, pl.ds(0, 128)])
    for ch in chunks:
        top = scores(0, qs, top, ch)
    for p in range(6):
        ln = pl.ds(p * 128, 128)
        peak = jnp.max(top, axis=0, keepdims=True)
        top = low
        total = jnp.zeros((8, 256), f32)
        if p < 5:
            qs = stack2(q_ref[:, pl.ds((p + 1) * 128, 128)])
        for ch in chunks:
            if p < 5:
                top = scores(p + 1, qs, top, ch)
            r = pl.ds(ch * CH, CH)
            e = jnp.exp(s_scr[p % 2, r, :] - peak)
            total = total + jnp.sum(e.reshape(CH // 8, 8, 256), axis=0)
            eb = e.astype(bf)
            e_ref[2 * p, r, :] = eb[:, :128]
            e_ref[2 * p + 1, r, :] = eb[:, 128:]
        linv = 1.0 / jnp.sum(total, axis=0, keepdims=True)
        l_ref[2 * p : 2 * p + 1, :] = linv[:, :128]
        l_ref[2 * p + 1 : 2 * p + 2, :] = linv[:, 128:]
        both = jnp.concatenate([e_ref[2 * p], e_ref[2 * p + 1]], axis=1)
        acc = lax.dot_general(vt_ref[ln, :], both, NN, preferred_element_type=f32) * linv
        o_ref[:, ln] = jnp.where(sub < 64, acc[:, :128], acc[:, 128:]).T.astype(bf)


def fwd_call(live, q, k, vt, b, CH=128):
    S, D = k.shape
    return pl.pallas_call(
        lambda *a: fwd_kernel(*a, CH=CH),
        grid_spec=pltpu.PrefetchScalarGridSpec(
            num_scalar_prefetch=1,
            grid=(S // BQ,),
            in_specs=[
                pl.BlockSpec((BQ, D), lambda i, *_: (i, 0)),
                pl.BlockSpec((S, D), lambda i, *_: (0, 0)),
                pl.BlockSpec((D, S), lambda i, *_: (0, 0)),
                pl.BlockSpec((6, S, BQ), lambda i, *_: (0, 0, i)),
            ],
            out_specs=[
                pl.BlockSpec((12, S, BQ), lambda i, *_: (0, 0, i)),
                pl.BlockSpec((BQ, D), lambda i, *_: (i, 0)),
                pl.BlockSpec((16, BQ), lambda i, *_: (0, i)),
            ],
            scratch_shapes=[pltpu.VMEM((2, S, 256), f32)],
        ),
        out_shape=[
            jax.ShapeDtypeStruct((12, S, S), bf),
            jax.ShapeDtypeStruct((S, D), bf),
            jax.ShapeDtypeStruct((16, S), f32),
        ],
        compiler_params=pltpu.CompilerParams(vmem_limit_bytes=VM),
        name="attention_forward",
    )(live, q, k, vt, b)


def bwd_kernel(where, q_ref, do_ref, kt_ref, v_ref, e_ref, l_ref, d_ref, g_ref, dq_ref, dk_ref, dv_ref, ds_ref, out_ref, ds_scr, dk_acc, dv_acc, *rest):
    S = v_ref.shape[0]
    pid = pl.program_id(0)
    me = Place(*where)
    travel = Scatter(me, g_ref, *rest)

    @pl.when(pid == 0)
    def _():
        me.greet()
        travel.begin()

    @pl.when(pid == 1)
    def _():
        travel.to_plane()

    @pl.when(pid == 6)
    def _():
        travel.to_column()

    @pl.when(pid == 0)
    def _():
        dk_acc[...] = jnp.zeros_like(dk_acc)
        dv_acc[...] = jnp.zeros_like(dv_acc)

    lane = lax.broadcasted_iota(jnp.int32, (BQ, 128), 1)
    sub = lax.broadcasted_iota(jnp.int32, (128, 128), 0)
    for p in range(6):
        ln = pl.ds(p * 128, 128)
        qs = stack2(q_ref[:, ln])
        l2 = l_ref[2 * p : 2 * p + 2, :]
        d2 = d_ref[2 * p : 2 * p + 2, :] * l2
        lcol = jnp.concatenate([l2] * 4, axis=0).T
        dos = stack2((do_ref[:, ln].astype(f32) * jnp.where(lane < 64, lcol[:, 0:1], lcol[:, 1:2])).astype(bf))
        dp = lax.dot_general(v_ref[:, ln], dos, NT, preferred_element_type=f32)
        e0 = e_ref[2 * p]
        e1 = e_ref[2 * p + 1]
        s0 = e0.astype(f32) * (dp[:, :128] - d2[0:1, :])
        s1 = e1.astype(f32) * (dp[:, 128:] - d2[1:2, :])
        ds_scr[pl.ds(2 * p, S, stride=16), :] = s0
        ds_scr[pl.ds(2 * p + 1, S, stride=16), :] = s1
        both = jnp.concatenate([s0.astype(bf), s1.astype(bf)], axis=1)
        dk_acc[:, ln] += lax.dot_general(both, qs, NN, preferred_element_type=f32)
        dv_acc[:, ln] += lax.dot_general(jnp.concatenate([e0, e1], axis=1), dos, NN, preferred_element_type=f32)
        a = lax.dot_general(kt_ref[ln, :], both, NN, preferred_element_type=f32)
        dq_ref[:, ln] = (jnp.where(sub < 64, a[:, :128], a[:, 128:]).T * 0.125).astype(bf)
    ds_ref[...] = ds_scr[...].astype(bf)

    @pl.when(pid == pl.num_programs(0) - 1)
    def _():
        dk_ref[...] = dk_acc[...].astype(bf)
        dv_ref[...] = dv_acc[...].astype(bf)
        travel.end(out_ref)


def bwd_call(where, q, do, kt, v, e, linv, dd, g):
    S, D = v.shape
    half = where[0] * where[1] // 2
    block = g.shape[3:]
    fixed = pl.Buffered(1)
    full = pl.BlockSpec((S, D), lambda i: (0, 0))
    blk = pl.BlockSpec((BQ, D), lambda i: (i, 0))
    row = pl.BlockSpec((16, BQ), lambda i: (0, i))
    return pl.pallas_call(
        lambda *a: bwd_kernel(where, *a),
        grid=(S // BQ,),
        in_specs=[
            blk,
            blk,
            pl.BlockSpec((D, S), lambda i: (0, 0), pipeline_mode=fixed),
            pl.BlockSpec((S, D), lambda i: (0, 0), pipeline_mode=fixed),
            pl.BlockSpec((12, S, BQ), lambda i: (0, 0, i)),
            row,
            row,
            pl.BlockSpec(memory_space=pl.ANY),
        ],
        out_specs=[blk, full, full, pl.BlockSpec((S * 16, BQ), lambda i: (0, i)), pl.BlockSpec(block, lambda i: (0, 0))],
        scratch_shapes=[pltpu.VMEM((S * 16, BQ), f32), pltpu.VMEM((S, D), f32), pltpu.VMEM((S, D), f32)]
        + Scatter.shapes(half, where[3], block, bf),
        out_shape=[jax.ShapeDtypeStruct((S, D), bf)] * 3 + [jax.ShapeDtypeStruct((S * 16, S), bf), jax.ShapeDtypeStruct(block, f32)],
        compiler_params=pltpu.CompilerParams(vmem_limit_bytes=VM, collective_id=2, has_side_effects=True),
        name="attention_backward_and_scatter",
    )(q, do, kt, v, e, linv, dd, g)


def tail_kernel(where, U, ds_ref, idx_ref, gw_ref, gv_ref, t_ref, w_out, v_out, *rest):
    acc, xi_scr, v_in, v_mine, v_near, v_far, h_mine, h_in, h_near, h_far, xssem, xrsem, ssem, rsem = rest[:14]
    S = idx_ref.shape[0]
    pid = pl.program_id(0)
    me = Place(*where)
    travel = Scatter(me, gw_ref, *rest[14:])
    near, far = pl.ds(0, me.plane - 1), pl.ds(0, me.depth - 1)

    @pl.when(pid == 0)
    def _():
        acc[...] = jnp.zeros_like(acc)
        me.greet()
        send(gv_ref, v_in, xssem.at[1], xrsem.at[1], me.partner())
        travel.begin()

    @pl.when(pid == 1)
    def _():
        drain(v_in, xssem.at[1])
        drain(v_in, xrsem.at[1])
        v_mine[0] = gv_ref[...] + v_in[...]

        def one(k):
            send(v_mine.at[0], v_near.at[me.q], ssem.at[0], rsem.at[0], me.across(k)[1])

        loop(1, me.plane, one)
        travel.to_plane()

    @pl.when(pid == 5)
    def _():
        drain(v_near.at[near], ssem.at[0])
        drain(v_near.at[near], rsem.at[0])
        v_mine[1] = lax.fori_loop(1, me.plane, lambda k, t: t + v_near[me.across(k)[0]], v_mine[0])

        def one(k):
            send(v_mine.at[1], v_far.at[me.z], ssem.at[1], rsem.at[1], me.column(k)[1])

        loop(1, me.depth, one)
        travel.to_column()

    t = idx_ref[...]
    xi_scr[0] = (t & 31).astype(f32)
    xi_scr[1] = ((t >> 5) & 63).astype(f32)
    xi_scr[2] = (t >> 11).astype(f32)
    iot = lax.broadcasted_iota(jnp.int32, (16, 128), 0).astype(f32).astype(bf)
    one = jnp.ones((16, 128), bf)
    zero = jnp.zeros((16, 128), bf)

    def one_j(j):
        bp, bx, by = [jnp.broadcast_to(xi_scr[n, pl.ds(j, 1), :], (16, 128)).astype(bf) for n in range(3)]
        d = ds_ref[pl.ds(pl.multiple_of(j * 16, 16), 16), :]
        xh = bx >= 32
        yh = by >= 32
        bxl = jnp.where(xh, bx - 32, bx)
        byl = jnp.where(yh, by - 32, by)
        ph = bp >= 16
        bpl = jnp.where(ph, bp - 16, bp)
        rows = [jnp.where(b == iot + bf(16 * k), one, zero) for b in (bxl, byl) for k in range(2)]
        rows.append(jnp.where(bpl == iot, one, zero))
        rhs = [d, jnp.where(xh, d, zero), jnp.where(yh, d, zero), jnp.where(ph, d, zero)]
        return jnp.concatenate(rows, 0), jnp.concatenate(rhs, 0)

    def body(t, total):
        for u in range(U):
            l0, r0 = one_j(t * 2 * U + 2 * u)
            l1, r1 = one_j(t * 2 * U + 2 * u + 1)
            total = total + lax.dot_general(
                jnp.concatenate([l0, l1], 1), jnp.concatenate([r0, r1], 1), NT, preferred_element_type=f32
            )
        return total

    acc[:, :64] += lax.fori_loop(0, S // (2 * U), body, jnp.zeros((80, 64), f32))

    @pl.when(pid == pl.num_programs(0) - 1)
    def _():
        h = acc[...].T
        total, x1, y1, p1 = h[0:16], h[16:32, 0:32], h[32:48, 32:64], h[48:64, 64:80]
        parts = [total[:, 0:32] - x1, x1, total[:, 32:64] - y1, y1, total[:, 64:80] - p1, p1, jnp.zeros((16, 96), f32)]
        h = jnp.concatenate(parts, axis=1)
        h_mine[...] = jnp.where(lax.broadcasted_iota(jnp.int32, h.shape, 0) < 12, h, 0.0)
        send(h_mine, h_in, xssem.at[2], xrsem.at[2], me.partner())
        drain(v_far.at[far], ssem.at[1])
        drain(v_far.at[far], rsem.at[1])
        v_out[...] = lax.fori_loop(1, me.depth, lambda k, t: t + v_far[me.column(k)[0]], v_mine[1])
        travel.end(w_out)
        drain(h_in, xssem.at[2])
        drain(h_in, xrsem.at[2])
        h_mine[...] = h_mine[...] + h_in[...]

        def across(k):
            send(h_mine, h_near.at[me.q], ssem.at[2], rsem.at[2], me.across(k)[1])

        loop(1, me.plane, across)
        drain(h_near.at[near], ssem.at[2])
        drain(h_near.at[near], rsem.at[2])
        h_in[...] = lax.fori_loop(1, me.plane, lambda k, t: t + h_near[me.across(k)[0]], h_mine[...])

        def along(k):
            send(h_in, h_far.at[me.z], ssem.at[3], rsem.at[3], me.column(k)[1])

        loop(1, me.depth, along)
        drain(h_far.at[far], ssem.at[3])
        drain(h_far.at[far], rsem.at[3])
        t_ref[...] = lax.fori_loop(1, me.depth, lambda k, t: t + h_far[me.column(k)[0]], h_in[...])


def tail_call(where, ds, codes, gw, gv, U=144):
    S = codes.shape[0]
    half, depth = where[0] * where[1] // 2, where[3]
    share, cols = gw.shape[3:]

    def whole(shape):
        return pl.BlockSpec(shape, lambda i: (0,) * len(shape))

    outs = [(16, 256), (share, cols), gv.shape]
    return pl.pallas_call(
        lambda *a: tail_kernel(where, U, *a),
        grid=(S // BQ,),
        in_specs=[
            pl.BlockSpec((S * 16, BQ), lambda i: (0, i)),
            pl.BlockSpec((S, BQ), lambda i: (0, i)),
            pl.BlockSpec(memory_space=pl.ANY),
            whole(gv.shape),
        ],
        out_specs=[whole(s) for s in outs],
        out_shape=[jax.ShapeDtypeStruct(s, f32) for s in outs],
        scratch_shapes=[
            pltpu.VMEM((80, 128), f32),
            pltpu.VMEM((3, S, BQ), f32),
            pltpu.VMEM(gv.shape, f32),
            pltpu.VMEM((2,) + gv.shape, f32),
            pltpu.VMEM((half // depth,) + gv.shape, f32),
            pltpu.VMEM((depth,) + gv.shape, f32),
            pltpu.VMEM((16, 256), f32),
            pltpu.VMEM((16, 256), f32),
            pltpu.VMEM((half // depth, 16, 256), f32),
            pltpu.VMEM((depth, 16, 256), f32),
        ]
        + [pltpu.SemaphoreType.DMA((4,))] * 4
        + Scatter.shapes(half, depth, (share, cols), bf),
        compiler_params=pltpu.CompilerParams(vmem_limit_bytes=VM, collective_id=1, has_side_effects=True),
        name="table_sums_and_scatter",
    )(ds, codes, gw, gv)


GELU_COEFS = (0.254829592, -0.284496736, 1.421413741, -1.453152027, 1.061405429)


def gelu_both(z):
    t = pltpu.reciprocal(1.0 + (0.3275911 * 0.7071067811865476) * jnp.abs(z), approx=False)
    q = jnp.exp(z * z * -0.5)
    poly = 0.5 * GELU_COEFS[4] * t + 0.5 * GELU_COEFS[3]
    for c in GELU_COEFS[2::-1]:
        poly = poly * t + 0.5 * c
    half = poly * t * q
    cdf = jnp.where(z >= 0, 1.0 - half, half)
    return z * cdf, cdf + z * (q * 0.3989422804014327)


def norm_stats(u):
    mean = jnp.mean(u, axis=-1, keepdims=True)
    center = u - mean
    inv = lax.rsqrt(jnp.mean(center * center, axis=-1, keepdims=True) + EPS)
    return center * inv, inv


def norm_pull(e, normed, inv):
    return (e - jnp.mean(e, axis=-1, keepdims=True) - normed * jnp.mean(e * normed, axis=-1, keepdims=True)) * inv


def fold8(u):
    return jnp.sum(u.reshape(u.shape[0] // 8, 8, u.shape[1]), axis=0)


def row_kernel(live_ref, at_ref, x_ref, ct_ref, w_ref, v_ref, b1_ref,
               out_ref, h_ref, g_ref, df_ref, dz_ref, da_ref, dr_ref, dat_ref, dd_ref, sum_ref, sb1_ref,
               gp_scr, z_scr, acc, h_scr, n1_scr, i1_scr, *, R, SL):
    pid = pl.program_id(0)
    D = x_ref.shape[1]
    live = live_ref[0]
    b_out, g1, s1, b_down, g2, s2 = [v_ref[n : n + 1, :] for n in range(2, 8)]

    @pl.when(pid == 0)
    def _():
        sum_ref[...] = jnp.zeros_like(sum_ref)
        sb1_ref[...] = jnp.zeros_like(sb1_ref)

    def add(row, part):
        sum_ref[row : row + 1, :] += jnp.sum(part, axis=0, keepdims=True)

    acc[...] = lax.dot_general(at_ref[...], w_ref[:, 8 * D :], NN, preferred_element_type=f32)
    for r in range(0, R, SL):
        sl = pl.ds(r, SL)
        n1, inv = norm_stats(x_ref[sl, :].astype(f32) + acc[sl, :] + b_out)
        n1_scr[sl, :] = n1
        i1_scr[sl, :] = jnp.broadcast_to(inv, (SL, 128))
        h1 = n1 * g1 + s1
        h_scr[sl, :] = h1
        h_ref[sl, :] = h1.astype(bf)
    for c in range(4):
        cols = pl.ds(c * D, D)
        z_scr[c % 2] = lax.dot_general(h_ref[...], w_ref[:, pl.ds(c * D, D)], NN, preferred_element_type=f32)
        for r in range(0, R, SL):
            sl = pl.ds(r, SL)
            g, gp = gelu_both(z_scr[c % 2, sl, :] + b1_ref[c : c + 1, :])
            g_ref[sl, cols] = g.astype(bf)
            gp_scr[sl, cols] = gp
        part = lax.dot_general(g_ref[:, cols], w_ref[:, pl.ds((4 + c) * D, D)], NN, preferred_element_type=f32)
        if c == 0:
            acc[...] = part
        else:
            acc[...] += part
    p_gain = p_shift = p_down = jnp.zeros((8, D), f32)
    rows = lax.broadcasted_iota(jnp.int32, (SL, 1), 0) + pid * R
    for r in range(0, R, SL):
        sl = pl.ds(r, SL)
        n2, inv = norm_stats(h_scr[sl, :] + acc[sl, :] + b_down)
        out_ref[sl, :] = (n2 * g2 + s2).astype(bf)
        dy = jnp.where(rows + r < live, ct_ref[sl, :].astype(f32), 0.0)
        dr2 = norm_pull(dy * g2, n2, inv)
        df = dr2.astype(bf)
        df_ref[sl, :] = df
        h_scr[sl, :] = dr2
        p_gain = p_gain + fold8(dy * n2)
        p_shift = p_shift + fold8(dy)
        p_down = p_down + fold8(df.astype(f32))
    add(5, p_down)
    add(6, p_gain)
    add(7, p_shift)
    for c in range(4):
        cols = pl.ds(c * D, D)
        z_scr[c % 2] = lax.dot_general(df_ref[...], w_ref[:, pl.ds((4 + c) * D, D)], NT, preferred_element_type=f32)
        p_up = jnp.zeros((8, D), f32)
        for r in range(0, R, SL):
            sl = pl.ds(r, SL)
            dz = (z_scr[c % 2, sl, :] * gp_scr[sl, cols]).astype(bf)
            dz_ref[sl, cols] = dz
            p_up = p_up + fold8(dz.astype(f32))
        sb1_ref[c : c + 1, :] += jnp.sum(p_up, axis=0, keepdims=True)
        part = lax.dot_general(dz_ref[:, cols], w_ref[:, pl.ds(c * D, D)], NT, preferred_element_type=f32)
        if c == 0:
            acc[...] = part
        else:
            acc[...] += part
    p_gain = p_shift = p_out = jnp.zeros((8, D), f32)
    for r in range(0, R, SL):
        sl = pl.ds(r, SL)
        dh = h_scr[sl, :] + acc[sl, :]
        n1 = n1_scr[sl, :]
        dr1 = norm_pull(dh * g1, n1, i1_scr[sl, 0:1])
        da = dr1.astype(bf)
        dr_ref[sl, :] = dr1
        da_ref[sl, :] = da
        p_gain = p_gain + fold8(dh * n1)
        p_shift = p_shift + fold8(dh)
        p_out = p_out + fold8(da.astype(f32))
    add(2, p_out)
    add(3, p_gain)
    add(4, p_shift)
    dat_ref[...] = lax.dot_general(da_ref[...], w_ref[:, 8 * D :], NT, preferred_element_type=f32).astype(bf)
    seg = (lax.div(lax.broadcasted_iota(jnp.int32, (D, 128), 0), 64) == lax.broadcasted_iota(jnp.int32, (D, 128), 1)).astype(f32).astype(bf)
    for r in range(0, R, 128):
        sl = pl.ds(r, 128)
        prod = dat_ref[sl, :].astype(f32) * at_ref[sl, :].astype(f32)
        high = prod.astype(bf)
        low = (prod - high.astype(f32)).astype(bf)
        d = lax.dot_general(high, seg, NN, preferred_element_type=f32) + lax.dot_general(low, seg, NN, preferred_element_type=f32)
        dd_ref[:, sl] = d.T[0:16, :]


def row_call(live, attended, x, ct, w, v, b1, R=384, SL=16):
    S, D = x.shape
    blk = pl.BlockSpec((R, D), lambda i, *_: (i, 0))
    big = pl.BlockSpec((R, 4 * D), lambda i, *_: (i, 0))

    def whole(shape, **kw):
        return pl.BlockSpec(shape, lambda i, *_: (0,) * len(shape), **kw)

    shapes = [((S, D), bf), ((S, D), bf), ((S, 4 * D), bf), ((S, D), bf), ((S, 4 * D), bf), ((S, D), bf), ((S, D), f32), ((S, D), bf),
              ((16, S), f32), ((8, D), f32), ((4, D), f32)]
    return pl.pallas_call(
        lambda *a: row_kernel(*a, R=R, SL=SL),
        grid_spec=pltpu.PrefetchScalarGridSpec(
            num_scalar_prefetch=1,
            grid=(S // R,),
            in_specs=[blk, blk, blk, whole(w.shape, pipeline_mode=pl.Buffered(1)), whole(v.shape), whole(b1.shape)],
            out_specs=[blk, blk, big, blk, big, blk, blk, blk, pl.BlockSpec((16, R), lambda i, *_: (0, i)), whole((8, D)), whole((4, D))],
            scratch_shapes=[
                pltpu.VMEM((R, 4 * D), f32),
                pltpu.VMEM((2, R, D), f32),
                pltpu.VMEM((R, D), f32),
                pltpu.VMEM((R, D), f32),
                pltpu.VMEM((R, D), f32),
                pltpu.VMEM((R, 128), f32),
            ],
        ),
        out_shape=[jax.ShapeDtypeStruct(s, d) for s, d in shapes],
        compiler_params=pltpu.CompilerParams(vmem_limit_bytes=VM),
        name="rows_forward_backward",
    )(live, attended, x, ct, w, v, b1)


def share_kernel(kin, at_ref, h_ref, g_ref, da_ref, dz_ref, df_ref, early_ref, late_ref):
    c = pl.program_id(0)
    for first, last, a_ref, b_ref in ((0, 1, at_ref, da_ref), (1, 5, h_ref, dz_ref), (5, 9, g_ref, df_ref)):
        for low, high, out in ((first, min(last, kin), early_ref), (max(first, kin), last, late_ref)):
            if low < high:

                @pl.when((c >= low) & (c < high))
                def _(a_ref=a_ref, b_ref=b_ref, out=out):
                    out[...] = lax.dot_general(a_ref[...], b_ref[...], TN, preferred_element_type=f32).astype(bf)


def share_call(attended, h, g, da, dz, df, kin):
    S, D = h.shape

    def fixed():
        return pl.BlockSpec((S, D), lambda c: (0, 0), pipeline_mode=pl.Buffered(1))

    return pl.pallas_call(
        lambda *a: share_kernel(kin, *a),
        grid=(9,),
        in_specs=[
            fixed(),
            fixed(),
            pl.BlockSpec((S, D), lambda c: (0, jnp.clip(c - 5, 0, 3))),
            fixed(),
            pl.BlockSpec((S, D), lambda c: (0, jnp.clip(c - 1, 0, 3))),
            fixed(),
        ],
        out_specs=[
            pl.BlockSpec((D, D), lambda c: (0, jnp.minimum(c, kin - 1))),
            pl.BlockSpec((D, D), lambda c: (0, jnp.maximum(c - kin, 0))),
        ],
        out_shape=[jax.ShapeDtypeStruct((D, kin * D), bf), jax.ShapeDtypeStruct((D, (9 - kin) * D), bf)],
        compiler_params=pltpu.CompilerParams(vmem_limit_bytes=VM),
        name="weight_gradients",
    )(attended, h, g, da, dz, df)


def qkv_call(x, w, v, R=384):
    S, D = x.shape

    def kernel(x_ref, w_ref, v_ref, q_ref, k_ref, o_ref, kt_ref, ot_ref):
        x = x_ref[...]
        q_ref[...] = (lax.dot_general(x, w_ref[:, :D], NN, preferred_element_type=f32) + v_ref[0:1, :]).astype(bf) * bf(0.125)
        k_ref[...] = lax.dot_general(x, w_ref[:, D : 2 * D], NN, preferred_element_type=f32).astype(bf)
        o_ref[...] = (lax.dot_general(x, w_ref[:, 2 * D :], NN, preferred_element_type=f32) + v_ref[1:2, :]).astype(bf)
        kt_ref[...] = k_ref[...].T
        ot_ref[...] = o_ref[...].T

    blk = pl.BlockSpec((R, D), lambda i: (i, 0))
    turned = pl.BlockSpec((D, R), lambda i: (0, i))
    return pl.pallas_call(
        kernel,
        grid=(S // R,),
        in_specs=[blk, pl.BlockSpec((D, 3 * D), lambda i: (0, 0), pipeline_mode=pl.Buffered(1)), pl.BlockSpec(v.shape, lambda i: (0, 0))],
        out_specs=[blk] * 3 + [turned] * 2,
        out_shape=[jax.ShapeDtypeStruct((S, D), bf)] * 3 + [jax.ShapeDtypeStruct((D, S), bf)] * 2,
        compiler_params=pltpu.CompilerParams(vmem_limit_bytes=VM),
        name="project_qkv",
    )(x, w, v)


def input_kernel(x_ref, dq_ref, dk_ref, dv_ref, dr_ref, w_ref, s_ref, b1_ref, gw_ref, rg_ref, v_ref):
    D = x_ref.shape[1]
    for n, ref in enumerate((dq_ref, dk_ref, dv_ref)):
        gw_ref[:, n * D : (n + 1) * D] = lax.dot_general(x_ref[...], ref[...], TN, preferred_element_type=f32).astype(bf)
    S = x_ref.shape[0]
    v_ref[...] = jnp.concatenate([s_ref[...], b1_ref[...], jnp.zeros((4, D), f32)], axis=0)
    for row, ref in ((0, dq_ref), (1, dv_ref)):
        part = jnp.zeros((8, D), f32)
        for r in range(0, S, 64):
            part = part + fold8(ref[pl.ds(r, 64), :].astype(f32))
        v_ref[row : row + 1, :] = jnp.sum(part, axis=0, keepdims=True)
    for r in range(0, S, 384):
        sl = pl.ds(r, 384)
        total = dr_ref[sl, :]
        for n, ref in enumerate((dq_ref, dk_ref, dv_ref)):
            total = total + lax.dot_general(ref[sl, :], w_ref[:, n * D : (n + 1) * D], NT, preferred_element_type=f32)
        rg_ref[sl, :] = total.astype(bf)


def input_call(x, dq, dk, dv, dr, w, sums, sb1):
    S, D = x.shape
    return pl.pallas_call(
        input_kernel,
        grid=(1,),
        in_specs=[pl.BlockSpec(a.shape, lambda i: (0, 0)) for a in (x, dq, dk, dv, dr)]
        + [pl.BlockSpec((D, 3 * D), lambda i: (0, 0))]
        + [pl.BlockSpec(a.shape, lambda i: (0, 0)) for a in (sums, sb1)],
        out_specs=[pl.BlockSpec(s, lambda i: (0, 0)) for s in ((D, 3 * D), (S, D), (16, D))],
        out_shape=[jax.ShapeDtypeStruct((D, 3 * D), bf), jax.ShapeDtypeStruct((S, D), bf), jax.ShapeDtypeStruct((16, D), f32)],
        compiler_params=pltpu.CompilerParams(vmem_limit_bytes=VM),
        name="input_gradients",
    )(x, dq, dk, dv, dr, w, sums, sb1)


def gather(shard):
    return lax.all_gather(shard, AXES, axis=0, tiled=True)


def scatter(grad):
    return lax.psum_scatter(grad, AXES, scatter_dimension=0, tiled=True)


def local(where, rows, cotangent, page_rows, pos_bucket, x_bucket, y_bucket, wq, bq, wk, wv, bv, wo, bo,
          ln1_gain, ln1_bias, w1, b1, w2, b2, ln2_gain, ln2_bias, pos_table, x_table, y_table):
    length, width = rows.shape[1:]
    share = wq.shape[0]
    wide, narrow, span = where[:3]
    n = wide * narrow
    kin = KIN if share % 8 == 0 else 1
    w_rest = gather(pack_call(wo, w1, w2, n))
    bias, codes, w_all, small, b_up = front_call(
        where, pos_bucket[0], x_bucket[0], y_bucket[0], (pos_table.T, x_table.T, y_table.T), (wq, wk, wv),
        (bq, bv, bo, ln1_gain, ln1_bias, b2, ln2_gain, ln2_bias, b1),
    )
    w_qkv = w_all.reshape(width, 3 * width)
    query, keys, values, keys_t, values_t = qkv_call(rows[0], w_qkv, small)
    prob, attended, inverse = fwd_call(page_rows, query, keys, values_t, bias)
    out_rows, normed, act, d_ffn, d_pre, d_mixed, d_branch, d_attended, inner, sums, sum_up = row_call(
        page_rows, attended, rows[0], cotangent[0], w_rest, small, b_up
    )
    early, late = share_call(attended, normed, act, d_mixed, d_pre, d_ffn, kin)
    early, late, d_attended = lax.optimization_barrier((early, late, d_attended))
    late = scatter(late)
    early = early.reshape(n // (2 * span), 2, span, share, kin * width)
    dq, dk, dv, ds, early = bwd_call(where, query, d_attended, keys_t, values, prob, inverse, inner, early)
    grad_qkv, rows_grad, sums = input_call(rows[0], dq, dk, dv, d_branch, w_qkv, sums, sum_up)
    grad_qkv = grad_qkv.reshape(n // (2 * span), 2, span, share, 3 * width)
    tables, first, vec = tail_call(where, ds, codes, grad_qkv, sums)
    g_out, g_up, g_down, g_query, g_key, g_value, g_pos, g_x, g_y, own = finish_call(early, late, first, vec, tables, n, narrow)
    return (
        out_rows[None], rows_grad[None], g_query, own[0], g_key, g_value, own[1], g_out, own[2], own[3], own[4],
        g_up, own[8], g_down, own[5], own[6], own[7], g_pos, g_x, g_y,
    )


def solution(mesh):
    wide, narrow = mesh.shape["wide"], mesh.shape["narrow"]
    small = wide <= 8
    where = (wide, narrow, 1 if small else narrow, wide // 2 if small else 8, 4 if small else narrow)
    cut3 = P(AXES, None, None)
    cut2 = P(AXES, None)
    cut1 = P(AXES)
    params = (cut2, cut1, cut2, cut2, cut1, cut2, cut1, cut1, cut1, cut2, cut1, cut2, cut1, cut1, cut1)
    in_specs = (cut3, cut3, cut1, cut3, cut3, cut3) + params + (P(), P(), P())
    out_specs = (cut3, cut3) + params + (P(), P(), P())
    return jax.shard_map(lambda *a: local(where, *a), mesh=mesh, in_specs=in_specs, out_specs=out_specs, check_vma=False)
```

```python
import jax
import jax.numpy as jnp
from jax import lax
from jax.experimental import pallas as pl
from jax.experimental.pallas import tpu as pltpu
from jax.sharding import PartitionSpec as P

bf = jnp.bfloat16
f32 = jnp.float32
NT = (((1,), (1,)), ((), ()))
NN = (((1,), (0,)), ((), ()))
TN = (((0,), (0,)), ((), ()))
AXES = ("wide", "narrow")
MESH = pl.DeviceIdType.MESH
BQ = 128
VM = 60 << 20
TABLE_SCALE = 3500.0
EPS = 1e-05
KIN = 3
SHORTEST = 709


class Place:
    def __init__(self, wide, narrow, span, depth, low):
        self.n = wide * narrow
        self.half = self.n // 2
        self.narrow = narrow
        self.span = span
        self.depth = depth
        self.low = low
        self.plane = self.half // depth
        self.flat = lax.axis_index("wide") * narrow + lax.axis_index("narrow")
        self.par = lax.rem(lax.div(self.flat, span), 2)
        self.group = lax.div(self.flat, 2 * span) * span + lax.rem(self.flat, span)
        self.q, self.z = self.split(self.group)

    def split(self, group):
        q = lax.div(group, self.depth * self.low) * self.low + lax.rem(group, self.low)
        return q, lax.rem(lax.div(group, self.low), self.depth)

    def join(self, q, z):
        return (lax.div(q, self.low) * self.depth + z) * self.low + lax.rem(q, self.low)

    def flat_of(self, group, par):
        return (lax.div(group, self.span) * 2 + par) * self.span + lax.rem(group, self.span)

    def device(self, flat):
        return (lax.div(flat, self.narrow), lax.rem(flat, self.narrow))

    def partner(self):
        return self.device(self.flat_of(self.group, 1 - self.par))

    def peer(self, k):
        return lax.rem(self.group + k, self.half)

    def peer_device(self, k):
        return self.device(self.flat_of(self.peer(k), self.par))

    def column(self, k):
        z = lax.rem(self.z + k, self.depth)
        return z, self.device(self.flat_of(self.join(self.q, z), self.par))

    def across(self, k):
        q = lax.rem(self.q + k, self.plane)
        return q, self.device(self.flat_of(self.join(q, self.z), self.par))

    def greet(self):
        barrier = pltpu.get_barrier_semaphore()
        pl.semaphore_signal(barrier, inc=1, device_id=self.partner(), device_id_type=MESH)

        def one(k, c):
            pl.semaphore_signal(barrier, inc=1, device_id=self.peer_device(k), device_id_type=MESH)
            return c

        lax.fori_loop(1, self.half, one, 0)
        pl.semaphore_wait(barrier, self.half)


def loop(first, last, body):
    def one(k, c):
        body(k)
        return c

    lax.fori_loop(first, last, one, 0)


class Scatter:
    shapes = staticmethod(
        lambda half, depth, block, kind: [
            pltpu.VMEM((half // depth, depth) + block, kind),
            pltpu.VMEM((half // depth, depth) + block, kind),
            pltpu.VMEM((half // depth, depth) + block, kind),
            pltpu.VMEM((depth,) + block, kind),
            pltpu.SemaphoreType.DMA((7,)),
        ]
    )

    def __init__(self, me, src, mine, came, plane, column, sem):
        self.me, self.src, self.mine, self.came, self.plane, self.column, self.sem = me, src, mine, came, plane, column, sem

    def begin(self):
        me, sem = self.me, self.sem

        def one(g):
            q, z = me.split(g)
            a, b = lax.div(g, me.span), lax.rem(g, me.span)
            send(self.src.at[a, 1 - me.par, b], self.came.at[q, z], sem.at[1], sem.at[2], me.partner())
            pltpu.make_async_copy(self.src.at[a, me.par, b], self.mine.at[q, z], sem.at[0]).start()

        loop(0, me.half, one)

    def to_plane(self):
        me, sem = self.me, self.sem
        drain(self.mine, sem.at[0])
        drain(self.came, sem.at[1])
        drain(self.came, sem.at[2])

        def add(g):
            q, z = me.split(g)
            self.mine[q, z] = (self.mine[q, z].astype(f32) + self.came[q, z].astype(f32)).astype(bf)

        loop(0, me.half, add)

        def one(k):
            q, device = me.across(k)
            send(self.mine.at[q], self.plane.at[me.q], sem.at[3], sem.at[4], device)

        loop(1, me.plane, one)

    def to_column(self):
        me, sem = self.me, self.sem
        others = pl.ds(0, me.plane - 1)
        drain(self.plane.at[others], sem.at[3])
        drain(self.plane.at[others], sem.at[4])

        def add(z):
            total = self.mine[me.q, z].astype(f32)
            for k in range(1, me.plane):
                total = total + self.plane[me.across(k)[0], z].astype(f32)
            self.mine[me.q, z] = total.astype(bf)

        loop(0, me.depth, add)

        def one(k):
            z, device = me.column(k)
            send(self.mine.at[me.q, z], self.column.at[me.z], sem.at[5], sem.at[6], device)

        loop(1, me.depth, one)

    def end(self, out):
        me, sem = self.me, self.sem
        others = pl.ds(0, me.depth - 1)
        drain(self.column.at[others], sem.at[5])
        drain(self.column.at[others], sem.at[6])
        total = self.mine[me.q, me.z].astype(f32)
        for k in range(1, me.depth):
            total = total + self.column[me.column(k)[0]].astype(f32)
        out[...] = total


def send(src, dst, send_sem, recv_sem, device):
    pltpu.make_async_remote_copy(src, dst, send_sem, recv_sem, device_id=device, device_id_type=MESH).start()


def drain(ref, sem):
    pltpu.make_async_copy(ref, ref, sem).wait()


def take(t, i):
    return jnp.take_along_axis(t, i, axis=1, mode="promise_in_bounds")


def front_kernel(where, pos_ref, x_ref, y_ref, pt_ref, xt_ref, yt_ref, wq_ref, wk_ref, wv_ref, *rest):
    vec_refs = rest[:9]
    out_ref, idx_ref, w_all, small_ref, up_ref, v_all, wpack, vpack, tab, lsem, ssem, rsem, xssem, xrsem = rest[9:]
    S = out_ref.shape[1]
    pid = pl.program_id(0)
    me = Place(*where)
    width = wq_ref.shape[1]

    @pl.when(pid == 0)
    def _():
        for n, ref in enumerate((wq_ref, wk_ref, wv_ref)):
            wpack[:, n * width : (n + 1) * width] = ref[...].astype(bf)
        vpack[...] = jnp.zeros_like(vpack)
        for n, ref in enumerate(vec_refs):
            vpack[n : n + 1, : ref.shape[1]] = ref[...].astype(bf)
        me.greet()
        pltpu.make_async_copy(wpack, w_all.at[me.flat], lsem.at[0]).start()
        pltpu.make_async_copy(vpack, v_all.at[me.flat], lsem.at[1]).start()
        send(vpack, v_all.at[me.flat], xssem.at[1], xrsem.at[1], me.partner())
        send(wpack, w_all.at[me.flat], xssem.at[0], xrsem.at[0], me.partner())

        def one(k):
            device = me.column(k)[1]
            send(vpack, v_all.at[me.flat], ssem.at[1], rsem.at[1], device)
            send(wpack, w_all.at[me.flat], ssem.at[0], rsem.at[0], device)

        loop(1, me.depth, one)
        tab[...] = jnp.zeros_like(tab)

        def pack(ref, row, lane):
            fixed = jnp.floor(ref[...].astype(bf).astype(f32) * TABLE_SCALE + 0.5).astype(jnp.int32)
            n = fixed.shape[1]
            for p in range(6):
                tab[row, p : p + 1, lane : lane + n] = fixed[2 * p : 2 * p + 1] * 65536 + fixed[2 * p + 1 : 2 * p + 2]

        pack(pt_ref, 0, 0)
        pack(xt_ref, 1, 0)
        pack(yt_ref, 1, 64)

    @pl.when(pid == 2)
    def _():
        others = pl.ds(0, me.depth - 1)
        drain(v_all.at[others], rsem.at[1])
        drain(w_all.at[others], rsem.at[0])
        pltpu.make_async_copy(wpack, w_all.at[me.flat], lsem.at[0]).wait()
        pltpu.make_async_copy(vpack, v_all.at[me.flat], lsem.at[1]).wait()

        def one(k):
            device = me.across(k)[1]

            def block(z):
                at = me.flat_of(me.join(me.q, z), me.par)
                send(v_all.at[at], v_all.at[at], ssem.at[3], rsem.at[3], device)
                send(w_all.at[at], w_all.at[at], ssem.at[2], rsem.at[2], device)

            loop(0, me.depth, block)

        loop(1, me.plane, one)

    @pl.when(pid == pl.num_programs(0) - 1)
    def _():
        others = pl.ds(0, (me.plane - 1) * me.depth)
        drain(v_all.at[others], rsem.at[3])
        drain(w_all.at[others], rsem.at[2])

        def one(k):
            at = me.flat_of(me.peer(k), me.par)
            send(v_all.at[at], v_all.at[at], xssem.at[1], xrsem.at[1], me.partner())
            send(w_all.at[at], w_all.at[at], xssem.at[0], xrsem.at[0], me.partner())

        loop(1, me.half, one)

    packed = pos_ref[...] | (x_ref[...] << 5) | (y_ref[...] << 11)
    idx_ref[...] = packed.T
    tp = [jnp.broadcast_to(tab[0, p : p + 1, :], (8, 128)) for p in range(6)]
    tx = [jnp.broadcast_to(tab[1, p : p + 1, :], (8, 128)) for p in range(6)]

    def body(r, c):
        for u in range(48):
            sl = pl.ds(pl.multiple_of((r * 48 + u) * 8, 8), 8)
            t = idx_ref[sl, :]
            p = t & 31
            x = (t >> 5) & 63
            y = (t >> 11) + 64
            g = [take(a, p) for a in tp]
            g = [a + take(b, x) for a, b in zip(g, tx)]
            g = [a + take(b, y) for a, b in zip(g, tx)]
            for k in range(6):
                out_ref[k, sl, :] = g[k]
        return c

    lax.fori_loop(0, S // (48 * 8), body, 0)

    @pl.when(pid == pl.num_programs(0) - 1)
    def _():
        mine = pl.ds(0, me.half)
        near, far = pl.ds(0, me.depth - 1), pl.ds(0, (me.plane - 1) * me.depth)
        drain(w_all.at[near], ssem.at[0])
        drain(v_all.at[near], ssem.at[1])
        drain(w_all.at[far], ssem.at[2])
        drain(v_all.at[far], ssem.at[3])
        for sem in (xssem, xrsem):
            drain(w_all.at[mine], sem.at[0])
            drain(v_all.at[mine], sem.at[1])
        share = wpack.shape[0]
        for d in range(me.n):
            block = v_all[d].astype(f32)
            at = pl.ds(d * share, share)
            small_ref[:, at] = block[0:8, :share]
            for m in range(4):
                up_ref[m : m + 1, at] = block[8:9, m * share : (m + 1) * share]


def front_call(where, pos, x, y, tables, weights, vectors):
    S = pos.shape[0]
    share, width = weights[0].shape
    n = where[0] * where[1]

    def whole(a):
        return pl.BlockSpec(a.shape, lambda i: (0,) * a.ndim)

    small = tuple(tables) + tuple(weights) + tuple(v.reshape(1, -1) for v in vectors)
    return pl.pallas_call(
        lambda *a: front_kernel(where, *a),
        grid=(S // BQ,),
        in_specs=[pl.BlockSpec((BQ, S), lambda i: (i, 0))] * 3 + [whole(a) for a in small],
        out_specs=[
            pl.BlockSpec((6, S, BQ), lambda i: (0, 0, i)),
            pl.BlockSpec((S, BQ), lambda i: (0, i)),
            pl.BlockSpec(memory_space=pl.ANY),
            pl.BlockSpec((8, width), lambda i: (0, 0)),
            pl.BlockSpec((4, width), lambda i: (0, 0)),
        ],
        out_shape=[
            jax.ShapeDtypeStruct((6, S, S), jnp.int32),
            jax.ShapeDtypeStruct((S, S), jnp.int32),
            jax.ShapeDtypeStruct((n, share, 3 * width), bf),
            jax.ShapeDtypeStruct((8, width), f32),
            jax.ShapeDtypeStruct((4, width), f32),
        ],
        scratch_shapes=[
            pltpu.VMEM((n, 16, 128), bf),
            pltpu.VMEM((share, 3 * width), bf),
            pltpu.VMEM((16, 128), bf),
            pltpu.VMEM((2, 8, 128), jnp.int32),
        ]
        + [pltpu.SemaphoreType.DMA((4,))] * 5,
        compiler_params=pltpu.CompilerParams(vmem_limit_bytes=VM, collective_id=0, has_side_effects=True),
        name="bias_and_gather",
    )(pos, x, y, *small)


def pack_call(wo, w1, w2, n):
    share, wide = w1.shape
    width = wide // 4
    pieces = share % 8 == 0
    if not pieces:
        w1 = jnp.transpose(w1.reshape(share, n, 4, share), (0, 2, 1, 3)).reshape(share, 4 * width)

    def kernel(wo_ref, w1_ref, w2_ref, a_ref, scr):
        a_ref[:, 8 * width :] = wo_ref[...].astype(bf)
        if pieces:
            for d in range(n):
                for m in range(4):
                    at = m * width + d * share
                    scr[:, at : at + share] = w1_ref[:, (4 * d + m) * share : (4 * d + m + 1) * share]
            a_ref[:, : 4 * width] = scr[...].astype(bf)
        else:
            a_ref[:, : 4 * width] = w1_ref[...].astype(bf)
        for m in range(4):
            a_ref[:, (4 + m) * width : (5 + m) * width] = w2_ref[m * share : (m + 1) * share, :].astype(bf)

    return pl.pallas_call(
        kernel,
        out_shape=jax.ShapeDtypeStruct((share, 9 * width), bf),
        scratch_shapes=[pltpu.VMEM((share, 4 * width), f32)],
        name="round_shares",
    )(wo, w1, w2)


def finish_call(early, late, first, vec, tables, n, narrow):
    share, width = first.shape[0], vec.shape[1]
    pieces = share % 8 == 0
    kin = early.shape[1] // width

    def kernel(e_ref, s_ref, f_ref, v_ref, t_ref, wo_ref, w1_ref, w2_ref, wq_ref, wk_ref, wv_ref, gp_ref, gx_ref, gy_ref, *rest):
        vec_refs, scr = rest[:9], rest[9]
        flat = lax.axis_index("wide") * narrow + lax.axis_index("narrow")

        def part(k):
            if k < kin:
                return e_ref[:, k * width : (k + 1) * width]
            return s_ref[:, (k - kin) * width : (k - kin + 1) * width].astype(f32)

        for k, ref in enumerate((wq_ref, wk_ref, wv_ref)):
            ref[...] = f_ref[:, k * width : (k + 1) * width]
        gx_ref[...] = t_ref[0:12, 0:64]
        gy_ref[...] = t_ref[0:12, 64:128]
        gp_ref[...] = t_ref[0:12, 128:160]
        wo_ref[...] = part(0)
        for m in range(4):
            scr[:, m * width : (m + 1) * width] = part(1 + m)
            w2_ref[m * share : (m + 1) * share, :] = part(5 + m)
        if pieces:
            for d in range(n):
                for m in range(4):
                    at = m * width + d * share
                    w1_ref[:, (4 * d + m) * share : (4 * d + m + 1) * share] = scr[:, at : at + share]
        else:
            w1_ref[...] = scr[...]
        own = jnp.zeros((16, share), f32)
        for d in range(n):
            own = jnp.where(flat == d, v_ref[:, d * share : (d + 1) * share], own)
        for k in range(8):
            vec_refs[k][...] = own[k : k + 1, :]
        for m in range(4):
            vec_refs[8][:, m * share : (m + 1) * share] = own[8 + m : 9 + m, :]

    outs = [(share, width), (share, 4 * width), (4 * share, width)] + [(share, width)] * 3 + [(12, 32), (12, 64), (12, 64)]
    outs += [(1, share)] * 8 + [(1, 4 * share)]
    outs = pl.pallas_call(
        kernel,
        out_shape=[jax.ShapeDtypeStruct(s, f32) for s in outs],
        scratch_shapes=[pltpu.VMEM((share, 4 * width), f32)],
        name="own_shares",
    )(early, late, first, vec, tables)
    g_up = outs[1]
    if not pieces:
        g_up = jnp.transpose(g_up.reshape(share, 4, n, share), (0, 2, 1, 3)).reshape(share, 4 * width)
    return [outs[0], g_up, outs[2], *outs[3:6], *[t.T for t in outs[6:9]], [v.reshape(-1) for v in outs[9:]]]


def stack2(a):
    lane=lax.broadcasted_iota(jnp.int32,a.shape,1)
    z=jnp.zeros_like(a)
    return jnp.concatenate([jnp.where(lane<64,a,z),jnp.where(lane<64,z,a)],axis=0)

def fwd_kernel(live_ref, q_ref, k_ref, vt_ref, b_ref, e_ref, o_ref, l_ref, s_scr, *, CH):
    S = k_ref.shape[0]
    live = live_ref[0]
    c = 1.0 / (TABLE_SCALE * 65536.0)
    chunks = range(S // CH)
    rows = lax.broadcasted_iota(jnp.int32, (CH, 1), 0)
    sub = lax.broadcasted_iota(jnp.int32, (128, 128), 0)

    def scores(p, qs, top, ch):
        r = pl.ds(ch * CH, CH)
        s = lax.dot_general(k_ref[r, pl.ds(p * 128, 128)], qs, NT, preferred_element_type=f32)
        b = b_ref[p, r, :]
        s = s + jnp.concatenate([b.astype(f32) * c, (b << 16).astype(f32) * c], axis=1)
        if (ch + 1) * CH > SHORTEST:
            s = jnp.where(rows + ch * CH < live, s, -1e9)
        s_scr[p % 2, r, :] = s
        return jnp.maximum(top, jnp.max(s.reshape(CH // 8, 8, 256), axis=0))

    low = jnp.full((8, 256), -3e38, f32)
    top = low
    qs = stack2(q_ref[:, pl.ds(0, 128)])
    for ch in chunks:
        top = scores(0, qs, top, ch)
    for p in range(6):
        ln = pl.ds(p * 128, 128)
        peak = jnp.max(top, axis=0, keepdims=True)
        top = low
        total = jnp.zeros((8, 256), f32)
        if p < 5:
            qs = stack2(q_ref[:, pl.ds((p + 1) * 128, 128)])
        for ch in chunks:
            if p < 5:
                top = scores(p + 1, qs, top, ch)
            r = pl.ds(ch * CH, CH)
            e = jnp.exp(s_scr[p % 2, r, :] - peak)
            total = total + jnp.sum(e.reshape(CH // 8, 8, 256), axis=0)
            eb = e.astype(bf)
            e_ref[2 * p, r, :] = eb[:, :128]
            e_ref[2 * p + 1, r, :] = eb[:, 128:]
        linv = 1.0 / jnp.sum(total, axis=0, keepdims=True)
        l_ref[2 * p : 2 * p + 1, :] = linv[:, :128]
        l_ref[2 * p + 1 : 2 * p + 2, :] = linv[:, 128:]
        both = jnp.concatenate([e_ref[2 * p], e_ref[2 * p + 1]], axis=1)
        acc = lax.dot_general(vt_ref[ln, :], both, NN, preferred_element_type=f32) * linv
        o_ref[:, ln] = jnp.where(sub < 64, acc[:, :128], acc[:, 128:]).T.astype(bf)


def fwd_call(live, q, k, vt, b, CH=128):
    S, D = k.shape
    return pl.pallas_call(
        lambda *a: fwd_kernel(*a, CH=CH),
        grid_spec=pltpu.PrefetchScalarGridSpec(
            num_scalar_prefetch=1,
            grid=(S // BQ,),
            in_specs=[
                pl.BlockSpec((BQ, D), lambda i, *_: (i, 0)),
                pl.BlockSpec((S, D), lambda i, *_: (0, 0)),
                pl.BlockSpec((D, S), lambda i, *_: (0, 0)),
                pl.BlockSpec((6, S, BQ), lambda i, *_: (0, 0, i)),
            ],
            out_specs=[
                pl.BlockSpec((12, S, BQ), lambda i, *_: (0, 0, i)),
                pl.BlockSpec((BQ, D), lambda i, *_: (i, 0)),
                pl.BlockSpec((16, BQ), lambda i, *_: (0, i)),
            ],
            scratch_shapes=[pltpu.VMEM((2, S, 256), f32)],
        ),
        out_shape=[
            jax.ShapeDtypeStruct((12, S, S), bf),
            jax.ShapeDtypeStruct((S, D), bf),
            jax.ShapeDtypeStruct((16, S), f32),
        ],
        compiler_params=pltpu.CompilerParams(vmem_limit_bytes=VM),
        name="attention_forward",
    )(live, q, k, vt, b)


def bwd_kernel(where, q_ref, do_ref, kt_ref, v_ref, e_ref, l_ref, d_ref, g_ref, dq_ref, dk_ref, dv_ref, ds_ref, out_ref, ds_scr, dk_acc, dv_acc, *rest):
    S = v_ref.shape[0]
    pid = pl.program_id(0)
    me = Place(*where)
    travel = Scatter(me, g_ref, *rest)

    @pl.when(pid == 0)
    def _():
        me.greet()
        travel.begin()

    @pl.when(pid == 1)
    def _():
        travel.to_plane()

    @pl.when(pid == 6)
    def _():
        travel.to_column()

    @pl.when(pid == 0)
    def _():
        dk_acc[...] = jnp.zeros_like(dk_acc)
        dv_acc[...] = jnp.zeros_like(dv_acc)

    lane = lax.broadcasted_iota(jnp.int32, (BQ, 128), 1)
    sub = lax.broadcasted_iota(jnp.int32, (128, 128), 0)
    for p in range(6):
        ln = pl.ds(p * 128, 128)
        qs = stack2(q_ref[:, ln])
        l2 = l_ref[2 * p : 2 * p + 2, :]
        d2 = d_ref[2 * p : 2 * p + 2, :] * l2
        lcol = jnp.concatenate([l2] * 4, axis=0).T
        dos = stack2((do_ref[:, ln].astype(f32) * jnp.where(lane < 64, lcol[:, 0:1], lcol[:, 1:2])).astype(bf))
        dp = lax.dot_general(v_ref[:, ln], dos, NT, preferred_element_type=f32)
        e0 = e_ref[2 * p]
        e1 = e_ref[2 * p + 1]
        s0 = e0.astype(f32) * (dp[:, :128] - d2[0:1, :])
        s1 = e1.astype(f32) * (dp[:, 128:] - d2[1:2, :])
        ds_scr[pl.ds(2 * p, S, stride=16), :] = s0
        ds_scr[pl.ds(2 * p + 1, S, stride=16), :] = s1
        both = jnp.concatenate([s0.astype(bf), s1.astype(bf)], axis=1)
        dk_acc[:, ln] += lax.dot_general(both, qs, NN, preferred_element_type=f32)
        dv_acc[:, ln] += lax.dot_general(jnp.concatenate([e0, e1], axis=1), dos, NN, preferred_element_type=f32)
        a = lax.dot_general(kt_ref[ln, :], both, NN, preferred_element_type=f32)
        dq_ref[:, ln] = (jnp.where(sub < 64, a[:, :128], a[:, 128:]).T * 0.125).astype(bf)
    ds_ref[...] = ds_scr[...].astype(bf)

    @pl.when(pid == pl.num_programs(0) - 1)
    def _():
        dk_ref[...] = dk_acc[...].astype(bf)
        dv_ref[...] = dv_acc[...].astype(bf)
        travel.end(out_ref)


def bwd_call(where, q, do, kt, v, e, linv, dd, g):
    S, D = v.shape
    half = where[0] * where[1] // 2
    block = g.shape[3:]
    fixed = pl.Buffered(1)
    full = pl.BlockSpec((S, D), lambda i: (0, 0))
    blk = pl.BlockSpec((BQ, D), lambda i: (i, 0))
    row = pl.BlockSpec((16, BQ), lambda i: (0, i))
    return pl.pallas_call(
        lambda *a: bwd_kernel(where, *a),
        grid=(S // BQ,),
        in_specs=[
            blk,
            blk,
            pl.BlockSpec((D, S), lambda i: (0, 0), pipeline_mode=fixed),
            pl.BlockSpec((S, D), lambda i: (0, 0), pipeline_mode=fixed),
            pl.BlockSpec((12, S, BQ), lambda i: (0, 0, i)),
            row,
            row,
            pl.BlockSpec(memory_space=pl.ANY),
        ],
        out_specs=[blk, full, full, pl.BlockSpec((S * 16, BQ), lambda i: (0, i)), pl.BlockSpec(block, lambda i: (0, 0))],
        scratch_shapes=[pltpu.VMEM((S * 16, BQ), f32), pltpu.VMEM((S, D), f32), pltpu.VMEM((S, D), f32)]
        + Scatter.shapes(half, where[3], block, bf),
        out_shape=[jax.ShapeDtypeStruct((S, D), bf)] * 3 + [jax.ShapeDtypeStruct((S * 16, S), bf), jax.ShapeDtypeStruct(block, f32)],
        compiler_params=pltpu.CompilerParams(vmem_limit_bytes=VM, collective_id=2, has_side_effects=True),
        name="attention_backward_and_scatter",
    )(q, do, kt, v, e, linv, dd, g)


def tail_kernel(where, U, ds_ref, idx_ref, gw_ref, gv_ref, t_ref, w_out, v_out, *rest):
    acc, xi_scr, v_in, v_mine, v_near, v_far, h_mine, h_in, h_near, h_far, xssem, xrsem, ssem, rsem = rest[:14]
    S = idx_ref.shape[0]
    pid = pl.program_id(0)
    me = Place(*where)
    travel = Scatter(me, gw_ref, *rest[14:])
    near, far = pl.ds(0, me.plane - 1), pl.ds(0, me.depth - 1)

    @pl.when(pid == 0)
    def _():
        acc[...] = jnp.zeros_like(acc)
        me.greet()
        send(gv_ref, v_in, xssem.at[1], xrsem.at[1], me.partner())
        travel.begin()

    @pl.when(pid == 1)
    def _():
        drain(v_in, xssem.at[1])
        drain(v_in, xrsem.at[1])
        v_mine[0] = gv_ref[...] + v_in[...]

        def one(k):
            send(v_mine.at[0], v_near.at[me.q], ssem.at[0], rsem.at[0], me.across(k)[1])

        loop(1, me.plane, one)
        travel.to_plane()

    @pl.when(pid == 5)
    def _():
        drain(v_near.at[near], ssem.at[0])
        drain(v_near.at[near], rsem.at[0])
        v_mine[1] = lax.fori_loop(1, me.plane, lambda k, t: t + v_near[me.across(k)[0]], v_mine[0])

        def one(k):
            send(v_mine.at[1], v_far.at[me.z], ssem.at[1], rsem.at[1], me.column(k)[1])

        loop(1, me.depth, one)
        travel.to_column()

    t = idx_ref[...]
    xi_scr[0] = (t & 31).astype(f32)
    xi_scr[1] = ((t >> 5) & 63).astype(f32)
    xi_scr[2] = (t >> 11).astype(f32)
    iot = lax.broadcasted_iota(jnp.int32, (16, 128), 0).astype(f32).astype(bf)
    one = jnp.ones((16, 128), bf)
    zero = jnp.zeros((16, 128), bf)

    def one_j(j):
        bp, bx, by = [jnp.broadcast_to(xi_scr[n, pl.ds(j, 1), :], (16, 128)).astype(bf) for n in range(3)]
        d = ds_ref[pl.ds(pl.multiple_of(j * 16, 16), 16), :]
        xh = bx >= 32
        yh = by >= 32
        bxl = jnp.where(xh, bx - 32, bx)
        byl = jnp.where(yh, by - 32, by)
        ph = bp >= 16
        bpl = jnp.where(ph, bp - 16, bp)
        rows = [jnp.where(b == iot + bf(16 * k), one, zero) for b in (bxl, byl) for k in range(2)]
        rows.append(jnp.where(bpl == iot, one, zero))
        rhs = [d, jnp.where(xh, d, zero), jnp.where(yh, d, zero), jnp.where(ph, d, zero)]
        return jnp.concatenate(rows, 0), jnp.concatenate(rhs, 0)

    def body(t, total):
        for u in range(U):
            l0, r0 = one_j(t * 2 * U + 2 * u)
            l1, r1 = one_j(t * 2 * U + 2 * u + 1)
            total = total + lax.dot_general(
                jnp.concatenate([l0, l1], 1), jnp.concatenate([r0, r1], 1), NT, preferred_element_type=f32
            )
        return total

    acc[:, :64] += lax.fori_loop(0, S // (2 * U), body, jnp.zeros((80, 64), f32))

    @pl.when(pid == pl.num_programs(0) - 1)
    def _():
        h = acc[...].T
        total, x1, y1, p1 = h[0:16], h[16:32, 0:32], h[32:48, 32:64], h[48:64, 64:80]
        parts = [total[:, 0:32] - x1, x1, total[:, 32:64] - y1, y1, total[:, 64:80] - p1, p1, jnp.zeros((16, 96), f32)]
        h = jnp.concatenate(parts, axis=1)
        h_mine[...] = jnp.where(lax.broadcasted_iota(jnp.int32, h.shape, 0) < 12, h, 0.0)
        send(h_mine, h_in, xssem.at[2], xrsem.at[2], me.partner())
        drain(v_far.at[far], ssem.at[1])
        drain(v_far.at[far], rsem.at[1])
        v_out[...] = lax.fori_loop(1, me.depth, lambda k, t: t + v_far[me.column(k)[0]], v_mine[1])
        travel.end(w_out)
        drain(h_in, xssem.at[2])
        drain(h_in, xrsem.at[2])
        h_mine[...] = h_mine[...] + h_in[...]

        def across(k):
            send(h_mine, h_near.at[me.q], ssem.at[2], rsem.at[2], me.across(k)[1])

        loop(1, me.plane, across)
        drain(h_near.at[near], ssem.at[2])
        drain(h_near.at[near], rsem.at[2])
        h_in[...] = lax.fori_loop(1, me.plane, lambda k, t: t + h_near[me.across(k)[0]], h_mine[...])

        def along(k):
            send(h_in, h_far.at[me.z], ssem.at[3], rsem.at[3], me.column(k)[1])

        loop(1, me.depth, along)
        drain(h_far.at[far], ssem.at[3])
        drain(h_far.at[far], rsem.at[3])
        t_ref[...] = lax.fori_loop(1, me.depth, lambda k, t: t + h_far[me.column(k)[0]], h_in[...])


def tail_call(where, ds, codes, gw, gv, U=144):
    S = codes.shape[0]
    half, depth = where[0] * where[1] // 2, where[3]
    share, cols = gw.shape[3:]

    def whole(shape):
        return pl.BlockSpec(shape, lambda i: (0,) * len(shape))

    outs = [(16, 256), (share, cols), gv.shape]
    return pl.pallas_call(
        lambda *a: tail_kernel(where, U, *a),
        grid=(S // BQ,),
        in_specs=[
            pl.BlockSpec((S * 16, BQ), lambda i: (0, i)),
            pl.BlockSpec((S, BQ), lambda i: (0, i)),
            pl.BlockSpec(memory_space=pl.ANY),
            whole(gv.shape),
        ],
        out_specs=[whole(s) for s in outs],
        out_shape=[jax.ShapeDtypeStruct(s, f32) for s in outs],
        scratch_shapes=[
            pltpu.VMEM((80, 128), f32),
            pltpu.VMEM((3, S, BQ), f32),
            pltpu.VMEM(gv.shape, f32),
            pltpu.VMEM((2,) + gv.shape, f32),
            pltpu.VMEM((half // depth,) + gv.shape, f32),
            pltpu.VMEM((depth,) + gv.shape, f32),
            pltpu.VMEM((16, 256), f32),
            pltpu.VMEM((16, 256), f32),
            pltpu.VMEM((half // depth, 16, 256), f32),
            pltpu.VMEM((depth, 16, 256), f32),
        ]
        + [pltpu.SemaphoreType.DMA((4,))] * 4
        + Scatter.shapes(half, depth, (share, cols), bf),
        compiler_params=pltpu.CompilerParams(vmem_limit_bytes=VM, collective_id=1, has_side_effects=True),
        name="table_sums_and_scatter",
    )(ds, codes, gw, gv)


GELU_COEFS = (0.254829592, -0.284496736, 1.421413741, -1.453152027, 1.061405429)


def gelu_both(z):
    t = pltpu.reciprocal(1.0 + (0.3275911 * 0.7071067811865476) * jnp.abs(z), approx=False)
    q = jnp.exp(z * z * -0.5)
    poly = 0.5 * GELU_COEFS[4] * t + 0.5 * GELU_COEFS[3]
    for c in GELU_COEFS[2::-1]:
        poly = poly * t + 0.5 * c
    half = poly * t * q
    cdf = jnp.where(z >= 0, 1.0 - half, half)
    return z * cdf, cdf + z * (q * 0.3989422804014327)


def norm_stats(u):
    mean = jnp.mean(u, axis=-1, keepdims=True)
    center = u - mean
    inv = lax.rsqrt(jnp.mean(center * center, axis=-1, keepdims=True) + EPS)
    return center * inv, inv


def norm_pull(e, normed, inv):
    return (e - jnp.mean(e, axis=-1, keepdims=True) - normed * jnp.mean(e * normed, axis=-1, keepdims=True)) * inv


def fold8(u):
    return jnp.sum(u.reshape(u.shape[0] // 8, 8, u.shape[1]), axis=0)


def row_kernel(live_ref, at_ref, x_ref, ct_ref, w_ref, v_ref, b1_ref,
               out_ref, h_ref, g_ref, df_ref, dz_ref, da_ref, dr_ref, dat_ref, dd_ref, sum_ref, sb1_ref,
               gp_scr, z_scr, acc, h_scr, n1_scr, i1_scr, *, R, SL):
    pid = pl.program_id(0)
    D = x_ref.shape[1]
    live = live_ref[0]
    b_out, g1, s1, b_down, g2, s2 = [v_ref[n : n + 1, :] for n in range(2, 8)]

    @pl.when(pid == 0)
    def _():
        sum_ref[...] = jnp.zeros_like(sum_ref)
        sb1_ref[...] = jnp.zeros_like(sb1_ref)

    def add(row, part):
        sum_ref[row : row + 1, :] += jnp.sum(part, axis=0, keepdims=True)

    acc[...] = lax.dot_general(at_ref[...], w_ref[:, 8 * D :], NN, preferred_element_type=f32)
    for r in range(0, R, SL):
        sl = pl.ds(r, SL)
        n1, inv = norm_stats(x_ref[sl, :].astype(f32) + acc[sl, :] + b_out)
        n1_scr[sl, :] = n1
        i1_scr[sl, :] = jnp.broadcast_to(inv, (SL, 128))
        h1 = n1 * g1 + s1
        h_scr[sl, :] = h1
        h_ref[sl, :] = h1.astype(bf)
    for c in range(4):
        cols = pl.ds(c * D, D)
        z_scr[c % 2] = lax.dot_general(h_ref[...], w_ref[:, pl.ds(c * D, D)], NN, preferred_element_type=f32)
        for r in range(0, R, SL):
            sl = pl.ds(r, SL)
            g, gp = gelu_both(z_scr[c % 2, sl, :] + b1_ref[c : c + 1, :])
            g_ref[sl, cols] = g.astype(bf)
            gp_scr[sl, cols] = gp
        part = lax.dot_general(g_ref[:, cols], w_ref[:, pl.ds((4 + c) * D, D)], NN, preferred_element_type=f32)
        if c == 0:
            acc[...] = part
        else:
            acc[...] += part
    p_gain = p_shift = p_down = jnp.zeros((8, D), f32)
    rows = lax.broadcasted_iota(jnp.int32, (SL, 1), 0) + pid * R
    for r in range(0, R, SL):
        sl = pl.ds(r, SL)
        n2, inv = norm_stats(h_scr[sl, :] + acc[sl, :] + b_down)
        out_ref[sl, :] = (n2 * g2 + s2).astype(bf)
        dy = jnp.where(rows + r < live, ct_ref[sl, :].astype(f32), 0.0)
        dr2 = norm_pull(dy * g2, n2, inv)
        df = dr2.astype(bf)
        df_ref[sl, :] = df
        h_scr[sl, :] = dr2
        p_gain = p_gain + fold8(dy * n2)
        p_shift = p_shift + fold8(dy)
        p_down = p_down + fold8(df.astype(f32))
    add(5, p_down)
    add(6, p_gain)
    add(7, p_shift)
    for c in range(4):
        cols = pl.ds(c * D, D)
        z_scr[c % 2] = lax.dot_general(df_ref[...], w_ref[:, pl.ds((4 + c) * D, D)], NT, preferred_element_type=f32)
        p_up = jnp.zeros((8, D), f32)
        for r in range(0, R, SL):
            sl = pl.ds(r, SL)
            dz = (z_scr[c % 2, sl, :] * gp_scr[sl, cols]).astype(bf)
            dz_ref[sl, cols] = dz
            p_up = p_up + fold8(dz.astype(f32))
        sb1_ref[c : c + 1, :] += jnp.sum(p_up, axis=0, keepdims=True)
        part = lax.dot_general(dz_ref[:, cols], w_ref[:, pl.ds(c * D, D)], NT, preferred_element_type=f32)
        if c == 0:
            acc[...] = part
        else:
            acc[...] += part
    p_gain = p_shift = p_out = jnp.zeros((8, D), f32)
    for r in range(0, R, SL):
        sl = pl.ds(r, SL)
        dh = h_scr[sl, :] + acc[sl, :]
        n1 = n1_scr[sl, :]
        dr1 = norm_pull(dh * g1, n1, i1_scr[sl, 0:1])
        da = dr1.astype(bf)
        dr_ref[sl, :] = dr1
        da_ref[sl, :] = da
        p_gain = p_gain + fold8(dh * n1)
        p_shift = p_shift + fold8(dh)
        p_out = p_out + fold8(da.astype(f32))
    add(2, p_out)
    add(3, p_gain)
    add(4, p_shift)
    dat_ref[...] = lax.dot_general(da_ref[...], w_ref[:, 8 * D :], NT, preferred_element_type=f32).astype(bf)
    seg = (lax.div(lax.broadcasted_iota(jnp.int32, (D, 128), 0), 64) == lax.broadcasted_iota(jnp.int32, (D, 128), 1)).astype(f32).astype(bf)
    for r in range(0, R, 128):
        sl = pl.ds(r, 128)
        prod = dat_ref[sl, :].astype(f32) * at_ref[sl, :].astype(f32)
        high = prod.astype(bf)
        low = (prod - high.astype(f32)).astype(bf)
        d = lax.dot_general(high, seg, NN, preferred_element_type=f32) + lax.dot_general(low, seg, NN, preferred_element_type=f32)
        dd_ref[:, sl] = d.T[0:16, :]


def row_call(live, attended, x, ct, w, v, b1, R=384, SL=16):
    S, D = x.shape
    blk = pl.BlockSpec((R, D), lambda i, *_: (i, 0))
    big = pl.BlockSpec((R, 4 * D), lambda i, *_: (i, 0))

    def whole(shape, **kw):
        return pl.BlockSpec(shape, lambda i, *_: (0,) * len(shape), **kw)

    shapes = [((S, D), bf), ((S, D), bf), ((S, 4 * D), bf), ((S, D), bf), ((S, 4 * D), bf), ((S, D), bf), ((S, D), f32), ((S, D), bf),
              ((16, S), f32), ((8, D), f32), ((4, D), f32)]
    return pl.pallas_call(
        lambda *a: row_kernel(*a, R=R, SL=SL),
        grid_spec=pltpu.PrefetchScalarGridSpec(
            num_scalar_prefetch=1,
            grid=(S // R,),
            in_specs=[blk, blk, blk, whole(w.shape, pipeline_mode=pl.Buffered(1)), whole(v.shape), whole(b1.shape)],
            out_specs=[blk, blk, big, blk, big, blk, blk, blk, pl.BlockSpec((16, R), lambda i, *_: (0, i)), whole((8, D)), whole((4, D))],
            scratch_shapes=[
                pltpu.VMEM((R, 4 * D), f32),
                pltpu.VMEM((2, R, D), f32),
                pltpu.VMEM((R, D), f32),
                pltpu.VMEM((R, D), f32),
                pltpu.VMEM((R, D), f32),
                pltpu.VMEM((R, 128), f32),
            ],
        ),
        out_shape=[jax.ShapeDtypeStruct(s, d) for s, d in shapes],
        compiler_params=pltpu.CompilerParams(vmem_limit_bytes=VM),
        name="rows_forward_backward",
    )(live, attended, x, ct, w, v, b1)


def share_kernel(kin, at_ref, h_ref, g_ref, da_ref, dz_ref, df_ref, early_ref, late_ref):
    c = pl.program_id(0)
    for first, last, a_ref, b_ref in ((0, 1, at_ref, da_ref), (1, 5, h_ref, dz_ref), (5, 9, g_ref, df_ref)):
        for low, high, out in ((first, min(last, kin), early_ref), (max(first, kin), last, late_ref)):
            if low < high:

                @pl.when((c >= low) & (c < high))
                def _(a_ref=a_ref, b_ref=b_ref, out=out):
                    out[...] = lax.dot_general(a_ref[...], b_ref[...], TN, preferred_element_type=f32).astype(bf)


def share_call(attended, h, g, da, dz, df, kin):
    S, D = h.shape

    def fixed():
        return pl.BlockSpec((S, D), lambda c: (0, 0), pipeline_mode=pl.Buffered(1))

    return pl.pallas_call(
        lambda *a: share_kernel(kin, *a),
        grid=(9,),
        in_specs=[
            fixed(),
            fixed(),
            pl.BlockSpec((S, D), lambda c: (0, jnp.clip(c - 5, 0, 3))),
            fixed(),
            pl.BlockSpec((S, D), lambda c: (0, jnp.clip(c - 1, 0, 3))),
            fixed(),
        ],
        out_specs=[
            pl.BlockSpec((D, D), lambda c: (0, jnp.minimum(c, kin - 1))),
            pl.BlockSpec((D, D), lambda c: (0, jnp.maximum(c - kin, 0))),
        ],
        out_shape=[jax.ShapeDtypeStruct((D, kin * D), bf), jax.ShapeDtypeStruct((D, (9 - kin) * D), bf)],
        compiler_params=pltpu.CompilerParams(vmem_limit_bytes=VM),
        name="weight_gradients",
    )(attended, h, g, da, dz, df)


def qkv_call(x, w, v, R=384):
    S, D = x.shape

    def kernel(x_ref, w_ref, v_ref, q_ref, k_ref, o_ref, kt_ref, ot_ref):
        x = x_ref[...]
        q_ref[...] = (lax.dot_general(x, w_ref[:, :D], NN, preferred_element_type=f32) + v_ref[0:1, :]).astype(bf) * bf(0.125)
        k_ref[...] = lax.dot_general(x, w_ref[:, D : 2 * D], NN, preferred_element_type=f32).astype(bf)
        o_ref[...] = (lax.dot_general(x, w_ref[:, 2 * D :], NN, preferred_element_type=f32) + v_ref[1:2, :]).astype(bf)
        kt_ref[...] = k_ref[...].T
        ot_ref[...] = o_ref[...].T

    blk = pl.BlockSpec((R, D), lambda i: (i, 0))
    turned = pl.BlockSpec((D, R), lambda i: (0, i))
    return pl.pallas_call(
        kernel,
        grid=(S // R,),
        in_specs=[blk, pl.BlockSpec((D, 3 * D), lambda i: (0, 0), pipeline_mode=pl.Buffered(1)), pl.BlockSpec(v.shape, lambda i: (0, 0))],
        out_specs=[blk] * 3 + [turned] * 2,
        out_shape=[jax.ShapeDtypeStruct((S, D), bf)] * 3 + [jax.ShapeDtypeStruct((D, S), bf)] * 2,
        compiler_params=pltpu.CompilerParams(vmem_limit_bytes=VM),
        name="project_qkv",
    )(x, w, v)


def input_kernel(x_ref, dq_ref, dk_ref, dv_ref, dr_ref, w_ref, s_ref, b1_ref, gw_ref, rg_ref, v_ref):
    D = x_ref.shape[1]
    for n, ref in enumerate((dq_ref, dk_ref, dv_ref)):
        gw_ref[:, n * D : (n + 1) * D] = lax.dot_general(x_ref[...], ref[...], TN, preferred_element_type=f32).astype(bf)
    S = x_ref.shape[0]
    v_ref[...] = jnp.concatenate([s_ref[...], b1_ref[...], jnp.zeros((4, D), f32)], axis=0)
    for row, ref in ((0, dq_ref), (1, dv_ref)):
        part = jnp.zeros((8, D), f32)
        for r in range(0, S, 64):
            part = part + fold8(ref[pl.ds(r, 64), :].astype(f32))
        v_ref[row : row + 1, :] = jnp.sum(part, axis=0, keepdims=True)
    for r in range(0, S, 384):
        sl = pl.ds(r, 384)
        total = dr_ref[sl, :]
        for n, ref in enumerate((dq_ref, dk_ref, dv_ref)):
            total = total + lax.dot_general(ref[sl, :], w_ref[:, n * D : (n + 1) * D], NT, preferred_element_type=f32)
        rg_ref[sl, :] = total.astype(bf)


def input_call(x, dq, dk, dv, dr, w, sums, sb1):
    S, D = x.shape
    return pl.pallas_call(
        input_kernel,
        grid=(1,),
        in_specs=[pl.BlockSpec(a.shape, lambda i: (0, 0)) for a in (x, dq, dk, dv, dr)]
        + [pl.BlockSpec((D, 3 * D), lambda i: (0, 0))]
        + [pl.BlockSpec(a.shape, lambda i: (0, 0)) for a in (sums, sb1)],
        out_specs=[pl.BlockSpec(s, lambda i: (0, 0)) for s in ((D, 3 * D), (S, D), (16, D))],
        out_shape=[jax.ShapeDtypeStruct((D, 3 * D), bf), jax.ShapeDtypeStruct((S, D), bf), jax.ShapeDtypeStruct((16, D), f32)],
        compiler_params=pltpu.CompilerParams(vmem_limit_bytes=VM),
        name="input_gradients",
    )(x, dq, dk, dv, dr, w, sums, sb1)


def gather(shard):
    return lax.all_gather(shard, AXES, axis=0, tiled=True)


def scatter(grad):
    return lax.psum_scatter(grad, AXES, scatter_dimension=0, tiled=True)


def local(where, rows, cotangent, page_rows, pos_bucket, x_bucket, y_bucket, wq, bq, wk, wv, bv, wo, bo,
          ln1_gain, ln1_bias, w1, b1, w2, b2, ln2_gain, ln2_bias, pos_table, x_table, y_table):
    length, width = rows.shape[1:]
    share = wq.shape[0]
    wide, narrow, span = where[:3]
    n = wide * narrow
    kin = KIN if share % 8 == 0 else 1
    w_rest = gather(pack_call(wo, w1, w2, n))
    bias, codes, w_all, small, b_up = front_call(
        where, pos_bucket[0], x_bucket[0], y_bucket[0], (pos_table.T, x_table.T, y_table.T), (wq, wk, wv),
        (bq, bv, bo, ln1_gain, ln1_bias, b2, ln2_gain, ln2_bias, b1),
    )
    w_qkv = w_all.reshape(width, 3 * width)
    query, keys, values, keys_t, values_t = qkv_call(rows[0], w_qkv, small)
    prob, attended, inverse = fwd_call(page_rows, query, keys, values_t, bias)
    out_rows, normed, act, d_ffn, d_pre, d_mixed, d_branch, d_attended, inner, sums, sum_up = row_call(
        page_rows, attended, rows[0], cotangent[0], w_rest, small, b_up
    )
    early, late = share_call(attended, normed, act, d_mixed, d_pre, d_ffn, kin)
    early, late, d_attended = lax.optimization_barrier((early, late, d_attended))
    late = scatter(late)
    early = early.reshape(n // (2 * span), 2, span, share, kin * width)
    dq, dk, dv, ds, early = bwd_call(where, query, d_attended, keys_t, values, prob, inverse, inner, early)
    grad_qkv, rows_grad, sums = input_call(rows[0], dq, dk, dv, d_branch, w_qkv, sums, sum_up)
    grad_qkv = grad_qkv.reshape(n // (2 * span), 2, span, share, 3 * width)
    tables, first, vec = tail_call(where, ds, codes, grad_qkv, sums)
    g_out, g_up, g_down, g_query, g_key, g_value, g_pos, g_x, g_y, own = finish_call(early, late, first, vec, tables, n, narrow)
    return (
        out_rows[None], rows_grad[None], g_query, own[0], g_key, g_value, own[1], g_out, own[2], own[3], own[4],
        g_up, own[8], g_down, own[5], own[6], own[7], g_pos, g_x, g_y,
    )


def solution(mesh):
    wide, narrow = mesh.shape["wide"], mesh.shape["narrow"]
    small = wide <= 8
    where = (wide, narrow, 1 if small else narrow, wide // 2 if small else 8, 4 if small else narrow)
    cut3 = P(AXES, None, None)
    cut2 = P(AXES, None)
    cut1 = P(AXES)
    params = (cut2, cut1, cut2, cut2, cut1, cut2, cut1, cut1, cut1, cut2, cut1, cut2, cut1, cut1, cut1)
    in_specs = (cut3, cut3, cut1, cut3, cut3, cut3) + params + (P(), P(), P())
    out_specs = (cut3, cut3) + params + (P(), P(), P())
    return jax.shard_map(lambda *a: local(where, *a), mesh=mesh, in_specs=in_specs, out_specs=out_specs, check_vma=False)
```
